32 devices in a mesh: dp: 4 (over y, x), seq: 8 (over z, core).
Axes of the slice: x: 2, y: 2, z: 4, core: 2. Of those that a mesh axis runs over, the one named last changes fastest.
Arguments:
- tokens: bfloat16 [2, 16, 1024, 768], P(None, 'dp', 'seq'), may hold values from -6 to 6
- w_qkv: float32 [768, 2304], P(('dp', 'seq')), may hold values from -0.21875 to 0.21875
- w_feat: float32 [2, 768, 64], P(None, ('dp', 'seq')), may hold values from -1.5 to 1.5
- w_out: float32 [768, 768], P(('dp', 'seq')), may hold values from -0.875 to 0.875
- w_fc: float32 [768, 3072], P(('dp', 'seq')), may hold values from -0.21875 to 0.21875
- w_proj: float32 [3072, 768], P(('dp', 'seq')), may hold values from -0.109375 to 0.109375
- gains: float32 [2, 768], P(None, ('dp', 'seq')), may hold values from 0.5 to 1.5
- biases: float32 [11, 768], P(None, ('dp', 'seq')), may hold values from -0.6 to 0.6
- cotangent: bfloat16 [2, 16, 1024, 768], P(None, 'dp', 'seq'), may hold values from -6 to 6
Outputs:
- outputs: bfloat16 [2, 16, 1024, 768], P(None, 'dp', 'seq')
- input_grad: float32 [2, 16, 1024, 768], P(None, 'dp', 'seq')
- grad_qkv: float32 [768, 2304], P(('dp', 'seq'))
- grad_feat: float32 [2, 768, 64], P(None, ('dp', 'seq'))
- grad_out: float32 [768, 768], P(('dp', 'seq'))
- grad_fc: float32 [768, 3072], P(('dp', 'seq'))
- grad_proj: float32 [3072, 768], P(('dp', 'seq'))
- grad_gains: float32 [2, 768], P(None, ('dp', 'seq'))
- grad_biases: float32 [11, 768], P(None, ('dp', 'seq'))
The draws below stay inside these ranges and needn't reach their ends.
All inputs are finite; a program needn't handle non-finite values.
Results may differ from the reference program's by a relative error of at most 0.017.
The reference program's roundings to bfloat16 on the way count: a program that leaves them out, or rounds other values in their place, can miss the bound.
Values may be sent and summed in bfloat16 or wider, within the bound.
No kernel may reach another device: no remote copies, remote signals or barrier semaphores. Data moves between devices by JAX's collectives and lax.ppermute only.
A program may use at most 320 MiB of HBM per device.

```python
import jax
import jax.numpy as jnp
from jax import lax

D = 768
HEADS = 12
HD = 64
FF = 3072
BLOCK = 64
SEQS = 4
MB = 2
LENGTH = 1024
BATCH = 16
N_DP = 4


def block_levels(own_key, dims, shards, low, high):
    gain, own = 1.0, jax.random.fold_in(own_key, 6)
    for dim, shards_of in shards:
        draws = jnp.exp(jax.random.uniform(jax.random.fold_in(own, dim), (shards_of,), jnp.float32, low / len(shards), high / len(shards)))
        gain = gain * jnp.repeat(draws, dims[dim] // shards_of).reshape([-1 if axis == dim else 1 for axis in range(len(dims))])
    return gain


def scatter_about(own_key, extent, scale, limit, shards=(), dtype=jnp.bfloat16):
    array = jax.random.normal(own_key, extent, jnp.float32) * scale
    if len(shards) > 0:
        array = block_levels(own_key, extent, shards, -0.22, 0.18) * array
    return jnp.clip(array, min=-limit, max=limit).astype(dtype)


def setup_inputs(seed: int = 0) -> dict:
    splits = jax.random.split(jax.random.key(seed), 10)
    tokens = scatter_about(splits[0], (MB, BATCH, LENGTH, D), 1.0, 6.0, ((1, 4), (2, 8)))
    w_qkv = scatter_about(splits[1], (D, 3 * D), D ** -0.5, 0.21875, ((0, 32),), jnp.float32)
    w_feat = scatter_about(splits[2], (2, D, HD), (HD // 4) ** -0.5, 1.5, ((1, 32),), jnp.float32)
    w_out = scatter_about(splits[3], (D, D), (D // 16) ** -0.5, 0.875, ((0, 32),), jnp.float32)
    w_fc = scatter_about(splits[4], (D, FF), D ** -0.5, 0.21875, ((0, 32),), jnp.float32)
    w_proj = scatter_about(splits[5], (FF, D), FF ** -0.5, 0.109375, ((0, 32),), jnp.float32)
    gains = jnp.clip(1.0 + 0.1 * jax.random.normal(splits[6], (2, D), jnp.float32), 0.5, 1.5)
    biases = scatter_about(splits[7], (11, D), 0.1, 0.6, ((1, 32),), jnp.float32)
    cotangent = scatter_about(splits[8], (MB, BATCH, LENGTH, D), 1.0, 6.0, ((1, 4), (2, 8)))
    return {"tokens": tokens, "w_qkv": w_qkv, "w_feat": w_feat, "w_out": w_out, "w_fc": w_fc, "w_proj": w_proj, "gains": gains, "biases": biases, "cotangent": cotangent}


@jax.custom_vjp
def low(v):
    return lax.optimization_barrier(v.astype(jnp.bfloat16)).astype(jnp.float32)

@jax.custom_vjp
def low_back(v):
    return v

def low_keep(v):
    return (low(v), None)

def low_pass(kept, grad):
    return (grad,)

def back_keep(v):
    return (v, None)

def back_low(kept, grad):
    return (low(grad),)
low.defvjp(low_keep, low_pass)
low_back.defvjp(back_keep, back_low)

def layer_norm(values, norm_gain, norm_shift):
    centred = values - lax.optimization_barrier(jnp.mean(values, axis=-1, keepdims=True))
    spread = lax.optimization_barrier(jnp.mean(centred * centred, axis=-1, keepdims=True))
    return centred * lax.rsqrt(spread + 1e-05) * norm_gain + norm_shift

def features(logits):
    return jnp.concatenate([jax.nn.softmax(logits, axis=-1), jax.nn.softmax(-logits, axis=-1)], axis=-1)

def matmul(first_op, second_op):
    return jnp.dot(first_op, second_op, preferred_element_type=jnp.float32, precision=lax.Precision.HIGHEST)

def attend(phi_q, phi_k, value_rows):
    group_count, length, head_count, feat_count = phi_q.shape
    blocks = length // BLOCK
    causal = jnp.tril(jnp.ones((BLOCK, BLOCK), jnp.float32))

    def by_block(values):
        return jnp.moveaxis(values.reshape(group_count, blocks, BLOCK, head_count, values.shape[-1]), 1, 0)

    def block_step(carried, block_in):
        prior_state, prior_sum = carried
        block_q, block_k, block_v = block_in
        scores = jnp.einsum('gthf,guhf->ghtu', block_q, block_k, precision=lax.Precision.HIGHEST) * causal
        scores = low(low_back(scores))
        numerator = jnp.einsum('ghtu,guhe->gthe', scores, block_v, precision=lax.Precision.HIGHEST)
        numerator = numerator + jnp.einsum('gthf,ghfe->gthe', block_q, low(prior_state), precision=lax.Precision.HIGHEST)
        numerator = low_back(numerator)
        denominator = jnp.swapaxes(lax.optimization_barrier(jnp.sum(scores, axis=-1)), 1, 2)
        denominator = denominator + jnp.einsum('gthf,ghf->gth', block_q, prior_sum, precision=lax.Precision.HIGHEST)
        contexts = numerator / denominator[..., None]
        own_state = low_back(jnp.einsum('guhf,guhe->ghfe', block_k, block_v, precision=lax.Precision.HIGHEST))
        return ((prior_state + own_state, prior_sum + lax.optimization_barrier(jnp.sum(block_k, axis=1))), contexts)
    start_carry = (jnp.zeros((group_count, head_count, feat_count, HD), jnp.float32), jnp.zeros((group_count, head_count, feat_count), jnp.float32))
    unused, contexts = lax.scan(jax.checkpoint(block_step), start_carry, (by_block(phi_q), by_block(phi_k), by_block(value_rows)))
    return jnp.moveaxis(contexts, 0, 1).reshape(group_count, length, head_count * HD)

def block_group(params, group_in):
    w_qkv, w_feat, w_out, w_fc, w_proj, gains, biases = params
    group_count, length, model_width = group_in.shape
    hidden = low(layer_norm(group_in, gains[0], biases[0]))
    mixed = low(low_back(matmul(hidden, w_qkv) + biases[1:4].reshape(-1)))
    queries = mixed[..., :D].reshape(group_count, length, HEADS, HD)
    key_rows = mixed[..., D:2 * D].reshape(group_count, length, HEADS, HD)
    value_rows = mixed[..., 2 * D:].reshape(group_count, length, HEADS, HD)
    logit_q = low_back(jnp.einsum('glhi,hij->glhj', queries, w_feat[0].reshape(HEADS, HD, HD), precision=lax.Precision.HIGHEST))
    logit_k = low_back(jnp.einsum('glhi,hij->glhj', key_rows, w_feat[1].reshape(HEADS, HD, HD), precision=lax.Precision.HIGHEST))
    phi_q = low(features(logit_q))
    phi_k = low(features(logit_k))
    merged = low(attend(phi_q, phi_k, value_rows))
    middle = group_in + low_back(matmul(merged, w_out) + biases[4])
    normed = low(layer_norm(middle, gains[1], biases[5]))
    pre_act = low_back(matmul(normed, w_fc) + biases[6:10].reshape(-1))
    activated = low(jax.nn.gelu(pre_act, approximate=True))
    return middle + low_back(matmul(activated, w_proj) + biases[10])

def reference(tokens, w_qkv, w_feat, w_out, w_fc, w_proj, gains, biases, cotangent):
    masters = (w_qkv, w_feat, w_out, w_fc, w_proj, gains, biases)
    inputs = tokens.astype(jnp.float32).reshape(MB * N_DP, SEQS, LENGTH, D)
    upstream = cotangent.astype(jnp.float32).reshape(MB * N_DP, SEQS, LENGTH, D)

    def forward(params, grouped):
        rounded = tuple((low(master) for master in params))

        def one_group(group_in):
            return block_group(rounded, group_in)
        return lax.map(jax.checkpoint(one_group), grouped)
    results, pullback = jax.vjp(forward, masters, inputs)
    grad_params, grad_inputs = pullback(upstream)
    full_shape = (MB, BATCH, LENGTH, D)
    return (results.reshape(full_shape).astype(jnp.bfloat16), grad_inputs.reshape(full_shape), grad_params[0], grad_params[1], grad_params[2], grad_params[3], grad_params[4], grad_params[5], grad_params[6])
```

```python
import jax
import jax.numpy as jnp
from jax import lax
from jax.sharding import PartitionSpec as P

HD = 64
BLOCK = 64


AXES = ("dp", "seq")


def grid_dims():
    n_dp, n_seq = lax.axis_size("dp"), lax.axis_size("seq")
    n_x = 1
    while n_x * n_x * 4 <= n_dp:
        n_x *= 2
    sizes = {"y": n_dp // n_x, "x": n_x, "z": n_seq // 2, "c": 2}
    at = lax.axis_index("dp") * n_seq + lax.axis_index("seq")
    place = {}
    for name in ("c", "z", "x", "y"):
        place[name] = lax.rem(at, sizes[name])
        at = at // sizes[name]
    return sizes, place


def turned(sizes, name, step):
    pairs = []
    for y in range(sizes["y"]):
        for x in range(sizes["x"]):
            for z in range(sizes["z"]):
                for c in range(sizes["c"]):
                    to = {"y": y, "x": x, "z": z, "c": c}
                    to[name] = (to[name] + step) % sizes[name]
                    flat = lambda p: ((p[0] * sizes["x"] + p[1]) * sizes["z"] + p[2]) * 2 + p[3]
                    pairs.append((flat((y, x, z, c)), flat((to["y"], to["x"], to["z"], to["c"]))))
    return pairs


def send(value, sizes, name, step):
    return lax.ppermute(value, AXES, turned(sizes, name, step))


def gather_dim(value, grid, name):
    sizes, place = grid
    count = sizes[name]
    if count == 1:
        return value[None]
    got = [value] + [send(value, sizes, name, k) for k in range(1, count)]
    if count == 2:
        low = place[name] == 0
        return jnp.stack([jnp.where(low, got[0], got[1]), jnp.where(low, got[1], got[0])])
    order = jnp.stack(got[::-1] + got[::-1][:-1])
    return lax.dynamic_slice_in_dim(order, count - 1 - place[name], count, 0)


def gather_rows(value, grid, order):
    out = value
    for name in order:
        out = gather_dim(out, grid, name)
    axes = [len(order) - 1 - order.index(name) for name in ("y", "x", "z", "c")]
    out = jnp.transpose(out, axes + list(range(len(order), out.ndim)))
    return out.reshape((-1,) + value.shape[1:])


def scatter_dim(value, grid, name, axis):
    sizes, place = grid
    count = sizes[name]
    mine = lax.dynamic_index_in_dim(value, place[name], axis, keepdims=False)
    if count == 1:
        return mine
    total = mine.astype(jnp.float32)
    for k in range(1, count):
        block = lax.dynamic_index_in_dim(
            value, lax.rem(place[name] + k, count), axis, keepdims=False
        )
        total = total + send(block, sizes, name, k).astype(jnp.float32)
    return total.astype(jnp.bfloat16)


def scatter_rows(value, grid, order):
    sizes, _ = grid
    names = ["y", "x", "z", "c"]
    rows = value.shape[0] // (sizes["y"] * sizes["x"] * sizes["z"] * sizes["c"])
    out = value.reshape(tuple(sizes[n] for n in names) + (rows,) + value.shape[1:])
    for name in order:
        axis = names.index(name)
        out = scatter_dim(out, grid, name, axis)
        names.pop(axis)
    return out


def prefix(value, grid, reverse):
    sizes, place = grid
    sign = -1 if reverse else 1
    count = sizes["z"]
    own = jax.tree.map(lambda v: v.astype(jnp.bfloat16), value)
    other = jax.tree.map(lambda v: send(v, sizes, "c", 1), own)
    total = jax.tree.map(lambda a, b: (a + b.astype(jnp.float32)).astype(jnp.bfloat16), value, other)
    ahead = place["c"] == (0 if reverse else 1)
    out = jax.tree.map(lambda v: jnp.where(ahead, v.astype(jnp.float32), 0.0), other)
    for k in range(1, count):
        got = jax.tree.map(lambda v: send(v, sizes, "z", sign * k), total)
        valid = (place["z"] + k < count) if reverse else (place["z"] >= k)
        out = jax.tree.map(lambda o, g: o + jnp.where(valid, g.astype(jnp.float32), 0.0), out, got)
    return out


def layer_norm(values, norm_gain, norm_shift):
    centred = values - jnp.mean(values, axis=-1, keepdims=True)
    spread = jnp.mean(centred * centred, axis=-1, keepdims=True)
    return centred * lax.rsqrt(spread + 1e-05) * norm_gain + norm_shift


def features(logits):
    return jnp.concatenate(
        [jax.nn.softmax(logits, axis=-1), jax.nn.softmax(-logits, axis=-1)], axis=-1
    )


def gelu_tanh(values):
    return jax.nn.gelu(values, approximate=True)


def dot_plain(first_op, second_op):
    return jnp.dot(first_op, second_op, preferred_element_type=jnp.float32)


def dot_first(first_op, second_op):
    return lax.dot_general(
        first_op, second_op, (((0,), (0,)), ((), ())), preferred_element_type=jnp.float32
    )


def dot_second(first_op, second_op):
    return lax.dot_general(
        first_op, second_op, (((1,), (1,)), ((), ())), preferred_element_type=jnp.float32
    )


def earlier_sum(values):
    zero_row = jnp.zeros_like(values[:, :1])
    return jnp.concatenate([zero_row, jnp.cumsum(values[:, :-1], axis=1)], axis=1)


def later_sum(values):
    return jnp.flip(earlier_sum(jnp.flip(values, 1)), 1)


def forward_pass(grid, gathered, inputs, seq_count, seg_len):
    w_qkv, w_feat, w_out, w_fc, w_proj, gains, biases = gathered
    gains_f = gains.astype(jnp.float32)
    biases_f = biases.astype(jnp.float32)
    tok_rows, model_width = inputs.shape
    head_count = model_width // HD
    block_count = seg_len // BLOCK
    blocked = (seq_count, block_count, BLOCK, head_count)
    hidden = layer_norm(inputs, gains_f[0], biases_f[0]).astype(jnp.bfloat16)
    mixed = (dot_plain(hidden, w_qkv) + biases_f[1:4].reshape(-1)).astype(jnp.bfloat16)
    queries = mixed[:, :model_width].reshape(tok_rows, head_count, HD)
    key_rows = mixed[:, model_width : 2 * model_width].reshape(tok_rows, head_count, HD)
    value_rows = mixed[:, 2 * model_width :].reshape(blocked + (HD,))
    logit_q = jnp.einsum(
        "rhi,hij->rhj",
        queries,
        w_feat[0].reshape(head_count, HD, HD),
        preferred_element_type=jnp.float32,
    )
    logit_k = jnp.einsum(
        "rhi,hij->rhj",
        key_rows,
        w_feat[1].reshape(head_count, HD, HD),
        preferred_element_type=jnp.float32,
    )
    phi_q = features(logit_q).astype(jnp.bfloat16).reshape(blocked + (2 * HD,))
    phi_k = features(logit_k).astype(jnp.bfloat16).reshape(blocked + (2 * HD,))
    causal = jnp.tril(jnp.ones((BLOCK, BLOCK), jnp.float32))
    scores = (
        jnp.einsum("snthf,snuhf->snhtu", phi_q, phi_k, preferred_element_type=jnp.float32) * causal
    ).astype(jnp.bfloat16)
    numerator = jnp.einsum(
        "snhtu,snuhe->snthe", scores, value_rows, preferred_element_type=jnp.float32
    )
    denominator = jnp.swapaxes(jnp.sum(scores, axis=-1, dtype=jnp.float32), 2, 3)
    own_state = jnp.einsum(
        "snuhf,snuhe->snhfe", phi_k, value_rows, preferred_element_type=jnp.float32
    )
    own_sum = jnp.sum(phi_k, axis=2, dtype=jnp.float32)
    dev_state = jnp.sum(own_state, axis=1)
    dev_sum = jnp.sum(own_sum, axis=1)
    before_state, before_sum = prefix((dev_state, dev_sum), grid, False)
    prior_state = (before_state[:, None] + earlier_sum(own_state)).astype(jnp.bfloat16)
    prior_sum = before_sum[:, None] + earlier_sum(own_sum)
    numerator = numerator + jnp.einsum(
        "snthf,snhfe->snthe", phi_q, prior_state, preferred_element_type=jnp.float32
    )
    denominator = denominator + jnp.einsum(
        "snthf,snhf->snth", phi_q, prior_sum, preferred_element_type=jnp.float32
    )
    contexts = numerator / denominator[..., None]
    merged = contexts.reshape(tok_rows, model_width).astype(jnp.bfloat16)
    middle = inputs + dot_plain(merged, w_out) + biases_f[4]
    normed = layer_norm(middle, gains_f[1], biases_f[5]).astype(jnp.bfloat16)
    pre_act = dot_plain(normed, w_fc) + biases_f[6:10].reshape(-1)
    activated = gelu_tanh(pre_act).astype(jnp.bfloat16)
    result = middle + dot_plain(activated, w_proj) + biases_f[10]
    saved = (
        inputs,
        hidden,
        queries,
        key_rows,
        value_rows,
        logit_q,
        logit_k,
        phi_q,
        phi_k,
        prior_state,
        prior_sum,
        contexts,
        denominator,
        merged,
        middle,
        normed,
        pre_act,
        activated,
    )
    return (result, saved)


def backward_pass(grid, gathered, saved, upstream):
    w_qkv, w_feat, w_out, w_fc, w_proj, gains, biases = gathered
    (
        inputs,
        hidden,
        queries,
        key_rows,
        value_rows,
        logit_q,
        logit_k,
        phi_q,
        phi_k,
        prior_state,
        prior_sum,
        contexts,
        denominator,
        merged,
        middle,
        normed,
        pre_act,
        activated,
    ) = saved
    gains_f = gains.astype(jnp.float32)
    biases_f = biases.astype(jnp.float32)
    tok_rows, model_width = inputs.shape
    head_count = model_width // HD
    d_mlp = upstream.astype(jnp.bfloat16)
    grad_proj = dot_first(activated, d_mlp)
    bias_proj = jnp.sum(d_mlp, axis=0, dtype=jnp.float32)
    d_act = dot_second(d_mlp, w_proj)
    gelu_back = jax.vjp(gelu_tanh, pre_act)[1]
    d_pre = gelu_back(d_act)[0].astype(jnp.bfloat16)
    grad_fc = dot_first(normed, d_pre)
    bias_fc = jnp.sum(d_pre, axis=0, dtype=jnp.float32)
    d_normed = dot_second(d_pre, w_fc)
    norm_back_two = jax.vjp(layer_norm, middle, gains_f[1], biases_f[5])[1]
    d_middle, gain_two, shift_two = norm_back_two(d_normed)
    d_middle = d_middle + upstream
    d_branch = d_middle.astype(jnp.bfloat16)
    grad_out = dot_first(merged, d_branch)
    bias_out = jnp.sum(d_branch, axis=0, dtype=jnp.float32)
    d_context = dot_second(d_branch, w_out).reshape(contexts.shape)
    d_numer = (d_context / denominator[..., None]).astype(jnp.bfloat16)
    d_denom = -jnp.sum(d_context * contexts, axis=-1) / denominator
    causal = jnp.tril(jnp.ones((BLOCK, BLOCK), jnp.float32))
    scores = (
        jnp.einsum("snthf,snuhf->snhtu", phi_q, phi_k, preferred_element_type=jnp.float32) * causal
    ).astype(jnp.bfloat16)
    d_scores = jnp.einsum(
        "snthe,snuhe->snhtu", d_numer, value_rows, preferred_element_type=jnp.float32
    )
    d_scores = ((d_scores + jnp.swapaxes(d_denom, 2, 3)[..., None]) * causal).astype(jnp.bfloat16)
    d_values = jnp.einsum("snhtu,snthe->snuhe", scores, d_numer, preferred_element_type=jnp.float32)
    d_phi_q = jnp.einsum("snhtu,snuhf->snthf", d_scores, phi_k, preferred_element_type=jnp.float32)
    d_phi_q = d_phi_q + jnp.einsum(
        "snthe,snhfe->snthf", d_numer, prior_state, preferred_element_type=jnp.float32
    )
    d_phi_q = d_phi_q + d_denom[..., None] * prior_sum[:, :, None]
    d_phi_k = jnp.einsum("snhtu,snthf->snuhf", d_scores, phi_q, preferred_element_type=jnp.float32)
    d_state = jnp.einsum("snthf,snthe->snhfe", phi_q, d_numer, preferred_element_type=jnp.float32)
    d_sum = jnp.einsum("snthf,snth->snhf", phi_q, d_denom, preferred_element_type=jnp.float32)
    dev_state = jnp.sum(d_state, axis=1)
    dev_sum = jnp.sum(d_sum, axis=1)
    after_state, after_sum = prefix((dev_state, dev_sum), grid, True)
    d_own = (after_state[:, None] + later_sum(d_state)).astype(jnp.bfloat16)
    d_own_sum = after_sum[:, None] + later_sum(d_sum)
    d_phi_k = d_phi_k + jnp.einsum(
        "snuhe,snhfe->snuhf", value_rows, d_own, preferred_element_type=jnp.float32
    )
    d_phi_k = d_phi_k + d_own_sum[:, :, None]
    d_values = d_values + jnp.einsum(
        "snuhf,snhfe->snuhe", phi_k, d_own, preferred_element_type=jnp.float32
    )
    feat_back_q = jax.vjp(features, logit_q)[1]
    feat_back_k = jax.vjp(features, logit_k)[1]
    d_logit_q = feat_back_q(d_phi_q.reshape(tok_rows, head_count, 2 * HD))[0].astype(jnp.bfloat16)
    d_logit_k = feat_back_k(d_phi_k.reshape(tok_rows, head_count, 2 * HD))[0].astype(jnp.bfloat16)
    map_q = w_feat[0].reshape(head_count, HD, HD)
    map_k = w_feat[1].reshape(head_count, HD, HD)
    d_queries = jnp.einsum("rhj,hij->rhi", d_logit_q, map_q, preferred_element_type=jnp.float32)
    d_keys = jnp.einsum("rhj,hij->rhi", d_logit_k, map_k, preferred_element_type=jnp.float32)
    grad_map_q = jnp.einsum("rhi,rhj->hij", queries, d_logit_q, preferred_element_type=jnp.float32)
    grad_map_k = jnp.einsum("rhi,rhj->hij", key_rows, d_logit_k, preferred_element_type=jnp.float32)
    d_qkv = jnp.concatenate(
        [
            d_queries.reshape(tok_rows, model_width),
            d_keys.reshape(tok_rows, model_width),
            d_values.reshape(tok_rows, model_width),
        ],
        axis=1,
    ).astype(jnp.bfloat16)
    grad_qkv = dot_first(hidden, d_qkv)
    bias_qkv = jnp.sum(d_qkv, axis=0, dtype=jnp.float32)
    d_hidden = dot_second(d_qkv, w_qkv)
    norm_back_one = jax.vjp(layer_norm, inputs, gains_f[0], biases_f[0])[1]
    d_input, gain_one, shift_one = norm_back_one(d_hidden)
    input_grad = d_input + d_middle
    grad_feat = jnp.stack(
        [grad_map_q.reshape(model_width, HD), grad_map_k.reshape(model_width, HD)]
    )
    grad_gains = jnp.stack([gain_one, gain_two])
    grad_biases = jnp.concatenate(
        [
            shift_one[None],
            bias_qkv.reshape(3, model_width),
            bias_out[None],
            shift_two[None],
            bias_fc.reshape(4, model_width),
            bias_proj[None],
        ],
        axis=0,
    )
    grads = (grad_qkv, grad_feat, grad_out, grad_fc, grad_proj, grad_gains, grad_biases)
    return (grads, input_grad)


def shards(tokens, w_qkv, w_feat, w_out, w_fc, w_proj, gains, biases, cotangent):
    micro_count, seq_count, seg_len, model_width = tokens.shape
    grid = grid_dims()
    low = jnp.bfloat16
    rows = w_qkv.shape[0]
    hidden_width = w_fc.shape[1]
    first = jnp.concatenate(
        [
            w_qkv.astype(low),
            jnp.transpose(w_feat, (1, 0, 2)).reshape(rows, 2 * HD).astype(low),
            jnp.pad(jnp.concatenate([gains, biases]).T.astype(low), ((0, 0), (0, 128 - 13))),
        ],
        axis=1,
    )
    first = gather_rows(first, grid, ("z", "x", "y", "c"))
    later = jnp.concatenate(
        [w_fc.astype(low), w_proj.astype(low).reshape(rows, hidden_width), w_out.astype(low)],
        axis=1,
    )
    later = lax.all_gather(later, AXES, axis=0, tiled=True)
    wide = 3 * model_width
    small = first[:, wide + 2 * HD :].T
    gathered = (
        first[:, :wide],
        jnp.transpose(first[:, wide : wide + 2 * HD].reshape(model_width, 2, HD), (1, 0, 2)),
        later[:, 2 * hidden_width :],
        later[:, :hidden_width],
        later[:, hidden_width : 2 * hidden_width].reshape(hidden_width, model_width),
        small[:2],
        small[2:13],
    )
    inputs = tokens.reshape(-1, model_width).astype(jnp.float32)
    result, saved = forward_pass(grid, gathered, inputs, micro_count * seq_count, seg_len)
    upstream = cotangent.reshape(-1, model_width).astype(jnp.float32)
    grads, input_grad = backward_pass(grid, gathered, saved, upstream)
    g_qkv, g_feat, g_out, g_fc, g_proj, g_gains, g_biases = grads
    r_proj = scatter_rows(g_proj.astype(low), grid, ("c", "x", "y", "z"))
    r_fc = scatter_rows(g_fc.astype(low), grid, ("c", "y", "x", "z"))
    last = jnp.concatenate(
        [
            g_qkv.astype(low),
            g_out.astype(low),
            jnp.transpose(g_feat, (1, 0, 2)).reshape(model_width, 2 * HD).astype(low),
            jnp.pad(jnp.concatenate([g_gains, g_biases]).T.astype(low), ((0, 0), (0, 128 - 13))),
        ],
        axis=1,
    )
    last = scatter_rows(last, grid, ("c", "x", "y", "z")).astype(jnp.float32)
    small = last[:, wide + model_width + 2 * HD :].T
    return (
        result.reshape(tokens.shape).astype(low),
        input_grad.reshape(tokens.shape),
        last[:, :wide],
        jnp.transpose(
            last[:, wide + model_width : wide + model_width + 2 * HD].reshape(rows, 2, HD), (1, 0, 2)
        ),
        last[:, wide : wide + model_width],
        r_fc.astype(jnp.float32),
        r_proj.astype(jnp.float32),
        small[:2],
        small[2:13],
    )


def solution(mesh):
    return jax.shard_map(
        shards,
        mesh=mesh,
        in_specs=(
            P(None, "dp", "seq", None),
            P(("dp", "seq"), None),
            P(None, ("dp", "seq"), None),
            P(("dp", "seq"), None),
            P(("dp", "seq"), None),
            P(("dp", "seq"), None),
            P(None, ("dp", "seq")),
            P(None, ("dp", "seq")),
            P(None, "dp", "seq", None),
        ),
        out_specs=(
            P(None, "dp", "seq", None),
            P(None, "dp", "seq", None),
            P(("dp", "seq"), None),
            P(None, ("dp", "seq"), None),
            P(("dp", "seq"), None),
            P(("dp", "seq"), None),
            P(("dp", "seq"), None),
            P(None, ("dp", "seq")),
            P(None, ("dp", "seq")),
        ),
        check_vma=False,
    )
```

```python
import functools

import jax
import jax.numpy as jnp
from jax import lax
from jax.experimental import pallas as pl
from jax.experimental.pallas import tpu as pltpu
from jax.sharding import PartitionSpec as P

HD = 64
PAIR = 2 * HD
AXES = ("dp", "seq")
LOW = jnp.bfloat16
F32 = jnp.float32
VMEM_BYTES = 60 * 1024 * 1024
ZROWS = 16

def grid_dims():
    n_dp, n_seq = lax.axis_size("dp"), lax.axis_size("seq")
    n_x = 1
    while n_x * n_x * 4 <= n_dp:
        n_x *= 2
    sizes = {"y": n_dp // n_x, "x": n_x, "z": n_seq // 2, "c": 2}
    at = lax.axis_index("dp") * n_seq + lax.axis_index("seq")
    place = {}
    for name in ("c", "z", "x", "y"):
        place[name] = lax.rem(at, sizes[name])
        at = at // sizes[name]
    return sizes, place


def turned(sizes, name, step):
    pairs = []
    for y in range(sizes["y"]):
        for x in range(sizes["x"]):
            for z in range(sizes["z"]):
                for c in range(sizes["c"]):
                    to = {"y": y, "x": x, "z": z, "c": c}
                    to[name] = (to[name] + step) % sizes[name]
                    flat = lambda p: ((p[0] * sizes["x"] + p[1]) * sizes["z"] + p[2]) * 2 + p[3]
                    pairs.append((flat((y, x, z, c)), flat((to["y"], to["x"], to["z"], to["c"]))))
    return pairs


def send(value, sizes, name, step):
    return lax.ppermute(value, AXES, turned(sizes, name, step))


def gather_dim(value, grid, name):
    sizes, place = grid
    count = sizes[name]
    if count == 1:
        return value[None]
    got = [value] + [send(value, sizes, name, k) for k in range(1, count)]
    if count == 2:
        low = place[name] == 0
        return jnp.stack([jnp.where(low, got[0], got[1]), jnp.where(low, got[1], got[0])])
    order = jnp.stack(got[::-1] + got[::-1][:-1])
    return lax.dynamic_slice_in_dim(order, count - 1 - place[name], count, 0)


def gather_rows(value, grid, order):
    out = value
    for name in order:
        out = gather_dim(out, grid, name)
    axes = [len(order) - 1 - order.index(name) for name in ("y", "x", "z", "c")]
    out = jnp.transpose(out, axes + list(range(len(order), out.ndim)))
    return out.reshape((-1,) + value.shape[1:])


def scatter_dim(value, grid, name, axis):
    sizes, place = grid
    count = sizes[name]
    mine = lax.dynamic_index_in_dim(value, place[name], axis, keepdims=False)
    if count == 1:
        return mine
    total = mine.astype(F32)
    for k in range(1, count):
        block = lax.dynamic_index_in_dim(
            value, lax.rem(place[name] + k, count), axis, keepdims=False
        )
        total = total + send(block, sizes, name, k).astype(F32)
    return total.astype(LOW)


def scatter_rows(value, grid, order):
    sizes, _ = grid
    names = ["y", "x", "z", "c"]
    rows = value.shape[0] // (sizes["y"] * sizes["x"] * sizes["z"] * sizes["c"])
    out = value.reshape(tuple(sizes[n] for n in names) + (rows,) + value.shape[1:])
    for name in order:
        axis = names.index(name)
        out = scatter_dim(out, grid, name, axis)
        names.pop(axis)
    return out


def moved(sizes, name, step):
    pairs = turned(sizes, name, step)
    span = 2
    return [
        (a, b)
        for a, b in pairs
        if 0 <= (a // span) % sizes["z"] + step < sizes["z"]
    ]


def prefix(own, grid, reverse):
    sizes, place = grid
    sign = -1 if reverse else 1
    half = own.shape[0] // 2
    other = send(own, sizes, "c", 1)
    first = place["c"] * half
    mine = lax.dynamic_slice_in_dim(own, first, half, 0).astype(F32)
    mine = (mine + lax.dynamic_slice_in_dim(other, first, half, 0).astype(F32)).astype(LOW)
    total = 0.0
    for k in range(1, sizes["z"]):
        total = total + lax.ppermute(mine, AXES, moved(sizes, "z", sign * k)).astype(F32)
    total = total.astype(LOW)
    theirs = send(total, sizes, "c", 1)
    low = place["c"] == 0
    both = jnp.concatenate([jnp.where(low, total, theirs), jnp.where(low, theirs, total)])
    ahead = place["c"] == (0 if reverse else 1)
    return (both.astype(F32) + jnp.where(ahead, other.astype(F32), 0.0)).astype(LOW)


def dot(a, b):
    return jnp.dot(a, b, preferred_element_type=F32)


def dot_nt(a, b):
    return lax.dot_general(a, b, (((1,), (1,)), ((), ())), preferred_element_type=F32)


def dot_tn(a, b):
    return lax.dot_general(a, b, (((0,), (0,)), ((), ())), preferred_element_type=F32)


def normed(values):
    centred = values - jnp.mean(values, axis=-1, keepdims=True)
    spread = jnp.mean(centred * centred, axis=-1, keepdims=True)
    scale = lax.rsqrt(spread + 1e-05)
    return centred * scale, scale


def norm_back(grad, gain, unit, scale):
    eg = grad * gain
    inner = eg - jnp.mean(eg, axis=-1, keepdims=True)
    return scale * (inner - unit * jnp.mean(eg * unit, axis=-1, keepdims=True))


def lanes(shape=(PAIR, PAIR)):
    return lax.broadcasted_iota(jnp.int32, shape, 1)


def subs(shape=(PAIR, PAIR)):
    return lax.broadcasted_iota(jnp.int32, shape, 0)


def soft_pair(logits):
    high = jnp.max(logits, axis=0, keepdims=True)
    small = jnp.min(logits, axis=0, keepdims=True)
    e1 = jnp.exp(logits - high)
    e2 = jnp.exp(small - logits)
    p1 = e1 * (1.0 / jnp.sum(e1, axis=0, keepdims=True))
    p2 = e2 * (1.0 / jnp.sum(e2, axis=0, keepdims=True))
    return jnp.concatenate([p1, p2], axis=0)


def soft_back(phi, grad):
    prod = phi * grad
    s1 = jnp.sum(prod[:HD], axis=0, keepdims=True)
    s2 = jnp.sum(prod[HD:], axis=0, keepdims=True)
    return (prod[:HD] - phi[:HD] * s1) - (prod[HD:] - phi[HD:] * s2)


def enter_kernel(x_ref, w_ref, maps_ref, vec_ref, hid_ref, qkv_ref, pq_ref, pk_ref, st_ref):
    width = x_ref.shape[1]
    seqs = pq_ref.shape[0]
    heads = pq_ref.shape[1]
    unit, _ = normed(x_ref[...].astype(F32))
    hid_ref[...] = (unit * vec_ref[0:1, :] + vec_ref[2:3, :]).astype(LOW)
    for part in range(3):
        span = slice(part * width, (part + 1) * width)
        qkv_ref[:, span] = (dot(hid_ref[...], w_ref[:, span]) + vec_ref[3 + part : 4 + part, :]).astype(LOW)

    def one(s, carry):
        rows = pl.ds(pl.multiple_of(s * PAIR, PAIR), PAIR)
        lane = lanes()
        cols = jnp.zeros((PAIR, PAIR), F32)
        for p in range(heads // 2):
            at = slice(p * PAIR, (p + 1) * PAIR)
            for which, ref in ((0, pq_ref), (1, pk_ref)):
                value = qkv_ref[rows, which * width + p * PAIR : which * width + (p + 1) * PAIR]
                logits = dot_nt(maps_ref[which, p], value)
                ref[s, 2 * p] = soft_pair(logits[:HD]).astype(LOW)
                ref[s, 2 * p + 1] = soft_pair(logits[HD:]).astype(LOW)
            value = qkv_ref[rows, 2 * width + p * PAIR : 2 * width + (p + 1) * PAIR]
            own = []
            for h in (2 * p, 2 * p + 1):
                keys = pk_ref[s, h]
                own.append(dot(keys, value))
                cols = jnp.where(lane == h, jnp.sum(keys.astype(F32), axis=1, keepdims=True), cols)
            st_ref[s, at, :] = jnp.where(lane < HD, own[0], own[1]).astype(LOW)
        st_ref[s, width : width + ZROWS, :] = cols.T[:ZROWS].astype(LOW)
        return carry

    lax.fori_loop(0, seqs, one, 0)


def middle_kernel(
    x_ref, dy_ref, v_ref, pq_ref, pk_ref, pri_ref, w_ref, vec_ref, *rest
):
    (out_ref, a_ref, h2_ref, g_ref, du_ref, dmid_ref, dmb_ref, dn_ref, ds_ref, sum_ref,
     ctx_s, den_s, unit_s, acc_s, back_s) = rest[-15:]
    rows_all, width = x_ref.shape
    seqs, heads = pq_ref.shape[0], pq_ref.shape[1]
    blocks = g_ref.shape[1] // width
    hidden = g_ref.shape[1]

    def attend(s, carry):
        rows = pl.ds(pl.multiple_of(s * PAIR, PAIR), PAIR)
        lane, sub = lanes(), subs()
        zsum = pri_ref[s, width : width + ZROWS, :].astype(F32)
        for p in range(heads // 2):
            at = slice(p * PAIR, (p + 1) * PAIR)
            left, dens = [], []
            for h in (2 * p, 2 * p + 1):
                phi = pq_ref[s, h].T
                score = jnp.where(sub >= lane, dot(phi, pk_ref[s, h]), 0.0).astype(LOW)
                dens.append(
                    jnp.sum(
                        score.astype(F32) + phi.astype(F32) * zsum[h : h + 1, :],
                        axis=1,
                        keepdims=True,
                    )
                )
                left.append(jnp.concatenate([score, phi], axis=1))
            right = jnp.concatenate([v_ref[rows, at], pri_ref[s, at, :]], axis=0)
            both = dot(jnp.concatenate(left, axis=0), right)
            numer = jnp.where(lane < HD, both[:PAIR], both[PAIR:])
            den = jnp.where(lane < HD, dens[0], dens[1])
            ctx = numer / den
            ctx_s[rows, at] = ctx
            den_s[rows, at] = den
            a_ref[rows, at] = ctx.astype(LOW)
        return carry

    lax.fori_loop(0, seqs, attend, 0)

    w_out = w_ref[:, 2 * hidden : 2 * hidden + width]
    mid = x_ref[...].astype(F32) + dot(a_ref[...], w_out) + vec_ref[6:7, :]
    acc_s[...] = mid + vec_ref[12:13, :]
    unit, scale = normed(mid)
    unit_s[...] = unit
    h2_ref[...] = (unit * vec_ref[1:2, :] + vec_ref[7:8, :]).astype(LOW)
    back_s[...] = jnp.zeros_like(back_s)
    c0 = 0.7978845608028654
    c1 = 0.044715

    def mlp(j, carry):
        at = pl.ds(pl.multiple_of(j * width, width), width)
        at2 = pl.ds(pl.multiple_of(hidden + j * width, width), width)
        u = dot(h2_ref[...], w_ref[:, at]) + vec_ref[pl.ds(8 + j, 1), :]
        dg = dot_nt(dy_ref[...], w_ref[:, at2])
        sq = u * u
        th = jnp.tanh(c0 * (u + c1 * (u * sq)))
        half = 0.5 + 0.5 * th
        g = (u * half).astype(LOW)
        slope = half + (0.5 * u) * ((1.0 - th * th) * (c0 + (3.0 * c0 * c1) * sq))
        du = (slope * dg).astype(LOW)
        g_ref[:, at] = g
        du_ref[:, at] = du
        sum_ref[pl.ds(8 + j, 1), :] = jnp.sum(du.astype(F32), axis=0, keepdims=True)
        acc_s[...] += dot(g, w_ref[:, at2])
        back_s[...] += dot_nt(du, w_ref[:, at])
        return carry

    lax.fori_loop(0, blocks, mlp, 0)
    out_ref[...] = acc_s[...].astype(LOW)
    dy = dy_ref[...].astype(F32)
    e = back_s[...]
    unit = unit_s[...]
    sum_ref[12:13, :] = jnp.sum(dy, axis=0, keepdims=True)
    sum_ref[1:2, :] = jnp.sum(e * unit, axis=0, keepdims=True)
    sum_ref[7:8, :] = jnp.sum(e, axis=0, keepdims=True)
    dmid = dy + norm_back(e, vec_ref[1:2, :], unit, scale)
    dmid_ref[...] = dmid
    dmb = dmid.astype(LOW)
    dmb_ref[...] = dmb
    sum_ref[6:7, :] = jnp.sum(dmb.astype(F32), axis=0, keepdims=True)
    back_s[...] = dot_nt(dmb, w_ref[:, 2 * hidden : 2 * hidden + width])

    def back(s, carry):
        rows = pl.ds(pl.multiple_of(s * PAIR, PAIR), PAIR)
        lane = lanes()
        low = lane < HD
        cols = jnp.zeros((PAIR, PAIR), F32)
        for p in range(heads // 2):
            at = slice(p * PAIR, (p + 1) * PAIR)
            dctx = back_s[rows, at]
            inv = 1.0 / den_s[rows, at]
            dn = dctx * inv
            prod = dctx * ctx_s[rows, at]
            swapped = pltpu.roll(inv, HD, 1)
            got = []
            for h, mine, first in ((2 * p, low, HD), (2 * p + 1, jnp.logical_not(low), 0)):
                dd = -jnp.sum(jnp.where(mine, prod, 0.0), axis=1, keepdims=True) * swapped
                rest_dd = dd - dd.astype(LOW).astype(F32)
                tail = jnp.where(lane == first, dd, jnp.where(lane == first + 1, rest_dd, 0.0))
                aug = jnp.where(mine, dn, tail).astype(LOW)
                dn_ref[rows, h * PAIR : (h + 1) * PAIR] = aug
                ds = dot(pq_ref[s, h], aug)
                got.append(ds)
                edge = jnp.logical_or(lane == first, lane == first + 1)
                col = jnp.sum(jnp.where(edge, ds, 0.0), axis=1, keepdims=True)
                cols = jnp.where(lane == h, col, cols)
            ds_ref[s, at, :] = jnp.where(low, got[0], got[1]).astype(LOW)
        ds_ref[s, width : width + ZROWS, :] = cols.T[:ZROWS].astype(LOW)
        return carry

    lax.fori_loop(0, seqs, back, 0)


def leave_kernel(
    x_ref, qkv_ref, pq_ref, pk_ref, pri_ref, dl_ref, dn_ref, dmid_ref, w_ref, maps_ref, vec_ref, *rest
):
    dqkv_ref, dx_ref, gmap_ref, sum_ref = rest[-4:]
    width = x_ref.shape[1]
    seqs, heads = pq_ref.shape[0], pq_ref.shape[1]
    gmap_ref[...] = jnp.zeros_like(gmap_ref)

    def back(s, carry):
        rows = pl.ds(pl.multiple_of(s * PAIR, PAIR), PAIR)
        lane, sub = lanes(), subs()
        low = lane < HD
        fill = jnp.zeros((PAIR - ZROWS, PAIR), F32)
        zcol = jnp.concatenate([pri_ref[s, width : width + ZROWS, :].astype(F32), fill], axis=0).T
        dzcol = jnp.concatenate([dl_ref[s, width : width + ZROWS, :].astype(F32), fill], axis=0).T
        for p in range(heads // 2):
            at = slice(p * PAIR, (p + 1) * PAIR)
            vp = qkv_ref[rows, 2 * width + p * PAIR : 2 * width + (p + 1) * PAIR]
            prior = pri_ref[s, at, :]
            dl = dl_ref[s, at, :]
            left, dfq, dfk, dns = [], [], [], []
            for h, mine, first in ((2 * p, low, HD), (2 * p + 1, jnp.logical_not(low), 0)):
                edge = jnp.logical_or(lane == first, lane == first + 1)
                pq, pk = pq_ref[s, h], pk_ref[s, h]
                dn = dn_ref[rows, h * PAIR : (h + 1) * PAIR]
                vaug = jnp.where(mine, vp.astype(F32), jnp.where(edge, 1.0, 0.0)).astype(LOW)
                saug = jnp.where(
                    mine, prior.astype(F32), jnp.where(edge, zcol[:, h : h + 1], 0.0)
                ).astype(LOW)
                laug = jnp.where(
                    mine, dl.astype(F32), jnp.where(lane == first, dzcol[:, h : h + 1], 0.0)
                ).astype(LOW)
                da = jnp.where(sub >= lane, dot_nt(dn, vaug), 0.0).astype(LOW)
                dpq = dot_nt(
                    jnp.concatenate([pk, saug], axis=1), jnp.concatenate([da, dn], axis=1)
                )
                dpk = dot(pq, da) + dot_nt(laug, vaug)
                dfq.append(soft_back(pq.astype(F32), dpq).astype(LOW))
                dfk.append(soft_back(pk.astype(F32), dpk).astype(LOW))
                keys = pk.T
                score = jnp.where(sub <= lane, dot(keys, pq), 0.0).astype(LOW)
                left.append(jnp.concatenate([score, keys], axis=1))
                dns.append(dn)
            dn = jnp.where(low, dns[0].astype(F32), dns[1].astype(F32)).astype(LOW)
            both = dot(jnp.concatenate(left, axis=0), jnp.concatenate([dn, dl], axis=0))
            dv = jnp.where(low, both[:PAIR], both[PAIR:])
            dqkv_ref[rows, 2 * width + p * PAIR : 2 * width + (p + 1) * PAIR] = dv.astype(LOW)
            for which, parts in ((0, dfq), (1, dfk)):
                df = jnp.concatenate(parts, axis=0)
                mine_at = slice(which * width + p * PAIR, which * width + (p + 1) * PAIR)
                gmap_ref[which, p] += dot(df, qkv_ref[rows, mine_at])
                dqkv_ref[rows, mine_at] = dot(df.T, maps_ref[which, p]).astype(LOW)
        return carry

    lax.fori_loop(0, seqs, back, 0)
    e = dot_nt(dqkv_ref[...], w_ref[...])
    unit, scale = normed(x_ref[...].astype(F32))
    dx_ref[...] = dmid_ref[...] + norm_back(e, vec_ref[0:1, :], unit, scale)
    sum_ref[...] = jnp.zeros_like(sum_ref)
    sum_ref[0:1, :] = jnp.sum(e * unit, axis=0, keepdims=True)
    sum_ref[2:3, :] = jnp.sum(e, axis=0, keepdims=True)
    for part in range(3):
        piece = dqkv_ref[:, part * width : (part + 1) * width].astype(F32)
        sum_ref[3 + part : 4 + part, :] = jnp.sum(piece, axis=0, keepdims=True)


def weight_kernel(h2_ref, du_ref, g_ref, dy_ref, a_ref, dmb_ref, out_ref):
    step = pl.program_id(0)
    blocks = (pl.num_programs(0) - 1) // 2

    @pl.when(step < blocks)
    def _():
        out_ref[...] = dot_tn(h2_ref[...], du_ref[...]).astype(LOW)

    @pl.when(jnp.logical_and(step >= blocks, step < 2 * blocks))
    def _():
        out_ref[...] = dot_tn(g_ref[...], dy_ref[...]).astype(LOW)

    @pl.when(step == 2 * blocks)
    def _():
        out_ref[...] = dot_tn(a_ref[...], dmb_ref[...]).astype(LOW)


def first_kernel(h_ref, d_ref, out_ref):
    out_ref[...] = dot_tn(h_ref[...], d_ref[...]).astype(LOW)


def whole(shape):
    return pl.BlockSpec(shape, lambda i: (0,) * len(shape), pipeline_mode=pl.Buffered(1))


def part(shape, *at):
    return pl.BlockSpec(shape, lambda i: at, pipeline_mode=pl.Buffered(1))


PARAMS = dict(
    compiler_params=pltpu.CompilerParams(
        dimension_semantics=("arbitrary",), vmem_limit_bytes=VMEM_BYTES
    )
)


def cost(flops, size):
    return pl.CostEstimate(flops=int(flops), bytes_accessed=int(size), transcendentals=0)


def enter(m, held, x, w, maps, vec, heads):
    total, width = x.shape
    rows = total // 2
    seqs = rows // PAIR
    pack = width + ZROWS
    return pl.pallas_call(
        enter_kernel,
        grid=(1,),
        in_specs=[
            part((rows, width), m, 0),
            whole(w.shape),
            whole(maps.shape),
            whole(vec.shape),
        ],
        out_specs=[
            whole((rows, width)),
            whole((rows, 3 * width)),
            whole((seqs, heads, PAIR, PAIR)),
            whole((seqs, heads, PAIR, PAIR)),
            whole((seqs, pack, PAIR)),
        ],
        out_shape=[
            jax.ShapeDtypeStruct((rows, width), LOW),
            jax.ShapeDtypeStruct((rows, 3 * width), LOW),
            jax.ShapeDtypeStruct((seqs, heads, PAIR, PAIR), LOW),
            jax.ShapeDtypeStruct((seqs, heads, PAIR, PAIR), LOW),
            jax.ShapeDtypeStruct((seqs, pack, PAIR), LOW),
        ],
        cost_estimate=cost(6 * rows * width * width, 12 * rows * width),
        name="enter",
        **PARAMS,
    )(x, w, maps, vec)


def middle(m, held, x, dy, qkv, pq, pk, pri, w, vec, hidden):
    total, width = x.shape
    rows = total // 2
    seqs, heads = pq.shape[0], pq.shape[1]
    pack = width + ZROWS
    extra = [] if held is None else list(held)
    shared = [
        ((total, width), LOW, (rows, width)),
        ((total, width), LOW, (rows, width)),
        ((total, width), LOW, (rows, width)),
        ((total, hidden), LOW, (rows, hidden)),
        ((total, hidden), LOW, (rows, hidden)),
        ((total, width), F32, (rows, width)),
        ((total, width), LOW, (rows, width)),
    ]
    return pl.pallas_call(
        middle_kernel,
        grid=(1,),
        in_specs=[
            part((rows, width), m, 0),
            part((rows, width), m, 0),
            part((rows, width), 0, 2),
            whole(pq.shape),
            whole(pk.shape),
            whole(pri.shape),
            whole(w.shape),
            whole(vec.shape),
        ]
        + [pl.BlockSpec(memory_space=pl.ANY)] * len(extra),
        out_specs=[part(b, m, 0) for _, _, b in shared]
        + [whole((rows, heads * PAIR)), whole((seqs, pack, PAIR)), whole((ZROWS, width))],
        out_shape=[jax.ShapeDtypeStruct(s, t) for s, t, _ in shared]
        + [
            jax.ShapeDtypeStruct((rows, heads * PAIR), LOW),
            jax.ShapeDtypeStruct((seqs, pack, PAIR), LOW),
            jax.ShapeDtypeStruct((ZROWS, width), F32),
        ],
        scratch_shapes=[pltpu.VMEM((rows, width), F32)] * 5,
        input_output_aliases={8 + k: k for k in range(len(extra))},
        cost_estimate=cost(8 * rows * width * hidden + 4 * rows * width * width, 30 * rows * width),
        name="middle",
        **PARAMS,
    )(x, dy, qkv, pq, pk, pri, w, vec, *extra)


def leave(m, held, x, qkv, pq, pk, pri, dl, dn, dmid, w, maps, vec):
    total, width = x.shape
    rows = total // 2
    extra = [] if held is None else list(held)
    return pl.pallas_call(
        leave_kernel,
        grid=(1,),
        in_specs=[
            part((rows, width), m, 0),
            whole(qkv.shape),
            whole(pq.shape),
            whole(pk.shape),
            whole(pri.shape),
            whole(dl.shape),
            whole(dn.shape),
            part((rows, width), m, 0),
            whole(w.shape),
            whole(maps.shape),
            whole(vec.shape),
        ]
        + [pl.BlockSpec(memory_space=pl.ANY)] * len(extra),
        out_specs=[
            part((rows, 3 * width), m, 0),
            part((rows, width), m, 0),
            whole(maps.shape),
            whole((ZROWS, width)),
        ],
        out_shape=[
            jax.ShapeDtypeStruct((total, 3 * width), LOW),
            jax.ShapeDtypeStruct((total, width), F32),
            jax.ShapeDtypeStruct(maps.shape, F32),
            jax.ShapeDtypeStruct((ZROWS, width), F32),
        ],
        input_output_aliases={11 + k: k for k in range(len(extra))},
        cost_estimate=cost(6 * rows * width * width, 24 * rows * width),
        name="leave",
        **PARAMS,
    )(x, qkv, pq, pk, pri, dl, dn, dmid, w, maps, vec, *extra)


def weight_grads(h2, du, g, dy, a, dmb):
    total, width = h2.shape
    blocks = du.shape[1] // width
    last = 2 * blocks
    block = (total, width)
    return pl.pallas_call(
        weight_kernel,
        grid=(last + 1,),
        in_specs=[
            pl.BlockSpec(block, lambda i: (0, 0)),
            pl.BlockSpec(block, lambda i: (0, jnp.minimum(i, blocks - 1))),
            pl.BlockSpec(block, lambda i: (0, jnp.clip(i - blocks, 0, blocks - 1))),
            pl.BlockSpec(block, lambda i: (0, 0)),
            pl.BlockSpec(block, lambda i: (0, 0)),
            pl.BlockSpec(block, lambda i: (0, 0)),
        ],
        out_specs=pl.BlockSpec((width, width), lambda i: (0, i)),
        out_shape=jax.ShapeDtypeStruct((width, (last + 1) * width), LOW),
        cost_estimate=cost(2 * total * width * width * (last + 1), 20 * total * width),
        name="weights",
        **PARAMS,
    )(h2, du, g, dy, a, dmb)


def first_grads(hid, dqkv):
    total, width = hid.shape
    block = (total, width)
    return pl.pallas_call(
        first_kernel,
        grid=(3,),
        in_specs=[pl.BlockSpec(block, lambda i: (0, 0)), pl.BlockSpec(block, lambda i: (0, i))],
        out_specs=pl.BlockSpec((width, width), lambda i: (0, i)),
        out_shape=jax.ShapeDtypeStruct((width, 3 * width), LOW),
        cost_estimate=cost(6 * total * width * width, 12 * total * width),
        name="first",
        **PARAMS,
    )(hid, dqkv)


def shards(tokens, w_qkv, w_feat, w_out, w_fc, w_proj, gains, biases, cotangent):
    micro_count, seq_count, seg_len, width = tokens.shape
    grid = grid_dims()
    rows = w_qkv.shape[0]
    hidden = w_fc.shape[1]
    ratio = hidden // width
    heads = width // HD
    pairs = heads // 2
    wide = 3 * width
    total = micro_count * seq_count * seg_len

    first = jnp.concatenate(
        [
            w_qkv.astype(LOW),
            jnp.transpose(w_feat, (1, 0, 2)).reshape(rows, PAIR).astype(LOW),
            jnp.pad(jnp.concatenate([gains, biases]).T.astype(LOW), ((0, 0), (0, PAIR - 13))),
        ],
        axis=1,
    )
    first = gather_rows(first, grid, ("z", "x", "y", "c"))
    later = jnp.concatenate(
        [
            w_fc.astype(LOW).reshape(rows, width, ratio).swapaxes(1, 2).reshape(rows, hidden),
            w_proj.astype(LOW).reshape(rows, hidden),
            w_out.astype(LOW),
        ],
        axis=1,
    )
    later = lax.all_gather(later, AXES, axis=0, tiled=True)
    small = first[:, wide + PAIR :].T[:13].astype(F32)
    fc_bias = small[8 : 8 + ratio].reshape(width, ratio).T
    vec = jnp.concatenate([small[:8], fc_bias, small[8 + ratio :], jnp.zeros((3, width), F32)])
    maps = first[:, wide : wide + PAIR].reshape(pairs, 2, HD, 2, HD)
    maps = jnp.transpose(maps, (3, 0, 1, 4, 2))
    none = jnp.zeros_like(maps[:, :, 0])
    maps = jnp.concatenate(
        [
            jnp.concatenate([maps[:, :, 0], none], axis=-1),
            jnp.concatenate([none, maps[:, :, 1]], axis=-1),
        ],
        axis=-2,
    )
    w_first = first[:, :wide]
    x = tokens.reshape(total, width)
    dy = cotangent.reshape(total, width)

    entered = [enter(m, None, x, w_first, maps, vec, heads) for m in range(2)]
    priors = [prefix(entered[m][4], grid, False) for m in range(2)]
    held, mids = None, []
    for m in range(2):
        _, qkv, pq, pk, _ = entered[m]
        got = middle(m, held, x, dy, qkv, pq, pk, priors[m], later, vec, hidden)
        held = got[:7]
        mids.append(got[7:])
    out, a, h2, g, du, dmid, dmb = held
    laters = [prefix(mids[m][1], grid, True) for m in range(2)]
    g_later = weight_grads(h2, du, g, dy, a, dmb)
    kept, ends = None, []
    for m in range(2):
        _, qkv, pq, pk, _ = entered[m]
        got = leave(m, kept, x, qkv, pq, pk, priors[m], laters[m], mids[m][0], dmid, w_first, maps, vec)
        kept = got[:2]
        ends.append(got[2:])
    dqkv, dx = kept
    hid = jnp.concatenate([entered[0][0], entered[1][0]])
    g_qkv = first_grads(hid, dqkv)

    gmap = (ends[0][0] + ends[1][0]).reshape(2, pairs, 2, HD, 2, HD)
    gmap = jnp.stack([gmap[:, :, 0, :, 0], gmap[:, :, 1, :, 1]], axis=2)
    gmap = jnp.transpose(gmap, (1, 2, 4, 0, 3)).reshape(width, PAIR)
    inner = mids[0][2] + mids[1][2]
    outer = ends[0][1] + ends[1][1]
    g_fc_bias = inner[8 : 8 + ratio].T.reshape(ratio, width)
    vec_rows = [outer[0:1], inner[1:2], outer[2:6], inner[6:8], g_fc_bias, inner[12:13]]
    g_small = jnp.concatenate(vec_rows).T

    r_fc = scatter_rows(g_later[:, :hidden], grid, ("c", "x", "y", "z"))
    r_proj = scatter_rows(g_later[:, hidden : 2 * hidden], grid, ("c", "y", "x", "z"))
    last = jnp.concatenate(
        [
            g_qkv,
            g_later[:, 2 * hidden :],
            gmap.astype(LOW),
            jnp.pad(g_small.astype(LOW), ((0, 0), (0, PAIR - 13))),
        ],
        axis=1,
    )
    last = scatter_rows(last, grid, ("c", "x", "y", "z")).astype(F32)
    small = last[:, wide + width + PAIR :].T
    return (
        out.reshape(tokens.shape),
        dx.reshape(tokens.shape),
        last[:, :wide],
        jnp.transpose(last[:, wide + width : wide + width + PAIR].reshape(rows, 2, HD), (1, 0, 2)),
        last[:, wide : wide + width],
        r_fc.astype(F32).reshape(rows, ratio, width).swapaxes(1, 2).reshape(rows, hidden),
        r_proj.astype(F32).reshape(rows * ratio, width),
        small[:2],
        small[2:13],
    )


def solution(mesh):
    return jax.shard_map(
        shards,
        mesh=mesh,
        in_specs=(
            P(None, "dp", "seq", None),
            P(("dp", "seq"), None),
            P(None, ("dp", "seq"), None),
            P(("dp", "seq"), None),
            P(("dp", "seq"), None),
            P(("dp", "seq"), None),
            P(None, ("dp", "seq")),
            P(None, ("dp", "seq")),
            P(None, "dp", "seq", None),
        ),
        out_specs=(
            P(None, "dp", "seq", None),
            P(None, "dp", "seq", None),
            P(("dp", "seq"), None),
            P(None, ("dp", "seq"), None),
            P(("dp", "seq"), None),
            P(("dp", "seq"), None),
            P(("dp", "seq"), None),
            P(None, ("dp", "seq")),
            P(None, ("dp", "seq")),
        ),
        check_vma=False,
    )
```

```python
import functools

import jax
import jax.numpy as jnp
from jax import lax
from jax.experimental import pallas as pl
from jax.experimental.pallas import tpu as pltpu
from jax.sharding import PartitionSpec as P

HD = 64
PAIR = 2 * HD
AXES = ("dp", "seq")
LOW = jnp.bfloat16
F32 = jnp.float32
VMEM_BYTES = 60 * 1024 * 1024
ZROWS = 16

def grid_dims():
    n_dp, n_seq = lax.axis_size("dp"), lax.axis_size("seq")
    n_x = 1
    while n_x * n_x * 4 <= n_dp:
        n_x *= 2
    sizes = {"y": n_dp // n_x, "x": n_x, "z": n_seq // 2, "c": 2}
    at = lax.axis_index("dp") * n_seq + lax.axis_index("seq")
    place = {}
    for name in ("c", "z", "x", "y"):
        place[name] = lax.rem(at, sizes[name])
        at = at // sizes[name]
    return sizes, place


def turned(sizes, name, step):
    pairs = []
    for y in range(sizes["y"]):
        for x in range(sizes["x"]):
            for z in range(sizes["z"]):
                for c in range(sizes["c"]):
                    to = {"y": y, "x": x, "z": z, "c": c}
                    to[name] = (to[name] + step) % sizes[name]
                    flat = lambda p: ((p[0] * sizes["x"] + p[1]) * sizes["z"] + p[2]) * 2 + p[3]
                    pairs.append((flat((y, x, z, c)), flat((to["y"], to["x"], to["z"], to["c"]))))
    return pairs


def send(value, sizes, name, step):
    return lax.ppermute(value, AXES, turned(sizes, name, step))


def tie(value, *others):
    others = [other for other in others if other is not None]
    return lax.optimization_barrier((value, *others))[0] if others else value


def spread(own, got, place):
    at = lax.broadcasted_iota(jnp.int32, (2,) + (1,) * own.ndim, 0)
    return jnp.where(at == place, own[None], got[None])


def gather_dim(value, grid, name):
    sizes, place = grid
    count = sizes[name]
    if count == 1:
        return value[None]
    got = [value] + [send(value, sizes, name, k) for k in range(1, count)]
    if count == 2:
        return spread(got[0], got[1], place[name])
    order = jnp.stack(got[::-1] + got[::-1][:-1])
    return lax.dynamic_slice_in_dim(order, count - 1 - place[name], count, 0)


def gather_rows(value, grid):
    sizes, _ = grid
    out = gather_dim(value, grid, "z")
    columns = value.shape[1] // 2
    left, right = out[..., :columns], out[..., columns:]
    left, right = gather_dim(left, grid, "x"), gather_dim(right, grid, "y")
    left, right = gather_dim(left, grid, "y"), gather_dim(right, grid, "x")
    out = jnp.concatenate([left, jnp.swapaxes(right, 0, 1)], axis=-1)
    out = out.reshape((-1,) + value.shape)
    return out, send(out, sizes, "c", 1)


def scatter_dim(value, grid, name, axis, after=None):
    sizes, place = grid
    count = sizes[name]
    mine = lax.dynamic_index_in_dim(value, place[name], axis, keepdims=False)
    if count == 1:
        return mine
    total = mine.astype(F32)
    for k in range(1, count):
        to = lax.rem(place[name] + k, count)
        block = lax.dynamic_index_in_dim(value, to, axis, keepdims=False)
        total = total + tie(send(block, sizes, name, k), after).astype(F32)
    return total.astype(LOW)


class Scatter:
    def __init__(self, keep, give, grid, after=None):
        sizes, _ = grid
        self.grid = grid
        got = tie(send(give, sizes, "c", 1), after)
        shape = (sizes["y"], sizes["x"], sizes["z"]) + keep.shape[1:]
        keep, got = keep.reshape(shape), got.reshape(shape)
        cut = keep.shape[-1] // 256 * 128
        add = lambda a, b: (a.astype(F32) + b.astype(F32)).astype(LOW)
        self.left = add(keep[..., :cut], got[..., :cut])
        self.right = add(keep[..., cut:], got[..., cut:])

    def one(self, after=None):
        self.left = scatter_dim(self.left, self.grid, "x", 1, after)
        self.right = scatter_dim(self.right, self.grid, "y", 0, after)

    def two(self, after=None):
        self.left = scatter_dim(self.left, self.grid, "y", 0, after)
        self.right = scatter_dim(self.right, self.grid, "x", 0, after)

    def end(self, after=None):
        both = jnp.concatenate([self.left, self.right], axis=-1)
        return scatter_dim(both, self.grid, "z", 0, after)


def halves(value, grid, rows):
    _, place = grid
    value = value.reshape(-1, 2, rows, value.shape[-1])
    pick = lambda at: lax.dynamic_index_in_dim(value, at, 1, keepdims=False)
    return pick(place["c"]), pick(1 - place["c"])


def some(sizes, step, chosen):
    pairs = []
    for a, b in turned(sizes, "z", step):
        z = (a // 2) % sizes["z"]
        if 0 <= z + step < sizes["z"] and chosen(z):
            pairs.append((a, b))
    return pairs


def swap(own, grid):
    sizes, place = grid
    half = own.shape[0] // 2
    other = send(own, sizes, "c", 1)
    first = place["c"] * half
    mine = lax.dynamic_slice_in_dim(own, first, half, 0).astype(F32)
    mine = (mine + lax.dynamic_slice_in_dim(other, first, half, 0).astype(F32)).astype(LOW)
    return mine, other


class Steps:
    def __init__(self, mine, grid, reverse):
        self.running, self.total, self.span = mine, 0.0, 1
        self.sizes, self.reverse = grid[0], reverse

    def round(self, after=None):
        span = self.span
        if span >= self.sizes["z"]:
            return
        sign, end = (-1, span) if self.reverse else (1, span - 1)
        got = 0.0
        for d in range(1, span + 1):
            pairs = some(self.sizes, sign * d, lambda z: z % (2 * span) == end)
            got = got + tie(lax.ppermute(self.running, AXES, pairs), after).astype(F32)
        self.total = self.total + got
        self.running = (self.running.astype(F32) + got).astype(LOW)
        self.span = 2 * span

    def end(self, other, after=None):
        while self.span < self.sizes["z"]:
            self.round(after)
        total = jnp.asarray(self.total + jnp.zeros(self.running.shape, F32)).astype(LOW)
        return total, send(total, self.sizes, "c", 1), other


def dot(a, b):
    return jnp.dot(a, b, preferred_element_type=F32)


def dot_nt(a, b):
    return lax.dot_general(a, b, (((1,), (1,)), ((), ())), preferred_element_type=F32)


def dot_tn(a, b):
    return lax.dot_general(a, b, (((0,), (0,)), ((), ())), preferred_element_type=F32)


def normed(values):
    centred = values - jnp.mean(values, axis=-1, keepdims=True)
    spread = jnp.mean(centred * centred, axis=-1, keepdims=True)
    scale = lax.rsqrt(spread + 1e-05)
    return centred * scale, scale


def norm_back(grad, gain, unit, scale):
    eg = grad * gain
    inner = eg - jnp.mean(eg, axis=-1, keepdims=True)
    return scale * (inner - unit * jnp.mean(eg * unit, axis=-1, keepdims=True))


def lanes(shape=(PAIR, PAIR)):
    return lax.broadcasted_iota(jnp.int32, shape, 1)


def subs(shape=(PAIR, PAIR)):
    return lax.broadcasted_iota(jnp.int32, shape, 0)


def soft_pair(logits):
    high = jnp.max(logits, axis=0, keepdims=True)
    small = jnp.min(logits, axis=0, keepdims=True)
    e1 = jnp.exp(logits - high)
    e2 = jnp.exp(small - logits)
    p1 = e1 * (1.0 / jnp.sum(e1, axis=0, keepdims=True))
    p2 = e2 * (1.0 / jnp.sum(e2, axis=0, keepdims=True))
    return jnp.concatenate([p1, p2], axis=0)


def soft_back(phi, grad):
    prod = phi * grad
    s1 = jnp.sum(prod[:HD], axis=0, keepdims=True)
    s2 = jnp.sum(prod[HD:], axis=0, keepdims=True)
    return (prod[:HD] - phi[:HD] * s1) - (prod[HD:] - phi[HD:] * s2)


def prepare_kernel(core_ref, mine_ref, theirs_ref, w_ref, maps_ref, vec_ref):
    cut = w_ref.shape[-1] - 2 * PAIR

    def write(even_ref, odd_ref):
        w_ref[:, 0] = even_ref[...]
        w_ref[:, 1] = odd_ref[...]
        even = even_ref[:, :, cut:].astype(F32)[:, None]
        odd = odd_ref[:, :, cut:].astype(F32)[:, None]
        tail = jnp.concatenate([even, odd], axis=1)
        split_tail(tail.reshape(-1, 2 * PAIR), maps_ref, vec_ref)

    @pl.when(core_ref[0] == 0)
    def _():
        write(mine_ref, theirs_ref)

    @pl.when(core_ref[0] != 0)
    def _():
        write(theirs_ref, mine_ref)


def tail_kernel(tail_ref, maps_ref, vec_ref):
    split_tail(tail_ref[...].astype(F32), maps_ref, vec_ref)


def split_tail(tail, maps_ref, vec_ref):
    low = lanes((HD, PAIR)) < HD
    for p in range(maps_ref.shape[1]):
        at = slice(p * PAIR, (p + 1) * PAIR)
        both = tail[at, :PAIR].T
        for which in range(2):
            one = both[which * HD : (which + 1) * HD]
            block = [jnp.where(low, one, 0.0), jnp.where(low, 0.0, one)]
            maps_ref[which, p] = jnp.concatenate(block, axis=0).astype(LOW)
        vec_ref[:, at] = tail[at, PAIR:].T[:ZROWS]


def enter_kernel(x_ref, w_ref, maps_ref, vec_ref, *rest):
    hid_ref, qkv_ref, pq_ref, pk_ref, st_ref = rest[-5:]
    width = x_ref.shape[1]
    seqs = pq_ref.shape[0]
    heads = pq_ref.shape[1]
    unit, _ = normed(x_ref[...].astype(F32))
    hid_ref[...] = (unit * vec_ref[0:1, :] + vec_ref[2:3, :]).astype(LOW)
    for part in range(3):
        span = slice(part * width, (part + 1) * width)
        qkv_ref[:, span] = (dot(hid_ref[...], w_ref[:, span]) + vec_ref[3 + part : 4 + part, :]).astype(LOW)

    def one(s, carry):
        rows = pl.ds(pl.multiple_of(s * PAIR, PAIR), PAIR)
        lane = lanes()
        cols = jnp.zeros((PAIR, PAIR), F32)
        for p in range(heads // 2):
            at = slice(p * PAIR, (p + 1) * PAIR)
            for which, ref in ((0, pq_ref), (1, pk_ref)):
                value = qkv_ref[rows, which * width + p * PAIR : which * width + (p + 1) * PAIR]
                logits = dot_nt(maps_ref[which, p], value)
                ref[s, 2 * p] = soft_pair(logits[:HD]).astype(LOW)
                ref[s, 2 * p + 1] = soft_pair(logits[HD:]).astype(LOW)
            value = qkv_ref[rows, 2 * width + p * PAIR : 2 * width + (p + 1) * PAIR]
            own = []
            for h in (2 * p, 2 * p + 1):
                keys = pk_ref[s, h]
                own.append(dot(keys, value))
                cols = jnp.where(lane == h, jnp.sum(keys.astype(F32), axis=1, keepdims=True), cols)
            st_ref[s, at, :] = jnp.where(lane < HD, own[0], own[1]).astype(LOW)
        st_ref[s, width : width + ZROWS, :] = cols.T[:ZROWS].astype(LOW)
        return carry

    lax.fori_loop(0, seqs, one, 0)


def compose(s, core_ref, refs, out_ref, reverse):
    mine_ref, theirs_ref, other_ref = refs
    half = mine_ref.shape[0]
    at = lax.rem(s, half)
    core = core_ref[0]

    @pl.when(s // half == core)
    def _():
        out_ref[...] = mine_ref[at]

    @pl.when(s // half != core)
    def _():
        out_ref[...] = theirs_ref[at]

    @pl.when(core == (0 if reverse else 1))
    def _():
        out_ref[...] = (out_ref[...].astype(F32) + other_ref[s].astype(F32)).astype(LOW)


def middle_kernel(
    core_ref, x_ref, dy_ref, v_ref, pq_ref, pk_ref, pa_ref, pb_ref, po_ref, w_ref, vec_ref, *rest
):
    (out_ref, a_ref, h2_ref, g_ref, du_ref, dmid_ref, dmb_ref, dn_ref, ds_ref, sum_ref,
     ctx_s, den_s, unit_s, acc_s, back_s, pri_s) = rest[-16:]
    rows_all, width = x_ref.shape
    seqs, heads = pq_ref.shape[0], pq_ref.shape[1]
    blocks = g_ref.shape[1] // width
    hidden = g_ref.shape[1]

    sum_ref[...] = jnp.zeros_like(sum_ref)

    def attend(s, carry):
        compose(s, core_ref, (pa_ref, pb_ref, po_ref), pri_s, False)
        rows = pl.ds(pl.multiple_of(s * PAIR, PAIR), PAIR)
        lane, sub = lanes(), subs()
        zsum = pri_s[width : width + ZROWS, :].astype(F32)
        for p in range(heads // 2):
            at = slice(p * PAIR, (p + 1) * PAIR)
            left, dens = [], []
            for h in (2 * p, 2 * p + 1):
                phi = pq_ref[s, h].T
                score = jnp.where(sub >= lane, dot(phi, pk_ref[s, h]), 0.0).astype(LOW)
                dens.append(
                    jnp.sum(
                        score.astype(F32) + phi.astype(F32) * zsum[h : h + 1, :],
                        axis=1,
                        keepdims=True,
                    )
                )
                left.append(jnp.concatenate([score, phi], axis=1))
            right = jnp.concatenate([v_ref[rows, at], pri_s[at, :]], axis=0)
            both = dot(jnp.concatenate(left, axis=0), right)
            numer = jnp.where(lane < HD, both[:PAIR], both[PAIR:])
            den = jnp.where(lane < HD, dens[0], dens[1])
            ctx = numer / den
            ctx_s[rows, at] = ctx
            den_s[rows, at] = den
            a_ref[rows, at] = ctx.astype(LOW)
        return carry

    lax.fori_loop(0, seqs, attend, 0)

    w_out = w_ref[:, 2 * hidden : 2 * hidden + width]
    mid = x_ref[...].astype(F32) + dot(a_ref[...], w_out) + vec_ref[6:7, :]
    acc_s[...] = mid + vec_ref[12:13, :]
    unit, scale = normed(mid)
    unit_s[...] = unit
    h2_ref[...] = (unit * vec_ref[1:2, :] + vec_ref[7:8, :]).astype(LOW)
    back_s[...] = jnp.zeros_like(back_s)
    c0 = 0.7978845608028654
    c1 = 0.044715

    def mlp(j, carry):
        at = pl.ds(pl.multiple_of(j * width, width), width)
        at2 = pl.ds(pl.multiple_of(hidden + j * width, width), width)
        u = dot(h2_ref[...], w_ref[:, at]) + vec_ref[pl.ds(8 + j, 1), :]
        dg = dot_nt(dy_ref[...], w_ref[:, at2])
        sq = u * u
        th = jnp.tanh(c0 * (u + c1 * (u * sq)))
        half = 0.5 + 0.5 * th
        g = (u * half).astype(LOW)
        slope = half + (0.5 * u) * ((1.0 - th * th) * (c0 + (3.0 * c0 * c1) * sq))
        du = (slope * dg).astype(LOW)
        g_ref[:, at] = g
        du_ref[:, at] = du
        sum_ref[pl.ds(8 + j, 1), :] = jnp.sum(du.astype(F32), axis=0, keepdims=True)
        acc_s[...] += dot(g, w_ref[:, at2])
        back_s[...] += dot_nt(du, w_ref[:, at])
        return carry

    lax.fori_loop(0, blocks, mlp, 0)
    out_ref[...] = acc_s[...].astype(LOW)
    dy = dy_ref[...].astype(F32)
    e = back_s[...]
    unit = unit_s[...]
    sum_ref[12:13, :] = jnp.sum(dy, axis=0, keepdims=True)
    sum_ref[1:2, :] = jnp.sum(e * unit, axis=0, keepdims=True)
    sum_ref[7:8, :] = jnp.sum(e, axis=0, keepdims=True)
    dmid = dy + norm_back(e, vec_ref[1:2, :], unit, scale)
    dmid_ref[...] = dmid
    dmb = dmid.astype(LOW)
    dmb_ref[...] = dmb
    sum_ref[6:7, :] = jnp.sum(dmb.astype(F32), axis=0, keepdims=True)
    back_s[...] = dot_nt(dmb, w_ref[:, 2 * hidden : 2 * hidden + width])

    def back(s, carry):
        rows = pl.ds(pl.multiple_of(s * PAIR, PAIR), PAIR)
        lane = lanes()
        low = lane < HD
        cols = jnp.zeros((PAIR, PAIR), F32)
        for p in range(heads // 2):
            at = slice(p * PAIR, (p + 1) * PAIR)
            dctx = back_s[rows, at]
            inv = 1.0 / den_s[rows, at]
            dn = dctx * inv
            prod = dctx * ctx_s[rows, at]
            swapped = pltpu.roll(inv, HD, 1)
            got = []
            for h, mine, first in ((2 * p, low, HD), (2 * p + 1, jnp.logical_not(low), 0)):
                dd = -jnp.sum(jnp.where(mine, prod, 0.0), axis=1, keepdims=True) * swapped
                rest_dd = dd - dd.astype(LOW).astype(F32)
                tail = jnp.where(lane == first, dd, jnp.where(lane == first + 1, rest_dd, 0.0))
                aug = jnp.where(mine, dn, tail).astype(LOW)
                dn_ref[rows, h * PAIR : (h + 1) * PAIR] = aug
                ds = dot(pq_ref[s, h], aug)
                got.append(ds)
                edge = jnp.logical_or(lane == first, lane == first + 1)
                col = jnp.sum(jnp.where(edge, ds, 0.0), axis=1, keepdims=True)
                cols = jnp.where(lane == h, col, cols)
            ds_ref[s, at, :] = jnp.where(low, got[0], got[1]).astype(LOW)
        ds_ref[s, width : width + ZROWS, :] = cols.T[:ZROWS].astype(LOW)
        return carry

    lax.fori_loop(0, seqs, back, 0)


def leave_kernel(
    core_ref, qkv_ref, pq_ref, pk_ref, pa_ref, pb_ref, po_ref, la_ref, lb_ref, lo_ref, dn_ref, maps_ref, *rest
):
    dqkv_ref, gmap_ref, pri_s, dl_s = rest[-4:]
    width = qkv_ref.shape[1] // 3
    seqs, heads = pq_ref.shape[0], pq_ref.shape[1]
    gmap_ref[...] = jnp.zeros_like(gmap_ref)

    def back(s, carry):
        compose(s, core_ref, (pa_ref, pb_ref, po_ref), pri_s, False)
        compose(s, core_ref, (la_ref, lb_ref, lo_ref), dl_s, True)
        rows = pl.ds(pl.multiple_of(s * PAIR, PAIR), PAIR)
        lane, sub = lanes(), subs()
        low = lane < HD
        fill = jnp.zeros((PAIR - ZROWS, PAIR), F32)
        zcol = jnp.concatenate([pri_s[width : width + ZROWS, :].astype(F32), fill], axis=0).T
        dzcol = jnp.concatenate([dl_s[width : width + ZROWS, :].astype(F32), fill], axis=0).T
        for p in range(heads // 2):
            at = slice(p * PAIR, (p + 1) * PAIR)
            vp = qkv_ref[rows, 2 * width + p * PAIR : 2 * width + (p + 1) * PAIR]
            prior = pri_s[at, :]
            dl = dl_s[at, :]
            left, dfq, dfk, dns = [], [], [], []
            for h, mine, first in ((2 * p, low, HD), (2 * p + 1, jnp.logical_not(low), 0)):
                edge = jnp.logical_or(lane == first, lane == first + 1)
                pq, pk = pq_ref[s, h], pk_ref[s, h]
                dn = dn_ref[rows, h * PAIR : (h + 1) * PAIR]
                vaug = jnp.where(mine, vp.astype(F32), jnp.where(edge, 1.0, 0.0)).astype(LOW)
                saug = jnp.where(
                    mine, prior.astype(F32), jnp.where(edge, zcol[:, h : h + 1], 0.0)
                ).astype(LOW)
                laug = jnp.where(
                    mine, dl.astype(F32), jnp.where(lane == first, dzcol[:, h : h + 1], 0.0)
                ).astype(LOW)
                da = jnp.where(sub >= lane, dot_nt(dn, vaug), 0.0).astype(LOW)
                dpq = dot_nt(
                    jnp.concatenate([pk, saug], axis=1), jnp.concatenate([da, dn], axis=1)
                )
                dpk = dot(pq, da) + dot_nt(laug, vaug)
                dfq.append(soft_back(pq.astype(F32), dpq).astype(LOW))
                dfk.append(soft_back(pk.astype(F32), dpk).astype(LOW))
                keys = pk.T
                score = jnp.where(sub <= lane, dot(keys, pq), 0.0).astype(LOW)
                left.append(jnp.concatenate([score, keys], axis=1))
                dns.append(dn)
            dn = jnp.where(low, dns[0].astype(F32), dns[1].astype(F32)).astype(LOW)
            both = dot(jnp.concatenate(left, axis=0), jnp.concatenate([dn, dl], axis=0))
            dv = jnp.where(low, both[:PAIR], both[PAIR:])
            dqkv_ref[rows, 2 * width + p * PAIR : 2 * width + (p + 1) * PAIR] = dv.astype(LOW)
            for which, parts in ((0, dfq), (1, dfk)):
                df = jnp.concatenate(parts, axis=0)
                mine_at = slice(which * width + p * PAIR, which * width + (p + 1) * PAIR)
                gmap_ref[which, p] += dot(df, qkv_ref[rows, mine_at])
                dqkv_ref[rows, mine_at] = dot(df.T, maps_ref[which, p]).astype(LOW)
        return carry

    lax.fori_loop(0, seqs, back, 0)


def norm_kernel(x_ref, d_ref, w_ref, dmid_ref, vec_ref, dx_ref):
    e = dot_nt(d_ref[...], w_ref[...])
    unit, scale = normed(x_ref[...].astype(F32))
    dx_ref[...] = dmid_ref[...] + norm_back(e, vec_ref[0:1, :], unit, scale)


def put(value, core_ref, keep_ref, give_ref):
    count, rows, _ = keep_ref.shape
    value = value.reshape(count, 2, rows, value.shape[-1])
    even, odd = value[:, 0], value[:, 1]
    low = core_ref[0] == 0
    keep_ref[...] = jnp.where(low, even, odd).astype(LOW)
    give_ref[...] = jnp.where(low, odd, even).astype(LOW)


def weight_kernel(core_ref, h2_ref, du_ref, g_ref, dy_ref, a_ref, dmb_ref, *outs):
    step = pl.program_id(0)
    blocks = (pl.num_programs(0) - 1) // 2

    def write(value):
        if len(outs) == 1:
            outs[0][...] = value.astype(LOW)
        else:
            put(value, core_ref, *outs)

    @pl.when(step < blocks)
    def _():
        write(dot_tn(h2_ref[...], du_ref[...]))

    @pl.when(jnp.logical_and(step >= blocks, step < 2 * blocks))
    def _():
        write(dot_tn(g_ref[...], dy_ref[...]))

    @pl.when(step == 2 * blocks)
    def _():
        write(dot_tn(a_ref[...], dmb_ref[...]))


def first_kernel(core_ref, h_ref, d_ref, w_ref, g0_ref, g1_ref, row_ref, *rest):
    outs, (turn_s, rows_s, gain_s, shift_s) = rest[:-4], rest[-4:]
    step = pl.program_id(0)
    last = pl.num_programs(0) - 1
    size = w_ref.shape[1]
    width = w_ref.shape[0]
    each = width // size

    def write(value):
        if len(outs) == 1:
            outs[0][...] = value.astype(LOW)
        else:
            put(value, core_ref, *outs)

    @pl.when(step == 0)
    def _():
        turn_s[...] = h_ref[...].T
        rows_s[...] = row_ref[...]
        gain_s[...] = jnp.zeros_like(gain_s)
        shift_s[...] = jnp.zeros_like(shift_s)

    @pl.when(step < last)
    def _():
        value = dot(turn_s[...], d_ref[...])
        write(value)
        w = w_ref[...].astype(F32)
        sums = jnp.sum(d_ref[...].astype(F32), axis=0, keepdims=True)
        at = pl.multiple_of(lax.rem(step, each) * size, size)
        rows_s[pl.ds(3 + step // each, 1), pl.ds(at, size)] = sums
        gain_s[...] += jnp.sum(w * value, axis=1, keepdims=True)
        shift_s[...] += jnp.sum(w * sums, axis=1, keepdims=True)

    @pl.when(step == last)
    def _():
        lane, sub = lanes(), subs()
        fill = jnp.zeros((PAIR - ZROWS, PAIR), F32)
        blocks = []
        for p in range(g0_ref.shape[1]):
            at = slice(p * PAIR, (p + 1) * PAIR)
            q = (g0_ref[0, p] + g1_ref[0, p]).T
            k = (g0_ref[1, p] + g1_ref[1, p]).T
            upper = sub < HD
            q = jnp.where(upper, q, pltpu.roll(q, HD, 1))
            k = jnp.where(upper, pltpu.roll(k, HD, 1), k)
            cols = jnp.concatenate([rows_s[:, at], fill], axis=0).T
            own = w_ref[at, PAIR:].astype(F32)
            shift = shift_s[at]
            gain = (gain_s[at] - own[:, 2:3] * shift) / own[:, 0:1]
            cols = jnp.where(lane == 0, gain, jnp.where(lane == 2, shift, cols))
            blocks.append(jnp.concatenate([jnp.where(lane < HD, q, k), cols], axis=1))
        write(jnp.concatenate(blocks, axis=0))


def whole(shape):
    return pl.BlockSpec(shape, lambda i: (0,) * len(shape), pipeline_mode=pl.Buffered(1))


def part(shape, *at):
    return pl.BlockSpec(shape, lambda i: at, pipeline_mode=pl.Buffered(1))


PLAIN = pltpu.CompilerParams(vmem_limit_bytes=VMEM_BYTES)
PARAMS = dict(
    compiler_params=pltpu.CompilerParams(
        dimension_semantics=("arbitrary",), vmem_limit_bytes=VMEM_BYTES
    )
)


def cost(flops, size):
    return pl.CostEstimate(flops=20 * int(flops), bytes_accessed=20 * int(size), transcendentals=0)


def enter(m, held, x, w, maps, vec, heads):
    total, width = x.shape
    rows = total // 2
    seqs = rows // PAIR
    pack = width + ZROWS
    extra = [] if held is None else [held]
    return pl.pallas_call(
        enter_kernel,
        grid=(1,),
        in_specs=[
            part((rows, width), m, 0),
            part((width, 3 * width), 0, 0),
            whole(maps.shape),
            whole(vec.shape),
        ]
        + [pl.BlockSpec(memory_space=pl.ANY)] * len(extra),
        out_specs=[
            part((rows, width), m, 0),
            whole((rows, 3 * width)),
            whole((seqs, heads, PAIR, PAIR)),
            whole((seqs, heads, PAIR, PAIR)),
            whole((seqs, pack, PAIR)),
        ],
        out_shape=[
            jax.ShapeDtypeStruct((total, width), LOW),
            jax.ShapeDtypeStruct((rows, 3 * width), LOW),
            jax.ShapeDtypeStruct((seqs, heads, PAIR, PAIR), LOW),
            jax.ShapeDtypeStruct((seqs, heads, PAIR, PAIR), LOW),
            jax.ShapeDtypeStruct((seqs, pack, PAIR), LOW),
        ],
        input_output_aliases={4 + k: k for k in range(len(extra))},
        cost_estimate=cost(6 * rows * width * width, 12 * rows * width),
        name="enter",
        **PARAMS,
    )(x, w, maps, vec, *extra)


def middle(m, held, core, x, dy, qkv, pq, pk, pri, w, vec, hidden):
    total, width = x.shape
    rows = total // 2
    seqs, heads = pq.shape[0], pq.shape[1]
    pack = width + ZROWS
    extra = [] if held is None else list(held)
    shared = [
        ((total, width), LOW, (rows, width)),
        ((total, width), LOW, (rows, width)),
        ((total, width), LOW, (rows, width)),
        ((total, hidden), LOW, (rows, hidden)),
        ((total, hidden), LOW, (rows, hidden)),
        ((total, width), F32, (rows, width)),
        ((total, width), LOW, (rows, width)),
    ]
    return pl.pallas_call(
        middle_kernel,
        grid=(1,),
        in_specs=[
            pl.BlockSpec(memory_space=pltpu.SMEM),
            part((rows, width), m, 0),
            part((rows, width), m, 0),
            part((rows, width), 0, 2),
            whole(pq.shape),
            whole(pk.shape),
        ]
        + [whole(piece.shape) for piece in pri]
        + [whole(w.shape), whole(vec.shape)]
        + [pl.BlockSpec(memory_space=pl.ANY)] * len(extra),
        out_specs=[part(b, m, 0) for _, _, b in shared]
        + [whole((rows, heads * PAIR)), whole((seqs, pack, PAIR)), whole((ZROWS, width))],
        out_shape=[jax.ShapeDtypeStruct(s, t) for s, t, _ in shared]
        + [
            jax.ShapeDtypeStruct((rows, heads * PAIR), LOW),
            jax.ShapeDtypeStruct((seqs, pack, PAIR), LOW),
            jax.ShapeDtypeStruct((ZROWS, width), F32),
        ],
        scratch_shapes=[pltpu.VMEM((rows, width), F32)] * 5 + [pltpu.VMEM((pack, PAIR), LOW)],
        input_output_aliases={11 + k: k for k in range(len(extra))},
        cost_estimate=cost(8 * rows * width * hidden + 4 * rows * width * width, 30 * rows * width),
        name="middle",
        **PARAMS,
    )(core, x, dy, qkv, pq, pk, *pri, w, vec, *extra)


def leave(m, held, core, qkv, pq, pk, pri, dl, dn, maps):
    rows, wide = qkv.shape
    total = 2 * rows
    extra = [] if held is None else [held]
    return pl.pallas_call(
        leave_kernel,
        grid=(1,),
        in_specs=[
            pl.BlockSpec(memory_space=pltpu.SMEM),
            whole(qkv.shape),
            whole(pq.shape),
            whole(pk.shape),
        ]
        + [whole(piece.shape) for piece in (*pri, *dl)]
        + [whole(dn.shape), whole(maps.shape)]
        + [pl.BlockSpec(memory_space=pl.ANY)] * len(extra),
        out_specs=[part((rows, wide), m, 0), whole(maps.shape)],
        out_shape=[
            jax.ShapeDtypeStruct((total, wide), LOW),
            jax.ShapeDtypeStruct(maps.shape, F32),
        ],
        scratch_shapes=[pltpu.VMEM(pri[0].shape[1:], LOW)] * 2,
        input_output_aliases={12 + k: k for k in range(len(extra))},
        cost_estimate=cost(8 * rows * wide * PAIR, 8 * rows * wide),
        name="leave",
        **PARAMS,
    )(core, qkv, pq, pk, *pri, *dl, dn, maps, *extra)


def norm_grads(x, dqkv, w, dmid, vec):
    total, width = x.shape
    rows = min(total, 256)
    return pl.pallas_call(
        norm_kernel,
        grid=(total // rows,),
        in_specs=[
            pl.BlockSpec((rows, width), lambda i: (i, 0)),
            pl.BlockSpec((rows, 3 * width), lambda i: (i, 0)),
            part((width, 3 * width), 0, 0),
            pl.BlockSpec((rows, width), lambda i: (i, 0)),
            whole(vec.shape),
        ],
        out_specs=pl.BlockSpec((rows, width), lambda i: (i, 0)),
        out_shape=jax.ShapeDtypeStruct((total, width), F32),
        cost_estimate=cost(6 * total * width * width, 12 * total * width),
        name="norm",
        **PARAMS,
    )(x, dqkv, w, dmid, vec)


def prepare(core, mine, theirs, heads):
    count, rows, columns = mine.shape
    width = 2 * count * rows
    outs = [
        jax.ShapeDtypeStruct((2, heads // 2, PAIR, PAIR), LOW),
        jax.ShapeDtypeStruct((ZROWS, width), F32),
    ]
    if rows % 8 != 0:
        low = core[0] == 0
        both = [jnp.where(low, mine, theirs), jnp.where(low, theirs, mine)]
        w = jnp.stack(both, axis=1).reshape(width, columns)
        maps, vec = pl.pallas_call(
            tail_kernel, out_shape=outs, name="tail", compiler_params=PLAIN
        )(w[:, columns - 2 * PAIR :])
        return w, maps, vec
    w, maps, vec = pl.pallas_call(
        prepare_kernel,
        grid=(1,),
        in_specs=[
            pl.BlockSpec(memory_space=pltpu.SMEM),
            whole(mine.shape),
            whole(theirs.shape),
        ],
        out_specs=[
            whole((count, 2, rows, columns)),
            whole(outs[0].shape),
            whole(outs[1].shape),
        ],
        out_shape=[jax.ShapeDtypeStruct((count, 2, rows, columns), LOW)] + outs,
        name="prepare",
        **PARAMS,
    )(core, mine, theirs)
    return w.reshape(width, columns), maps, vec


def out_halves(width, rows, columns, size):
    if rows % 8 != 0:
        return (
            [pl.BlockSpec((width, size), lambda i: (0, i))],
            [jax.ShapeDtypeStruct((width, columns), LOW)],
        )
    count = width // rows // 2
    return (
        [pl.BlockSpec((count, rows, size), lambda i: (0, 0, i))] * 2,
        [jax.ShapeDtypeStruct((count, rows, columns), LOW)] * 2,
    )


def weight_grads(core, rows, h2, du, g, dy, a, dmb):
    total, width = h2.shape
    blocks = du.shape[1] // width
    last = 2 * blocks
    block = (total, width)
    specs, shapes = out_halves(width, rows, (last + 1) * width, width)
    return pl.pallas_call(
        weight_kernel,
        grid=(last + 1,),
        in_specs=[
            pl.BlockSpec(memory_space=pltpu.SMEM),
            pl.BlockSpec(block, lambda i: (0, 0)),
            pl.BlockSpec(block, lambda i: (0, jnp.minimum(i, blocks - 1))),
            pl.BlockSpec(block, lambda i: (0, jnp.clip(i - blocks, 0, blocks - 1))),
            pl.BlockSpec(block, lambda i: (0, 0)),
            pl.BlockSpec(block, lambda i: (0, 0)),
            pl.BlockSpec(block, lambda i: (0, 0)),
        ],
        out_specs=specs,
        out_shape=shapes,
        cost_estimate=cost(2 * total * width * width * (last + 1), 20 * total * width),
        name="weights",
        **PARAMS,
    )(core, h2, du, g, dy, a, dmb)


def first_grads(core, rows, hid, dqkv, w, gmaps, sums):
    total, width = hid.shape
    size = 2 * PAIR
    steps = w.shape[1] // size
    specs, shapes = out_halves(width, rows, w.shape[1], size)
    return pl.pallas_call(
        first_kernel,
        grid=(steps,),
        in_specs=[
            pl.BlockSpec(memory_space=pltpu.SMEM),
            whole(hid.shape),
            pl.BlockSpec((total, size), lambda i: (0, jnp.minimum(i, steps - 2))),
            pl.BlockSpec((width, size), lambda i: (0, i)),
            whole(gmaps[0].shape),
            whole(gmaps[1].shape),
            whole(sums.shape),
        ],
        out_specs=specs,
        out_shape=shapes,
        scratch_shapes=[
            pltpu.VMEM((width, total), LOW),
            pltpu.VMEM((ZROWS, width), F32),
            pltpu.VMEM((width, 1), F32),
            pltpu.VMEM((width, 1), F32),
        ],
        cost_estimate=cost(6 * total * width * width, 12 * total * width),
        name="first",
        **PARAMS,
    )(core, hid, dqkv, w, *gmaps, sums)


def shards(tokens, w_qkv, w_feat, w_out, w_fc, w_proj, gains, biases, cotangent):
    micro_count, seq_count, seg_len, width = tokens.shape
    grid = grid_dims()
    rows = w_qkv.shape[0]
    hidden = w_fc.shape[1]
    ratio = hidden // width
    heads = width // HD
    pairs = heads // 2
    wide = 3 * width
    total = micro_count * seq_count * seg_len

    first = jnp.concatenate(
        [
            w_qkv.astype(LOW),
            jnp.transpose(w_feat, (1, 0, 2)).reshape(rows, PAIR).astype(LOW),
            jnp.pad(jnp.concatenate([gains, biases]).T.astype(LOW), ((0, 0), (0, PAIR - 13))),
        ],
        axis=1,
    )
    core = jnp.reshape(grid[1]["c"], (1,))
    first, maps, vec = prepare(core, *gather_rows(first, grid), heads)
    later = jnp.concatenate(
        [
            w_fc.astype(LOW).reshape(rows, width, ratio).swapaxes(1, 2).reshape(rows, hidden),
            w_proj.astype(LOW).reshape(rows, hidden),
            w_out.astype(LOW),
        ],
        axis=1,
    )
    later = lax.all_gather(later, AXES, axis=0, tiled=True)
    fc_bias = vec[8 : 8 + ratio].reshape(width, ratio).T
    mid_vec = jnp.concatenate([vec[:8], fc_bias, vec[8 + ratio :]])
    x = tokens.reshape(total, width)
    dy = cotangent.reshape(total, width)

    entered, swaps, steps = [], [], []
    for m in range(2):
        held = entered[0][0] if m else None
        held_vec = tie(vec, swaps[0][0]) if m else vec
        entered.append(enter(m, held, x, first, maps, held_vec, heads))
        own = entered[m][4]
        if m:
            steps[0].round(entered[1][1])
            own = tie(own, steps[0].running)
        swaps.append(swap(own, grid))
        steps.append(Steps(swaps[m][0], grid, False))
    hid = entered[1][0]
    steps[1].round()
    ready = steps[1].running
    priors = [steps[m].end(swaps[m][1]) for m in range(2)]
    held, mids, swaps, steps = None, [], [], []
    for m in range(2):
        _, qkv, pq, pk, _ = entered[m]
        held_vec = tie(mid_vec, swaps[0][0] if m else ready)
        got = middle(m, held, core, x, dy, qkv, pq, pk, priors[m], later, held_vec, hidden)
        held, rest = got[:7], got[7:]
        mids.append(rest)
        own = rest[1]
        if m:
            steps[0].round(rest[2])
            own = tie(own, steps[0].running)
        swaps.append(swap(own, grid))
        steps.append(Steps(swaps[m][0], grid, True))
    out, a, h2, g, du, dmid, dmb = held
    g_later = weight_grads(tie(core, swaps[1][0]), rows, h2, du, g, dy, a, dmb)
    if len(g_later) == 1:
        g_later = halves(g_later[0], grid, rows)
    inner = mids[0][2] + mids[1][2]
    g_fc_bias = inner[8 : 8 + ratio].T.reshape(ratio, width)
    sums = jnp.concatenate([inner[:8], g_fc_bias, inner[8 + ratio :]])
    keep, give = g_later
    laters = [steps[0].end(swaps[0][1], give)]
    steps[1].round(give)
    _, qkv, pq, pk, _ = entered[0]
    kept, gmap = leave(0, None, core, qkv, pq, pk, priors[0], laters[0], mids[0][0], maps)
    gmaps = [gmap]
    scatter = Scatter(keep, tie(give, laters[0][0], steps[1].running), grid, gmap)
    laters.append(steps[1].end(swaps[1][1], gmap))
    _, qkv, pq, pk, _ = entered[1]
    held_core = tie(core, scatter.left, scatter.right)
    dqkv, gmap = leave(1, kept, held_core, qkv, pq, pk, priors[1], laters[1], mids[1][0], maps)
    gmaps.append(gmap)
    scatter.one(gmap)
    held_core = tie(core, scatter.left, scatter.right)
    g_qkv = first_grads(held_core, rows, hid, dqkv, first, gmaps, sums)
    if len(g_qkv) == 1:
        g_qkv = halves(g_qkv[0], grid, rows)
    ending = Scatter(*g_qkv, grid)
    scatter.two(g_qkv[0])
    dx = norm_grads(x, dqkv, first, dmid, tie(vec, ending.left, ending.right))
    scatter.left = tie(scatter.left, ending.left)
    ending.one(dx)
    r_later = scatter.end(dx)
    ending.two()
    last = ending.end().astype(F32)
    r_fc = r_later[:, :hidden]
    r_proj = r_later[:, hidden : 2 * hidden]
    r_out = r_later[:, 2 * hidden :]
    small = last[:, wide + PAIR :].T
    return (
        out.reshape(tokens.shape),
        dx.reshape(tokens.shape),
        last[:, :wide],
        jnp.transpose(last[:, wide : wide + PAIR].reshape(rows, 2, HD), (1, 0, 2)),
        r_out.astype(F32),
        r_fc.astype(F32).reshape(rows, ratio, width).swapaxes(1, 2).reshape(rows, hidden),
        r_proj.astype(F32).reshape(rows * ratio, width),
        small[:2],
        small[2:13],
    )


def solution(mesh):
    return jax.shard_map(
        shards,
        mesh=mesh,
        in_specs=(
            P(None, "dp", "seq", None),
            P(("dp", "seq"), None),
            P(None, ("dp", "seq"), None),
            P(("dp", "seq"), None),
            P(("dp", "seq"), None),
            P(("dp", "seq"), None),
            P(None, ("dp", "seq")),
            P(None, ("dp", "seq")),
            P(None, "dp", "seq", None),
        ),
        out_specs=(
            P(None, "dp", "seq", None),
            P(None, "dp", "seq", None),
            P(("dp", "seq"), None),
            P(None, ("dp", "seq"), None),
            P(("dp", "seq"), None),
            P(("dp", "seq"), None),
            P(("dp", "seq"), None),
            P(None, ("dp", "seq")),
            P(None, ("dp", "seq")),
        ),
        check_vma=False,
    )
```

```python
import functools

import jax
import jax.numpy as jnp
from jax import lax
from jax.experimental import pallas as pl
from jax.experimental.pallas import tpu as pltpu
from jax.sharding import PartitionSpec as P

HD = 64
PAIR = 2 * HD
AXES = ("dp", "seq")
LOW = jnp.bfloat16
F32 = jnp.float32
VMEM_BYTES = 60 * 1024 * 1024
ZROWS = 16

def grid_dims():
    n_dp, n_seq = lax.axis_size("dp"), lax.axis_size("seq")
    n_x = 1
    while n_x * n_x * 4 <= n_dp:
        n_x *= 2
    sizes = {"y": n_dp // n_x, "x": n_x, "z": n_seq // 2, "c": 2}
    at = lax.axis_index("dp") * n_seq + lax.axis_index("seq")
    place = {}
    for name in ("c", "z", "x", "y"):
        place[name] = lax.rem(at, sizes[name])
        at = at // sizes[name]
    return sizes, place


def turned(sizes, name, step):
    pairs = []
    for y in range(sizes["y"]):
        for x in range(sizes["x"]):
            for z in range(sizes["z"]):
                for c in range(sizes["c"]):
                    to = {"y": y, "x": x, "z": z, "c": c}
                    to[name] = (to[name] + step) % sizes[name]
                    flat = lambda p: ((p[0] * sizes["x"] + p[1]) * sizes["z"] + p[2]) * 2 + p[3]
                    pairs.append((flat((y, x, z, c)), flat((to["y"], to["x"], to["z"], to["c"]))))
    return pairs


def send(value, sizes, name, step):
    return lax.ppermute(value, AXES, turned(sizes, name, step))


def tie(value, *others):
    others = [other for other in others if other is not None]
    return lax.optimization_barrier((value, *others))[0] if others else value


def spread(own, got, place):
    at = lax.broadcasted_iota(jnp.int32, (2,) + (1,) * own.ndim, 0)
    return jnp.where(at == place, own[None], got[None])


def gather_dim(value, grid, name):
    sizes, place = grid
    count = sizes[name]
    if count == 1:
        return value[None]
    got = [value] + [send(value, sizes, name, k) for k in range(1, count)]
    if count == 2:
        return spread(got[0], got[1], place[name])
    order = jnp.stack(got[::-1] + got[::-1][:-1])
    return lax.dynamic_slice_in_dim(order, count - 1 - place[name], count, 0)


def gather_rows(value, grid):
    sizes, _ = grid
    out = gather_dim(value, grid, "z")
    columns = value.shape[1] // 2
    left, right = out[..., :columns], out[..., columns:]
    left, right = gather_dim(left, grid, "x"), gather_dim(right, grid, "y")
    left, right = gather_dim(left, grid, "y"), gather_dim(right, grid, "x")
    out = jnp.concatenate([left, jnp.swapaxes(right, 0, 1)], axis=-1)
    out = out.reshape((-1,) + value.shape)
    return out, send(out, sizes, "c", 1)


def scatter_dim(value, grid, name, axis, after=None):
    sizes, place = grid
    count = sizes[name]
    mine = lax.dynamic_index_in_dim(value, place[name], axis, keepdims=False)
    if count == 1:
        return mine
    total = mine.astype(F32)
    for k in range(1, count):
        to = lax.rem(place[name] + k, count)
        block = lax.dynamic_index_in_dim(value, to, axis, keepdims=False)
        total = total + tie(send(block, sizes, name, k), after).astype(F32)
    return total.astype(LOW)


class Scatter:
    def __init__(self, keep, give, grid, after=None):
        sizes, _ = grid
        self.grid = grid
        got = tie(send(give, sizes, "c", 1), after)
        shape = (sizes["y"], sizes["x"], sizes["z"]) + keep.shape[1:]
        keep, got = keep.reshape(shape), got.reshape(shape)
        cut = keep.shape[-1] // 256 * 128
        add = lambda a, b: (a.astype(F32) + b.astype(F32)).astype(LOW)
        self.left = add(keep[..., :cut], got[..., :cut])
        self.right = add(keep[..., cut:], got[..., cut:])

    def one(self, after=None):
        self.left = scatter_dim(self.left, self.grid, "x", 1, after)
        self.right = scatter_dim(self.right, self.grid, "y", 0, after)

    def two(self, after=None):
        self.left = scatter_dim(self.left, self.grid, "y", 0, after)
        self.right = scatter_dim(self.right, self.grid, "x", 0, after)

    def end(self, after=None):
        both = jnp.concatenate([self.left, self.right], axis=-1)
        return scatter_dim(both, self.grid, "z", 0, after)


def halves(value, grid, rows):
    _, place = grid
    value = value.reshape(-1, 2, rows, value.shape[-1])
    pick = lambda at: lax.dynamic_index_in_dim(value, at, 1, keepdims=False)
    return pick(place["c"]), pick(1 - place["c"])


def some(sizes, step, chosen):
    pairs = []
    for a, b in turned(sizes, "z", step):
        z = (a // 2) % sizes["z"]
        if 0 <= z + step < sizes["z"] and chosen(z):
            pairs.append((a, b))
    return pairs


def swap(own, grid):
    sizes, place = grid
    half = own.shape[0] // 2
    other = send(own, sizes, "c", 1)
    first = place["c"] * half
    mine = lax.dynamic_slice_in_dim(own, first, half, 0).astype(F32)
    mine = (mine + lax.dynamic_slice_in_dim(other, first, half, 0).astype(F32)).astype(LOW)
    return mine, other


class Steps:
    def __init__(self, mine, grid, reverse):
        self.running, self.total, self.span = mine, 0.0, 1
        self.sizes, self.reverse = grid[0], reverse

    def round(self, after=None):
        span = self.span
        if span >= self.sizes["z"]:
            return
        sign, end = (-1, span) if self.reverse else (1, span - 1)
        got = 0.0
        for d in range(1, span + 1):
            pairs = some(self.sizes, sign * d, lambda z: z % (2 * span) == end)
            got = got + tie(lax.ppermute(self.running, AXES, pairs), after).astype(F32)
        self.total = self.total + got
        self.running = (self.running.astype(F32) + got).astype(LOW)
        self.span = 2 * span

    def end(self, other, after=None):
        while self.span < self.sizes["z"]:
            self.round(after)
        total = jnp.asarray(self.total + jnp.zeros(self.running.shape, F32)).astype(LOW)
        return total, send(total, self.sizes, "c", 1), other


def dot(a, b):
    return jnp.dot(a, b, preferred_element_type=F32)


def dot_nt(a, b):
    return lax.dot_general(a, b, (((1,), (1,)), ((), ())), preferred_element_type=F32)


def dot_tn(a, b):
    return lax.dot_general(a, b, (((0,), (0,)), ((), ())), preferred_element_type=F32)


def normed(values):
    centred = values - jnp.mean(values, axis=-1, keepdims=True)
    spread = jnp.mean(centred * centred, axis=-1, keepdims=True)
    scale = lax.rsqrt(spread + 1e-05)
    return centred * scale, scale


def norm_back(grad, gain, unit, scale):
    eg = grad * gain
    inner = eg - jnp.mean(eg, axis=-1, keepdims=True)
    return scale * (inner - unit * jnp.mean(eg * unit, axis=-1, keepdims=True))


def lanes(shape=(PAIR, PAIR)):
    return lax.broadcasted_iota(jnp.int32, shape, 1)


def subs(shape=(PAIR, PAIR)):
    return lax.broadcasted_iota(jnp.int32, shape, 0)


def head_lanes(first_only):
    lane, row = lanes((ZROWS, PAIR)), subs((ZROWS, PAIR))
    head = (lane % HD) // 2 * 2 + jnp.where(lane < HD, 1, 0)
    hit = head == row
    if first_only:
        hit = jnp.logical_and(hit, lane % 2 == 0)
    return jnp.where(hit, 1.0, 0.0).astype(LOW)


def edge_lanes(p, which):
    return lanes() // 2 == (p if which else HD // 2 + p)


def soft_pair(logits):
    high = jnp.max(logits, axis=0, keepdims=True)
    small = jnp.min(logits, axis=0, keepdims=True)
    e1 = jnp.exp(logits - high)
    e2 = jnp.exp(small - logits)
    p1 = e1 * (1.0 / jnp.sum(e1, axis=0, keepdims=True))
    p2 = e2 * (1.0 / jnp.sum(e2, axis=0, keepdims=True))
    return jnp.concatenate([p1, p2], axis=0)


def soft_back(phi, grad):
    prod = phi * grad
    s1 = jnp.sum(prod[:HD], axis=0, keepdims=True)
    s2 = jnp.sum(prod[HD:], axis=0, keepdims=True)
    return (prod[:HD] - phi[:HD] * s1) - (prod[HD:] - phi[HD:] * s2)


def prepare_kernel(core_ref, mine_ref, theirs_ref, w_ref, maps_ref, vec_ref):
    cut = w_ref.shape[-1] - 2 * PAIR

    def write(even_ref, odd_ref):
        w_ref[:, 0] = even_ref[...]
        w_ref[:, 1] = odd_ref[...]
        even = even_ref[:, :, cut:].astype(F32)[:, None]
        odd = odd_ref[:, :, cut:].astype(F32)[:, None]
        tail = jnp.concatenate([even, odd], axis=1)
        split_tail(tail.reshape(-1, 2 * PAIR), maps_ref, vec_ref)

    @pl.when(core_ref[0] == 0)
    def _():
        write(mine_ref, theirs_ref)

    @pl.when(core_ref[0] != 0)
    def _():
        write(theirs_ref, mine_ref)


def tail_kernel(tail_ref, maps_ref, vec_ref):
    split_tail(tail_ref[...].astype(F32), maps_ref, vec_ref)


def split_tail(tail, maps_ref, vec_ref):
    low = lanes((HD, PAIR)) < HD
    for p in range(maps_ref.shape[1]):
        at = slice(p * PAIR, (p + 1) * PAIR)
        both = tail[at, :PAIR].T
        for which in range(2):
            one = both[which * HD : (which + 1) * HD]
            block = [jnp.where(low, one, 0.0), jnp.where(low, 0.0, one)]
            maps_ref[which, p] = jnp.concatenate(block, axis=0).astype(LOW)
        vec_ref[:, at] = tail[at, PAIR:].T[:ZROWS]


def enter_kernel(x_ref, w_ref, maps_ref, vec_ref, *rest):
    hid_ref, qkv_ref, pq_ref, pk_ref, st_ref, hid_s, qkv_s = rest[-7:]
    width = x_ref.shape[1]
    pairs = pq_ref.shape[1] // 2
    step = pl.program_id(0)

    @pl.when(step == 0)
    def _():
        unit, _ = normed(x_ref[...].astype(F32))
        hid_s[...] = (unit * vec_ref[0:1, :] + vec_ref[2:3, :]).astype(LOW)
        for part in range(3):
            span = slice(part * width, (part + 1) * width)
            value = dot(hid_s[...], w_ref[:, span]) + vec_ref[3 + part : 4 + part, :]
            qkv_s[:, span] = value.astype(LOW)

    rows = pl.ds(pl.multiple_of(step * PAIR, PAIR), PAIR)
    hid_ref[...] = hid_s[rows, :]
    qkv_ref[...] = qkv_s[rows, :]
    low = lanes() < HD
    ones = jnp.ones((PAIR, PAIR), LOW)
    for which, ref in ((1, pk_ref), (0, pq_ref)):
        for p in range(pairs):
            at = slice(which * width + p * PAIR, which * width + (p + 1) * PAIR)
            logits = dot_nt(maps_ref[which, p], qkv_s[rows, at])
            ref[0, 2 * p] = soft_pair(logits[:HD]).astype(LOW)
            ref[0, 2 * p + 1] = soft_pair(logits[HD:]).astype(LOW)
    cols = jnp.zeros((PAIR, PAIR), F32)
    for p in range(pairs):
        at = slice(p * PAIR, (p + 1) * PAIR)
        value = qkv_s[rows, 2 * width + p * PAIR : 2 * width + (p + 1) * PAIR]
        own = []
        for which in range(2):
            both = dot(pk_ref[0, 2 * p + which], jnp.concatenate([value, ones], axis=1))
            own.append(both[:, :PAIR])
            cols = jnp.where(edge_lanes(p, which), both[:, PAIR:], cols)
        st_ref[0, at, :] = jnp.where(low, own[0], own[1]).astype(LOW)
    st_ref[0, width : width + ZROWS, :] = dot_nt(head_lanes(True), cols.astype(LOW)).astype(LOW)


def compose(s, core_ref, refs, out_ref, reverse):
    mine_ref, theirs_ref, other_ref = refs
    half = mine_ref.shape[0]
    at = lax.rem(s, half)
    core = core_ref[0]

    @pl.when(s // half == core)
    def _():
        out_ref[...] = mine_ref[at]

    @pl.when(s // half != core)
    def _():
        out_ref[...] = theirs_ref[at]

    @pl.when(core == (0 if reverse else 1))
    def _():
        own = other_ref[0 if other_ref.shape[0] == 1 else s]
        out_ref[...] = (out_ref[...].astype(F32) + own.astype(F32)).astype(LOW)


def middle_kernel(
    place, core_ref, x_hbm, dy_hbm, v_ref, pq_hbm, pk_hbm, pa_ref, pb_ref, po_ref, w_hbm, vec_ref, *rest
):
    (out_hbm, a_hbm, h2_hbm, g_hbm, du_hbm, dmid_hbm, dmb_hbm, dn_hbm, ds_ref, sum_ref,
     x_ref, dy_ref, pq_ref, pk_ref, w_ref, out_ref, a_ref, h2_ref, g_ref, du_ref, dmid_ref, dmb_ref, dn_ref,
     ctx_s, inv_s, swap_s, unit_s, acc_s, back_s, pri_s, left_s, seq_sem, in_sem, out_sem) = rest[-34:]
    rows_all, width = x_ref.shape
    seqs, heads = pq_ref.shape[0], pq_ref.shape[1]
    pairs = heads // 2
    hidden = g_ref.shape[1]
    blocks = hidden // width
    mine = pl.ds(place * rows_all, rows_all)
    lane, sub = lanes(), subs()
    low = lane < HD

    def features(s):
        return [
            pltpu.make_async_copy(pq_hbm.at[s], pq_ref.at[s], seq_sem.at[0, s]),
            pltpu.make_async_copy(pk_hbm.at[s], pk_ref.at[s], seq_sem.at[1, s]),
        ]

    def dn_out(s):
        rows = pl.ds(pl.multiple_of(s * PAIR, PAIR), PAIR)
        return pltpu.make_async_copy(dn_ref.at[rows, :], dn_hbm.at[rows, :], seq_sem.at[2, s])

    for s in range(seqs):
        for copy in features(s):
            copy.start()
    tail = pl.ds(2 * hidden, width)
    loads = [
        pltpu.make_async_copy(w_hbm.at[:, tail], w_ref.at[:, tail], in_sem.at[0]),
        pltpu.make_async_copy(x_hbm.at[mine, :], x_ref, in_sem.at[1]),
        pltpu.make_async_copy(dy_hbm.at[mine, :], dy_ref, in_sem.at[2]),
        pltpu.make_async_copy(
            w_hbm.at[:, pl.ds(0, 2 * hidden)], w_ref.at[:, pl.ds(0, 2 * hidden)], in_sem.at[3]
        ),
    ]
    for copy in loads:
        copy.start()
    stores = []

    def store(have, there):
        copy = pltpu.make_async_copy(have, there, out_sem.at[len(stores)])
        copy.start()
        stores.append(copy)

    sum_ref[...] = jnp.zeros_like(sum_ref)

    def attend(s, carry):
        for copy in features(s):
            copy.wait()
        compose(s, core_ref, (pa_ref, pb_ref, po_ref), pri_s, False)
        rows = pl.ds(pl.multiple_of(s * PAIR, PAIR), PAIR)
        zsum = pri_s[width : width + ZROWS, :].astype(F32)
        invs = []
        for h in range(heads):
            phi = pq_ref[s, h].T
            score = jnp.where(sub >= lane, dot(phi, pk_ref[s, h]), 0.0).astype(LOW)
            left_s[h, :, :PAIR] = score
            left_s[h, :, PAIR:] = phi
            each = score.astype(F32) + phi.astype(F32) * zsum[h : h + 1, :]
            invs.append(1.0 / jnp.sum(each, axis=1, keepdims=True))
        for p in range(pairs):
            at = slice(p * PAIR, (p + 1) * PAIR)
            inv = jnp.where(low, invs[2 * p], invs[2 * p + 1])
            inv_s[rows, at] = inv
            swap_s[rows, at] = jnp.where(low, invs[2 * p + 1], invs[2 * p])
            right = jnp.concatenate([v_ref[rows, at], pri_s[at, :]], axis=0)
            left = jnp.concatenate([left_s[2 * p], left_s[2 * p + 1]], axis=0)
            both = dot(left, right)
            ctx = jnp.where(low, both[:PAIR], both[PAIR:]) * inv
            ctx_s[rows, at] = ctx
            a_ref[rows, at] = ctx.astype(LOW)
        return carry

    lax.fori_loop(0, seqs, attend, 0)
    store(a_ref, a_hbm.at[mine, :])
    w_out = w_ref.at[:, tail]
    loads[0].wait()
    loads[1].wait()
    mid = x_ref[...].astype(F32) + dot(a_ref[...], w_out[...]) + vec_ref[6:7, :]
    acc_s[...] = mid + vec_ref[12:13, :]
    unit, scale = normed(mid)
    unit_s[...] = unit
    h2_ref[...] = (unit * vec_ref[1:2, :] + vec_ref[7:8, :]).astype(LOW)
    store(h2_ref, h2_hbm.at[mine, :])
    back_s[...] = jnp.zeros_like(back_s)
    c0 = 0.7978845608028654
    c1 = 0.044715
    loads[2].wait()
    loads[3].wait()

    def block_out(j):
        at = pl.ds(pl.multiple_of(j * width, width), width)
        return [
            pltpu.make_async_copy(g_ref.at[:, at], g_hbm.at[mine, at], out_sem.at[5 + 2 * j]),
            pltpu.make_async_copy(du_ref.at[:, at], du_hbm.at[mine, at], out_sem.at[6 + 2 * j]),
        ]

    def mlp(j, carry):
        at = pl.ds(pl.multiple_of(j * width, width), width)
        at2 = pl.ds(pl.multiple_of(hidden + j * width, width), width)
        u = dot(h2_ref[...], w_ref[:, at]) + vec_ref[pl.ds(8 + j, 1), :]
        dg = dot_nt(dy_ref[...], w_ref[:, at2])
        sq = u * u
        th = jnp.tanh(c0 * (u + c1 * (u * sq)))
        half = 0.5 + 0.5 * th
        g = (u * half).astype(LOW)
        slope = half + (0.5 * u) * ((1.0 - th * th) * (c0 + (3.0 * c0 * c1) * sq))
        du = (slope * dg).astype(LOW)
        g_ref[:, at] = g
        du_ref[:, at] = du
        for copy in block_out(j):
            copy.start()
        sum_ref[pl.ds(8 + j, 1), :] = jnp.sum(du.astype(F32), axis=0, keepdims=True)
        acc_s[...] += dot(g, w_ref[:, at2])
        back_s[...] += dot_nt(du, w_ref[:, at])
        return carry

    lax.fori_loop(0, blocks, mlp, 0)
    out_ref[...] = acc_s[...].astype(LOW)
    store(out_ref, out_hbm.at[mine, :])
    dy = dy_ref[...].astype(F32)
    e = back_s[...]
    unit = unit_s[...]
    sum_ref[12:13, :] = jnp.sum(dy, axis=0, keepdims=True)
    sum_ref[1:2, :] = jnp.sum(e * unit, axis=0, keepdims=True)
    sum_ref[7:8, :] = jnp.sum(e, axis=0, keepdims=True)
    dmid = dy + norm_back(e, vec_ref[1:2, :], unit, scale)
    dmid_ref[...] = dmid
    store(dmid_ref, dmid_hbm.at[mine, :])
    dmb = dmid.astype(LOW)
    dmb_ref[...] = dmb
    store(dmb_ref, dmb_hbm.at[mine, :])
    sum_ref[6:7, :] = jnp.sum(dmb.astype(F32), axis=0, keepdims=True)
    back_s[...] = dot_nt(dmb, w_out[...])

    def back(s, carry):
        rows = pl.ds(pl.multiple_of(s * PAIR, PAIR), PAIR)
        odd = lane % 2 == 1
        across = jnp.where((sub < HD) != low, 1.0, 0.0).astype(LOW)
        across = jnp.concatenate([across, across], axis=0)
        for p in range(pairs):
            at = slice(p * PAIR, (p + 1) * PAIR)
            dctx = back_s[rows, at]
            dn = dctx * inv_s[rows, at]
            prod = dctx * ctx_s[rows, at]
            high = prod.astype(LOW)
            rest_prod = (prod - high.astype(F32)).astype(LOW)
            dd = -dot(jnp.concatenate([high, rest_prod], axis=1), across) * swap_s[rows, at]
            extra = jnp.where(odd, dd - dd.astype(LOW).astype(F32), dd)
            for which, own in ((0, low), (1, jnp.logical_not(low))):
                h = 2 * p + which
                aug = jnp.where(own, dn, jnp.where(edge_lanes(p, which), extra, 0.0))
                dn_ref[rows, h * PAIR : (h + 1) * PAIR] = aug.astype(LOW)
        dn_out(s).start()
        cols = jnp.zeros((PAIR, PAIR), F32)
        for p in range(pairs):
            got = []
            for which in range(2):
                h = 2 * p + which
                got.append(dot(pq_ref[s, h], dn_ref[rows, h * PAIR : (h + 1) * PAIR]))
                cols = jnp.where(edge_lanes(p, which), got[-1], cols)
            ds_ref[s, p * PAIR : (p + 1) * PAIR, :] = jnp.where(low, got[0], got[1]).astype(LOW)
        ds_ref[s, width : width + ZROWS, :] = dot_nt(head_lanes(False), cols.astype(LOW)).astype(LOW)
        return carry

    lax.fori_loop(0, seqs, back, 0)
    for copy in stores:
        copy.wait()
    for j in range(blocks):
        for copy in block_out(j):
            copy.wait()
    for s in range(seqs):
        dn_out(s).wait()


def leave_kernel(
    core_ref, qkv_ref, pq_ref, pk_ref, pa_ref, pb_ref, po_ref, la_ref, lb_ref, lo_ref, dn_ref, maps_ref, *rest
):
    dqkv_ref, gmap_ref, pri_s, dl_s, da_s, df_s, left_s, back_s = rest[-8:]
    width = qkv_ref.shape[1] // 3
    heads = pq_ref.shape[1]
    pairs = heads // 2
    step = pl.program_id(0)

    @pl.when(step == 0)
    def _():
        gmap_ref[...] = jnp.zeros_like(gmap_ref)

    compose(step, core_ref, (pa_ref, pb_ref, po_ref), pri_s, False)
    compose(step, core_ref, (la_ref, lb_ref, lo_ref), dl_s, True)
    lane, sub = lanes(), subs()
    low = lane < HD
    masks = [jnp.where(low, 1.0, 0.0).astype(LOW), jnp.where(low, 0.0, 1.0).astype(LOW)]
    zcol = dot_tn(pri_s[width : width + ZROWS, :], head_lanes(False)).astype(LOW)
    dzcol = dot_tn(dl_s[width : width + ZROWS, :], head_lanes(True)).astype(LOW)
    every = [(p, which, 2 * p + which) for p in range(pairs) for which in range(2)]
    column = lambda part, p: slice(part * width + p * PAIR, part * width + (p + 1) * PAIR)
    edge = lambda p, which: jnp.where(edge_lanes(p, which), 1.0, 0.0).astype(LOW)
    dn_of = lambda h: dn_ref[:, h * PAIR : (h + 1) * PAIR]
    for p, which, h in every:
        dn = dn_of(h)
        vaug = qkv_ref[:, column(2, p)] * masks[which] + edge(p, which)
        da_s[h, :, :PAIR] = jnp.where(sub >= lane, dot_nt(dn, vaug), 0.0).astype(LOW)
        da_s[h, :, PAIR:] = dn
        back_s[h, :, :PAIR] = jnp.where(sub <= lane, dot_nt(vaug, dn), 0.0).astype(LOW)
        back_s[h, :, PAIR:] = vaug
        keys = pk_ref[0, h].T
        left_s[h, :, :PAIR] = jnp.where(sub <= lane, dot(keys, pq_ref[0, h]), 0.0).astype(LOW)
        left_s[h, :, PAIR:] = keys
    for p, which, h in every:
        half = slice(which * HD, (which + 1) * HD)
        saug = pri_s[column(0, p), :] * masks[which] + zcol * edge(p, which)
        dpq = dot_nt(jnp.concatenate([pk_ref[0, h], saug], axis=1), da_s[h])
        df_s[0, p, half, :] = soft_back(pq_ref[0, h].astype(F32), dpq).astype(LOW)
    for p, which, h in every:
        half = slice(which * HD, (which + 1) * HD)
        laug = dl_s[column(0, p), :] * masks[which] + dzcol * edge(p, which)
        dpk = dot_nt(jnp.concatenate([pq_ref[0, h], laug], axis=1), back_s[h])
        df_s[1, p, half, :] = soft_back(pk_ref[0, h].astype(F32), dpk).astype(LOW)
    for p in range(pairs):
        dn = dn_of(2 * p) * masks[0] + dn_of(2 * p + 1) * masks[1]
        right = jnp.concatenate([dn, dl_s[column(0, p), :]], axis=0)
        left = jnp.concatenate([left_s[2 * p], left_s[2 * p + 1]], axis=0)
        both = dot(left, right)
        dqkv_ref[:, column(2, p)] = jnp.where(low, both[:PAIR], both[PAIR:]).astype(LOW)
    for part in range(2):
        for p in range(pairs):
            df = df_s[part, p]
            gmap_ref[part, p] += dot(df, qkv_ref[:, column(part, p)])
            dqkv_ref[:, column(part, p)] = dot(df.T, maps_ref[part, p]).astype(LOW)


def norm_kernel(x_ref, d_ref, w_ref, dmid_ref, vec_ref, dx_ref):
    e = dot_nt(d_ref[...], w_ref[...])
    unit, scale = normed(x_ref[...].astype(F32))
    dx_ref[...] = dmid_ref[...] + norm_back(e, vec_ref[0:1, :], unit, scale)


def put(value, core_ref, keep_ref, give_ref):
    count, rows, _ = keep_ref.shape
    value = value.reshape(count, 2, rows, value.shape[-1])
    even, odd = value[:, 0], value[:, 1]
    low = core_ref[0] == 0
    keep_ref[...] = jnp.where(low, even, odd).astype(LOW)
    give_ref[...] = jnp.where(low, odd, even).astype(LOW)


def weight_kernel(core_ref, h2_ref, du_ref, g_ref, dy_ref, a_ref, dmb_ref, *outs):
    step = pl.program_id(0)
    blocks = (pl.num_programs(0) - 1) // 2

    def write(value):
        if len(outs) == 1:
            outs[0][...] = value.astype(LOW)
        else:
            put(value, core_ref, *outs)

    @pl.when(step < blocks)
    def _():
        write(dot_tn(h2_ref[...], du_ref[...]))

    @pl.when(jnp.logical_and(step >= blocks, step < 2 * blocks))
    def _():
        write(dot_tn(g_ref[...], dy_ref[...]))

    @pl.when(step == 2 * blocks)
    def _():
        write(dot_tn(a_ref[...], dmb_ref[...]))


def first_kernel(core_ref, h_ref, d_ref, w_ref, g0_ref, g1_ref, row_ref, *rest):
    outs, (rows_s, gain_s, shift_s) = rest[:-3], rest[-3:]
    step = pl.program_id(0)
    last = pl.num_programs(0) - 1
    width = h_ref.shape[1]

    def write(value, start):
        at = pl.ds(start, value.shape[1])
        if len(outs) == 1:
            outs[0][:, at] = value.astype(LOW)
        else:
            put(value, core_ref, *(out.at[:, :, at] for out in outs))

    @pl.when(step == 0)
    def _():
        rows_s[...] = row_ref[...]
        gain_s[...] = jnp.zeros_like(gain_s)
        shift_s[...] = jnp.zeros_like(shift_s)

    at = pl.ds(pl.multiple_of(step * width, width), width)
    value = dot_tn(h_ref[...], d_ref[...])
    write(value, pl.multiple_of(step * width, width))
    w = w_ref[:, at].astype(F32)
    sums = jnp.sum(d_ref[...].astype(F32), axis=0, keepdims=True)
    rows_s[pl.ds(3 + step, 1), :] = sums
    gain_s[...] += jnp.sum(w * value, axis=1, keepdims=True)
    shift_s[...] += jnp.sum(w * sums, axis=1, keepdims=True)

    @pl.when(step == last)
    def _():
        lane, sub = lanes(), subs()
        fill = jnp.zeros((PAIR - ZROWS, PAIR), F32)
        blocks = []
        for p in range(g0_ref.shape[1]):
            at = slice(p * PAIR, (p + 1) * PAIR)
            q = (g0_ref[0, p] + g1_ref[0, p]).T
            k = (g0_ref[1, p] + g1_ref[1, p]).T
            upper = sub < HD
            q = jnp.where(upper, q, pltpu.roll(q, HD, 1))
            k = jnp.where(upper, pltpu.roll(k, HD, 1), k)
            cols = jnp.concatenate([rows_s[:, at], fill], axis=0).T
            own = w_ref[at, 3 * width + PAIR :].astype(F32)
            shift = shift_s[at]
            gain = (gain_s[at] - own[:, 2:3] * shift) / own[:, 0:1]
            cols = jnp.where(lane == 0, gain, jnp.where(lane == 2, shift, cols))
            blocks.append(jnp.concatenate([jnp.where(lane < HD, q, k), cols], axis=1))
        write(jnp.concatenate(blocks, axis=0), 3 * width)


def whole(shape):
    return pl.BlockSpec(shape, lambda i: (0,) * len(shape), pipeline_mode=pl.Buffered(1))


def part(shape, *at):
    return pl.BlockSpec(shape, lambda i: at, pipeline_mode=pl.Buffered(1))


PLAIN = pltpu.CompilerParams(vmem_limit_bytes=VMEM_BYTES)
PARAMS = dict(
    compiler_params=pltpu.CompilerParams(
        dimension_semantics=("arbitrary",), vmem_limit_bytes=VMEM_BYTES
    )
)


def cost(flops, size):
    return pl.CostEstimate(flops=20 * int(flops), bytes_accessed=20 * int(size), transcendentals=0)


def enter(m, held, x, w, maps, vec, heads):
    total, width = x.shape
    rows = total // 2
    seqs = rows // PAIR
    pack = width + ZROWS
    extra = [] if held is None else [held]
    return pl.pallas_call(
        enter_kernel,
        grid=(seqs,),
        in_specs=[
            part((rows, width), m, 0),
            part((width, 3 * width), 0, 0),
            whole(maps.shape),
            whole(vec.shape),
        ]
        + [pl.BlockSpec(memory_space=pl.ANY)] * len(extra),
        out_specs=[
            pl.BlockSpec((PAIR, width), lambda i: (m * seqs + i, 0)),
            pl.BlockSpec((PAIR, 3 * width), lambda i: (i, 0)),
            pl.BlockSpec((1, heads, PAIR, PAIR), lambda i: (i, 0, 0, 0)),
            pl.BlockSpec((1, heads, PAIR, PAIR), lambda i: (i, 0, 0, 0)),
            pl.BlockSpec((1, pack, PAIR), lambda i: (i, 0, 0)),
        ],
        out_shape=[
            jax.ShapeDtypeStruct((total, width), LOW),
            jax.ShapeDtypeStruct((rows, 3 * width), LOW),
            jax.ShapeDtypeStruct((seqs, heads, PAIR, PAIR), LOW),
            jax.ShapeDtypeStruct((seqs, heads, PAIR, PAIR), LOW),
            jax.ShapeDtypeStruct((seqs, pack, PAIR), LOW),
        ],
        scratch_shapes=[pltpu.VMEM((rows, width), LOW), pltpu.VMEM((rows, 3 * width), LOW)],
        input_output_aliases={4 + k: k for k in range(len(extra))},
        cost_estimate=cost(6 * rows * width * width, 12 * rows * width),
        name="enter",
        **PARAMS,
    )(x, w, maps, vec, *extra)


def middle(m, held, core, x, dy, qkv, pq, pk, pri, w, vec, hidden):
    total, width = x.shape
    rows = total // 2
    seqs, heads = pq.shape[0], pq.shape[1]
    pack = width + ZROWS
    extra = [] if held is None else list(held)
    shared = [(width, LOW)] * 3 + [(hidden, LOW)] * 2 + [(width, F32), (width, LOW)]
    far = pl.BlockSpec(memory_space=pl.ANY)
    dn = jax.ShapeDtypeStruct((rows, heads * PAIR), LOW)
    ends = [
        jax.ShapeDtypeStruct((seqs, pack, PAIR), LOW),
        jax.ShapeDtypeStruct((ZROWS, width), F32),
    ]
    return pl.pallas_call(
        functools.partial(middle_kernel, m),
        grid=(1,),
        in_specs=[pl.BlockSpec(memory_space=pltpu.SMEM), far, far, part((rows, width), 0, 2), far, far]
        + [whole(piece.shape) for piece in pri]
        + [far, whole(vec.shape)]
        + [far] * len(extra),
        out_specs=[far] * (len(shared) + 1) + [whole(end.shape) for end in ends],
        out_shape=[jax.ShapeDtypeStruct((total, n), t) for n, t in shared] + [dn] + ends,
        scratch_shapes=[
            pltpu.VMEM((rows, width), LOW),
            pltpu.VMEM((rows, width), LOW),
            pltpu.VMEM(pq.shape, LOW),
            pltpu.VMEM(pk.shape, LOW),
            pltpu.VMEM(w.shape, LOW),
        ]
        + [pltpu.VMEM((rows, n), t) for n, t in shared]
        + [pltpu.VMEM(dn.shape, LOW)]
        + [pltpu.VMEM((rows, width), F32)] * 6
        + [
            pltpu.VMEM((pack, PAIR), LOW),
            pltpu.VMEM((heads, PAIR, 2 * PAIR), LOW),
            pltpu.SemaphoreType.DMA((3, seqs)),
            pltpu.SemaphoreType.DMA((4,)),
            pltpu.SemaphoreType.DMA((5 + 2 * (hidden // width),)),
        ],
        input_output_aliases={11 + k: k for k in range(len(extra))},
        cost_estimate=cost(8 * rows * width * hidden + 4 * rows * width * width, 30 * rows * width),
        name="middle",
        **PARAMS,
    )(core, x, dy, qkv, pq, pk, *pri, w, vec, *extra)


def leave(m, held, core, qkv, pq, pk, pri, dl, dn, maps):
    rows, wide = qkv.shape
    total = 2 * rows
    seqs, heads = pq.shape[:2]
    pack = pri[2].shape[1]
    each = lambda array: pl.BlockSpec((1,) + array.shape[1:], lambda i: (i,) + (0,) * (array.ndim - 1))
    state = lambda pieces: [whole(pieces[0].shape), whole(pieces[1].shape), each(pieces[2])]
    extra = [] if held is None else [held]
    return pl.pallas_call(
        leave_kernel,
        grid=(seqs,),
        in_specs=[
            pl.BlockSpec(memory_space=pltpu.SMEM),
            pl.BlockSpec((PAIR, wide), lambda i: (i, 0)),
            each(pq),
            each(pk),
        ]
        + state(pri)
        + state(dl)
        + [pl.BlockSpec((PAIR, dn.shape[1]), lambda i: (i, 0)), whole(maps.shape)]
        + [pl.BlockSpec(memory_space=pl.ANY)] * len(extra),
        out_specs=[pl.BlockSpec((PAIR, wide), lambda i: (m * seqs + i, 0)), whole(maps.shape)],
        out_shape=[
            jax.ShapeDtypeStruct((total, wide), LOW),
            jax.ShapeDtypeStruct(maps.shape, F32),
        ],
        scratch_shapes=[
            pltpu.VMEM((pack, PAIR), LOW),
            pltpu.VMEM((pack, PAIR), LOW),
            pltpu.VMEM((heads, PAIR, 2 * PAIR), LOW),
            pltpu.VMEM((2, heads // 2, PAIR, PAIR), LOW),
            pltpu.VMEM((heads, PAIR, 2 * PAIR), LOW),
            pltpu.VMEM((heads, PAIR, 2 * PAIR), LOW),
        ],
        input_output_aliases={12 + k: k for k in range(len(extra))},
        cost_estimate=cost(8 * rows * wide * PAIR, 8 * rows * wide),
        name="leave",
        **PARAMS,
    )(core, qkv, pq, pk, *pri, *dl, dn, maps, *extra)


def norm_grads(x, dqkv, w, dmid, vec):
    total, width = x.shape
    rows = min(total, 256)
    return pl.pallas_call(
        norm_kernel,
        grid=(total // rows,),
        in_specs=[
            pl.BlockSpec((rows, width), lambda i: (i, 0)),
            pl.BlockSpec((rows, 3 * width), lambda i: (i, 0)),
            part((width, 3 * width), 0, 0),
            pl.BlockSpec((rows, width), lambda i: (i, 0)),
            whole(vec.shape),
        ],
        out_specs=pl.BlockSpec((rows, width), lambda i: (i, 0)),
        out_shape=jax.ShapeDtypeStruct((total, width), F32),
        cost_estimate=cost(6 * total * width * width, 12 * total * width),
        name="norm",
        **PARAMS,
    )(x, dqkv, w, dmid, vec)


def prepare(core, mine, theirs, heads):
    count, rows, columns = mine.shape
    width = 2 * count * rows
    outs = [
        jax.ShapeDtypeStruct((2, heads // 2, PAIR, PAIR), LOW),
        jax.ShapeDtypeStruct((ZROWS, width), F32),
    ]
    if rows % 8 != 0:
        low = core[0] == 0
        both = [jnp.where(low, mine, theirs), jnp.where(low, theirs, mine)]
        w = jnp.stack(both, axis=1).reshape(width, columns)
        maps, vec = pl.pallas_call(
            tail_kernel, out_shape=outs, name="tail", compiler_params=PLAIN
        )(w[:, columns - 2 * PAIR :])
        return w, maps, vec
    w, maps, vec = pl.pallas_call(
        prepare_kernel,
        grid=(1,),
        in_specs=[
            pl.BlockSpec(memory_space=pltpu.SMEM),
            whole(mine.shape),
            whole(theirs.shape),
        ],
        out_specs=[
            whole((count, 2, rows, columns)),
            whole(outs[0].shape),
            whole(outs[1].shape),
        ],
        out_shape=[jax.ShapeDtypeStruct((count, 2, rows, columns), LOW)] + outs,
        name="prepare",
        **PARAMS,
    )(core, mine, theirs)
    return w.reshape(width, columns), maps, vec


def out_halves(width, rows, columns, size):
    if rows % 8 != 0:
        return (
            [pl.BlockSpec((width, size), lambda i: (0, i))],
            [jax.ShapeDtypeStruct((width, columns), LOW)],
        )
    count = width // rows // 2
    return (
        [pl.BlockSpec((count, rows, size), lambda i: (0, 0, i))] * 2,
        [jax.ShapeDtypeStruct((count, rows, columns), LOW)] * 2,
    )


def weight_grads(core, rows, h2, du, g, dy, a, dmb):
    total, width = h2.shape
    blocks = du.shape[1] // width
    last = 2 * blocks
    block = (total, width)
    specs, shapes = out_halves(width, rows, (last + 1) * width, width)
    return pl.pallas_call(
        weight_kernel,
        grid=(last + 1,),
        in_specs=[
            pl.BlockSpec(memory_space=pltpu.SMEM),
            pl.BlockSpec(block, lambda i: (0, 0)),
            pl.BlockSpec(block, lambda i: (0, jnp.minimum(i, blocks - 1))),
            pl.BlockSpec(block, lambda i: (0, jnp.clip(i - blocks, 0, blocks - 1))),
            pl.BlockSpec(block, lambda i: (0, 0)),
            pl.BlockSpec(block, lambda i: (0, 0)),
            pl.BlockSpec(block, lambda i: (0, 0)),
        ],
        out_specs=specs,
        out_shape=shapes,
        cost_estimate=cost(2 * total * width * width * (last + 1), 20 * total * width),
        name="weights",
        **PARAMS,
    )(core, h2, du, g, dy, a, dmb)


def first_grads(core, rows, hid, dqkv, w, gmaps, sums):
    total, width = hid.shape
    specs, shapes = out_halves(width, rows, w.shape[1], w.shape[1])
    specs = [whole(shape.shape) for shape in shapes]
    return pl.pallas_call(
        first_kernel,
        grid=(3,),
        in_specs=[
            pl.BlockSpec(memory_space=pltpu.SMEM),
            whole(hid.shape),
            pl.BlockSpec((total, width), lambda i: (0, i)),
            whole(w.shape),
            whole(gmaps[0].shape),
            whole(gmaps[1].shape),
            whole(sums.shape),
        ],
        out_specs=specs,
        out_shape=shapes,
        scratch_shapes=[
            pltpu.VMEM((ZROWS, width), F32),
            pltpu.VMEM((width, 1), F32),
            pltpu.VMEM((width, 1), F32),
        ],
        cost_estimate=cost(6 * total * width * width, 12 * total * width),
        name="first",
        **PARAMS,
    )(core, hid, dqkv, w, *gmaps, sums)


def shards(tokens, w_qkv, w_feat, w_out, w_fc, w_proj, gains, biases, cotangent):
    micro_count, seq_count, seg_len, width = tokens.shape
    grid = grid_dims()
    rows = w_qkv.shape[0]
    hidden = w_fc.shape[1]
    ratio = hidden // width
    heads = width // HD
    pairs = heads // 2
    wide = 3 * width
    total = micro_count * seq_count * seg_len

    first = jnp.concatenate(
        [
            w_qkv.astype(LOW),
            jnp.transpose(w_feat, (1, 0, 2)).reshape(rows, PAIR).astype(LOW),
            jnp.pad(jnp.concatenate([gains, biases]).T.astype(LOW), ((0, 0), (0, PAIR - 13))),
        ],
        axis=1,
    )
    core = jnp.reshape(grid[1]["c"], (1,))
    first, maps, vec = prepare(core, *gather_rows(first, grid), heads)
    later = jnp.concatenate(
        [
            w_fc.astype(LOW).reshape(rows, width, ratio).swapaxes(1, 2).reshape(rows, hidden),
            w_proj.astype(LOW).reshape(rows, hidden),
            w_out.astype(LOW),
        ],
        axis=1,
    )
    later = lax.all_gather(later, AXES, axis=0, tiled=True)
    fc_bias = vec[8 : 8 + ratio].reshape(width, ratio).T
    mid_vec = jnp.concatenate([vec[:8], fc_bias, vec[8 + ratio :]])
    x = tokens.reshape(total, width)
    dy = cotangent.reshape(total, width)

    entered, swaps, steps = [], [], []
    for m in range(2):
        held = entered[0][0] if m else None
        held_vec = tie(vec, swaps[0][0]) if m else vec
        entered.append(enter(m, held, x, first, maps, held_vec, heads))
        own = entered[m][4]
        if m:
            steps[0].round(entered[1][1])
            own = tie(own, steps[0].running)
        swaps.append(swap(own, grid))
        steps.append(Steps(swaps[m][0], grid, False))
    hid = entered[1][0]
    steps[1].round()
    ready = steps[1].running
    priors = [steps[m].end(swaps[m][1]) for m in range(2)]
    held, mids, swaps, steps = None, [], [], []
    for m in range(2):
        _, qkv, pq, pk, _ = entered[m]
        held_vec = tie(mid_vec, swaps[0][0] if m else ready)
        got = middle(m, held, core, x, dy, qkv, pq, pk, priors[m], later, held_vec, hidden)
        held, rest = got[:7], got[7:]
        mids.append(rest)
        own = rest[1]
        if m:
            steps[0].round(rest[2])
            own = tie(own, steps[0].running)
        swaps.append(swap(own, grid))
        steps.append(Steps(swaps[m][0], grid, True))
    out, a, h2, g, du, dmid, dmb = held
    g_later = weight_grads(tie(core, swaps[1][0]), rows, h2, du, g, dy, a, dmb)
    if len(g_later) == 1:
        g_later = halves(g_later[0], grid, rows)
    inner = mids[0][2] + mids[1][2]
    g_fc_bias = inner[8 : 8 + ratio].T.reshape(ratio, width)
    sums = jnp.concatenate([inner[:8], g_fc_bias, inner[8 + ratio :]])
    keep, give = g_later
    laters = [steps[0].end(swaps[0][1], give)]
    steps[1].round(give)
    _, qkv, pq, pk, _ = entered[0]
    kept, gmap = leave(0, None, core, qkv, pq, pk, priors[0], laters[0], mids[0][0], maps)
    gmaps = [gmap]
    scatter = Scatter(keep, tie(give, laters[0][0], steps[1].running), grid, gmap)
    laters.append(steps[1].end(swaps[1][1], gmap))
    _, qkv, pq, pk, _ = entered[1]
    held_core = tie(core, scatter.left, scatter.right)
    dqkv, gmap = leave(1, kept, held_core, qkv, pq, pk, priors[1], laters[1], mids[1][0], maps)
    gmaps.append(gmap)
    g_qkv = first_grads(core, rows, hid, dqkv, first, gmaps, sums)
    if len(g_qkv) == 1:
        g_qkv = halves(g_qkv[0], grid, rows)
    scatter.one(g_qkv[0])
    ending = Scatter(*g_qkv, grid, scatter.left)
    held_vec = tie(vec, ending.left, ending.right, scatter.right)
    dx = norm_grads(x, dqkv, first, dmid, held_vec)
    ending.one(dx)
    scatter.two(ending.left)
    scatter.left = tie(scatter.left, ending.left)
    ending.two()
    r_later = scatter.end(ending.left)
    last = ending.end().astype(F32)
    r_fc = r_later[:, :hidden]
    r_proj = r_later[:, hidden : 2 * hidden]
    r_out = r_later[:, 2 * hidden :]
    small = last[:, wide + PAIR :].T
    return (
        out.reshape(tokens.shape),
        dx.reshape(tokens.shape),
        last[:, :wide],
        jnp.transpose(last[:, wide : wide + PAIR].reshape(rows, 2, HD), (1, 0, 2)),
        r_out.astype(F32),
        r_fc.astype(F32).reshape(rows, ratio, width).swapaxes(1, 2).reshape(rows, hidden),
        r_proj.astype(F32).reshape(rows * ratio, width),
        small[:2],
        small[2:13],
    )


def solution(mesh):
    return jax.shard_map(
        shards,
        mesh=mesh,
        in_specs=(
            P(None, "dp", "seq", None),
            P(("dp", "seq"), None),
            P(None, ("dp", "seq"), None),
            P(("dp", "seq"), None),
            P(("dp", "seq"), None),
            P(("dp", "seq"), None),
            P(None, ("dp", "seq")),
            P(None, ("dp", "seq")),
            P(None, "dp", "seq", None),
        ),
        out_specs=(
            P(None, "dp", "seq", None),
            P(None, "dp", "seq", None),
            P(("dp", "seq"), None),
            P(None, ("dp", "seq"), None),
            P(("dp", "seq"), None),
            P(("dp", "seq"), None),
            P(("dp", "seq"), None),
            P(None, ("dp", "seq")),
            P(None, ("dp", "seq")),
        ),
        check_vma=False,
    )
```

```python
import functools

import jax
import jax.numpy as jnp
from jax import lax
from jax.experimental import pallas as pl
from jax.experimental.pallas import tpu as pltpu
from jax.sharding import PartitionSpec as P

HD = 64
PAIR = 2 * HD
AXES = ("dp", "seq")
LOW = jnp.bfloat16
F32 = jnp.float32
VMEM_BYTES = 60 * 1024 * 1024
ZROWS = 16

def grid_dims():
    n_dp, n_seq = lax.axis_size("dp"), lax.axis_size("seq")
    n_x = 1
    while n_x * n_x * 4 <= n_dp:
        n_x *= 2
    sizes = {"y": n_dp // n_x, "x": n_x, "z": n_seq // 2, "c": 2}
    at = lax.axis_index("dp") * n_seq + lax.axis_index("seq")
    place = {}
    for name in ("c", "z", "x", "y"):
        place[name] = lax.rem(at, sizes[name])
        at = at // sizes[name]
    return sizes, place


def turned(sizes, name, step):
    pairs = []
    for y in range(sizes["y"]):
        for x in range(sizes["x"]):
            for z in range(sizes["z"]):
                for c in range(sizes["c"]):
                    to = {"y": y, "x": x, "z": z, "c": c}
                    to[name] = (to[name] + step) % sizes[name]
                    flat = lambda p: ((p[0] * sizes["x"] + p[1]) * sizes["z"] + p[2]) * 2 + p[3]
                    pairs.append((flat((y, x, z, c)), flat((to["y"], to["x"], to["z"], to["c"]))))
    return pairs


def send(value, sizes, name, step):
    return lax.ppermute(value, AXES, turned(sizes, name, step))


def tie(value, *others):
    others = [other for other in others if other is not None]
    return lax.optimization_barrier((value, *others))[0] if others else value


def spread(own, got, place):
    at = lax.broadcasted_iota(jnp.int32, (2,) + (1,) * own.ndim, 0)
    return jnp.where(at == place, own[None], got[None])


def gather_dim(value, grid, name):
    sizes, place = grid
    count = sizes[name]
    if count == 1:
        return value[None]
    got = [value] + [send(value, sizes, name, k) for k in range(1, count)]
    if count == 2:
        return spread(got[0], got[1], place[name])
    order = jnp.stack(got[::-1] + got[::-1][:-1])
    return lax.dynamic_slice_in_dim(order, count - 1 - place[name], count, 0)


def gather_rows(value, grid):
    sizes, _ = grid
    out = gather_dim(value, grid, "z")
    columns = value.shape[1] // 2
    left, right = out[..., :columns], out[..., columns:]
    left, right = gather_dim(left, grid, "x"), gather_dim(right, grid, "y")
    left, right = gather_dim(left, grid, "y"), gather_dim(right, grid, "x")
    out = jnp.concatenate([left, jnp.swapaxes(right, 0, 1)], axis=-1)
    out = out.reshape((-1,) + value.shape)
    return out, send(out, sizes, "c", 1)


def scatter_dim(value, grid, name, axis, after=None):
    sizes, place = grid
    count = sizes[name]
    mine = lax.dynamic_index_in_dim(value, place[name], axis, keepdims=False)
    if count == 1:
        return mine
    total = mine.astype(F32)
    for k in range(1, count):
        to = lax.rem(place[name] + k, count)
        block = lax.dynamic_index_in_dim(value, to, axis, keepdims=False)
        total = total + tie(send(block, sizes, name, k), after).astype(F32)
    return total.astype(LOW)


class Scatter:
    def __init__(self, keep, give, grid, after=None):
        sizes, _ = grid
        self.grid = grid
        got = tie(send(give, sizes, "c", 1), after)
        shape = (sizes["y"], sizes["x"], sizes["z"]) + keep.shape[1:]
        keep, got = keep.reshape(shape), got.reshape(shape)
        cut = keep.shape[-1] // 256 * 128
        add = lambda a, b: (a.astype(F32) + b.astype(F32)).astype(LOW)
        self.left = add(keep[..., :cut], got[..., :cut])
        self.right = add(keep[..., cut:], got[..., cut:])

    def one(self, after=None):
        self.left = scatter_dim(self.left, self.grid, "x", 1, after)
        self.right = scatter_dim(self.right, self.grid, "y", 0, after)

    def two(self, after=None):
        self.left = scatter_dim(self.left, self.grid, "y", 0, after)
        self.right = scatter_dim(self.right, self.grid, "x", 0, after)

    def end(self, after=None):
        both = jnp.concatenate([self.left, self.right], axis=-1)
        return scatter_dim(both, self.grid, "z", 0, after)


def halves(value, grid, rows):
    _, place = grid
    value = value.reshape(-1, 2, rows, value.shape[-1])
    pick = lambda at: lax.dynamic_index_in_dim(value, at, 1, keepdims=False)
    return pick(place["c"]), pick(1 - place["c"])


def some(sizes, step, chosen):
    pairs = []
    for a, b in turned(sizes, "z", step):
        z = (a // 2) % sizes["z"]
        if 0 <= z + step < sizes["z"] and chosen(z):
            pairs.append((a, b))
    return pairs


def swap(own, grid):
    sizes, place = grid
    half = own.shape[0] // 2
    other = send(own, sizes, "c", 1)
    first = place["c"] * half
    mine = lax.dynamic_slice_in_dim(own, first, half, 0).astype(F32)
    mine = (mine + lax.dynamic_slice_in_dim(other, first, half, 0).astype(F32)).astype(LOW)
    return mine, other


class Steps:
    def __init__(self, mine, grid, reverse):
        self.running, self.mine, self.total, self.span = mine, mine, 0.0, 1
        self.sizes, self.reverse = grid[0], reverse

    def round(self, after=None):
        count, span = self.sizes["z"], self.span
        if span >= count:
            return
        back = lambda z: count - 1 - z if self.reverse else z
        four = count == 4 and self.reverse
        if four and span == 1:
            sends = [(1, lambda z: True), (2, lambda z: back(z) == 0)]
        elif four:
            sends = [(1, lambda z: back(z) == 2)]
        else:
            sends = [(d, lambda z: back(z) % (2 * span) == span - 1) for d in range(1, span + 1)]
        got = 0.0
        for d, chosen in sends:
            pairs = some(self.sizes, -d if self.reverse else d, chosen)
            got = got + tie(lax.ppermute(self.running, AXES, pairs), after).astype(F32)
        self.total = self.total + got
        self.running = got.astype(LOW)
        if not four:
            self.running = (self.mine.astype(F32) + self.total).astype(LOW)
        self.span = 2 * span

    def end(self, other, after=None):
        while self.span < self.sizes["z"]:
            self.round(after)
        total = jnp.asarray(self.total + jnp.zeros(self.running.shape, F32)).astype(LOW)
        return total, send(total, self.sizes, "c", 1), other


def dot(a, b):
    return jnp.dot(a, b, preferred_element_type=F32)


def dot_nt(a, b):
    return lax.dot_general(a, b, (((1,), (1,)), ((), ())), preferred_element_type=F32)


def dot_tn(a, b):
    return lax.dot_general(a, b, (((0,), (0,)), ((), ())), preferred_element_type=F32)


def normed(values):
    centred = values - jnp.mean(values, axis=-1, keepdims=True)
    spread = jnp.mean(centred * centred, axis=-1, keepdims=True)
    scale = lax.rsqrt(spread + 1e-05)
    return centred * scale, scale


def norm_back(grad, gain, unit, scale):
    eg = grad * gain
    inner = eg - jnp.mean(eg, axis=-1, keepdims=True)
    return scale * (inner - unit * jnp.mean(eg * unit, axis=-1, keepdims=True))


def lanes(shape=(PAIR, PAIR)):
    return lax.broadcasted_iota(jnp.int32, shape, 1)


def subs(shape=(PAIR, PAIR)):
    return lax.broadcasted_iota(jnp.int32, shape, 0)


def head_lanes(first_only):
    lane, row = lanes((ZROWS, PAIR)), subs((ZROWS, PAIR))
    head = (lane % HD) // 2 * 2 + jnp.where(lane < HD, 1, 0)
    hit = head == row
    if first_only:
        hit = jnp.logical_and(hit, lane % 2 == 0)
    return jnp.where(hit, 1.0, 0.0).astype(LOW)


def edge_lanes(p, which):
    return lanes() // 2 == (p if which else HD // 2 + p)


def soft_pair(logits):
    high = jnp.max(logits, axis=0, keepdims=True)
    small = jnp.min(logits, axis=0, keepdims=True)
    e1 = jnp.exp(logits - high)
    e2 = jnp.exp(small - logits)
    p1 = e1 * (1.0 / jnp.sum(e1, axis=0, keepdims=True))
    p2 = e2 * (1.0 / jnp.sum(e2, axis=0, keepdims=True))
    return jnp.concatenate([p1, p2], axis=0)


def soft_back(phi, grad):
    prod = phi * grad
    s1 = jnp.sum(prod[:HD], axis=0, keepdims=True)
    s2 = jnp.sum(prod[HD:], axis=0, keepdims=True)
    return (prod[:HD] - phi[:HD] * s1) - (prod[HD:] - phi[HD:] * s2)


def prepare_kernel(core_ref, mine_ref, theirs_ref, w_ref, maps_ref, vec_ref):
    cut = w_ref.shape[-1] - 2 * PAIR

    def write(even_ref, odd_ref):
        w_ref[:, 0] = even_ref[...]
        w_ref[:, 1] = odd_ref[...]
        even = even_ref[:, :, cut:].astype(F32)[:, None]
        odd = odd_ref[:, :, cut:].astype(F32)[:, None]
        tail = jnp.concatenate([even, odd], axis=1)
        split_tail(tail.reshape(-1, 2 * PAIR), maps_ref, vec_ref)

    @pl.when(core_ref[0] == 0)
    def _():
        write(mine_ref, theirs_ref)

    @pl.when(core_ref[0] != 0)
    def _():
        write(theirs_ref, mine_ref)


def tail_kernel(tail_ref, maps_ref, vec_ref):
    split_tail(tail_ref[...].astype(F32), maps_ref, vec_ref)


def split_tail(tail, maps_ref, vec_ref):
    low = lanes((HD, PAIR)) < HD
    for p in range(maps_ref.shape[1]):
        at = slice(p * PAIR, (p + 1) * PAIR)
        both = tail[at, :PAIR].T
        for which in range(2):
            one = both[which * HD : (which + 1) * HD]
            block = [jnp.where(low, one, 0.0), jnp.where(low, 0.0, one)]
            maps_ref[which, p] = jnp.concatenate(block, axis=0).astype(LOW)
        vec_ref[:, at] = tail[at, PAIR:].T[:ZROWS]


def enter_kernel(x_ref, w_ref, maps_ref, vec_ref, *rest):
    hid_ref, qkv_ref, pq_ref, pk_ref, st_ref, hid_s, qkv_s = rest[-7:]
    width = x_ref.shape[1]
    pairs = pq_ref.shape[1] // 2
    step = pl.program_id(0)

    @pl.when(step == 0)
    def _():
        unit, _ = normed(x_ref[...].astype(F32))
        hid_s[...] = (unit * vec_ref[0:1, :] + vec_ref[2:3, :]).astype(LOW)
        for part in range(3):
            span = slice(part * width, (part + 1) * width)
            value = dot(hid_s[...], w_ref[:, span]) + vec_ref[3 + part : 4 + part, :]
            qkv_s[:, span] = value.astype(LOW)

    rows = pl.ds(pl.multiple_of(step * PAIR, PAIR), PAIR)
    hid_ref[...] = hid_s[rows, :]
    qkv_ref[...] = qkv_s[rows, :]
    low = lanes() < HD
    ones = jnp.ones((PAIR, PAIR), LOW)
    for which, ref in ((1, pk_ref), (0, pq_ref)):
        for p in range(pairs):
            at = slice(which * width + p * PAIR, which * width + (p + 1) * PAIR)
            logits = dot_nt(maps_ref[which, p], qkv_s[rows, at])
            ref[0, 2 * p] = soft_pair(logits[:HD]).astype(LOW)
            ref[0, 2 * p + 1] = soft_pair(logits[HD:]).astype(LOW)
    cols = jnp.zeros((PAIR, PAIR), F32)
    for p in range(pairs):
        at = slice(p * PAIR, (p + 1) * PAIR)
        value = qkv_s[rows, 2 * width + p * PAIR : 2 * width + (p + 1) * PAIR]
        own = []
        for which in range(2):
            both = dot(pk_ref[0, 2 * p + which], jnp.concatenate([value, ones], axis=1))
            own.append(both[:, :PAIR])
            cols = jnp.where(edge_lanes(p, which), both[:, PAIR:], cols)
        st_ref[0, at, :] = jnp.where(low, own[0], own[1]).astype(LOW)
    st_ref[0, width : width + ZROWS, :] = dot_nt(head_lanes(True), cols.astype(LOW)).astype(LOW)


def compose(s, core_ref, refs, out_ref, reverse):
    mine_ref, theirs_ref, other_ref = refs
    half = mine_ref.shape[0]
    at = lax.rem(s, half)
    core = core_ref[0]

    @pl.when(s // half == core)
    def _():
        out_ref[...] = mine_ref[at]

    @pl.when(s // half != core)
    def _():
        out_ref[...] = theirs_ref[at]

    @pl.when(core == (0 if reverse else 1))
    def _():
        own = other_ref[0 if other_ref.shape[0] == 1 else s]
        out_ref[...] = (out_ref[...].astype(F32) + own.astype(F32)).astype(LOW)


def middle_kernel(
    place, core_ref, x_hbm, dy_hbm, v_ref, pq_hbm, pk_hbm, pa_ref, pb_ref, po_ref, w_hbm, vec_ref, *rest
):
    (out_hbm, a_hbm, h2_hbm, g_hbm, du_hbm, dmid_hbm, dmb_hbm, dn_hbm, ds_ref, sum_ref,
     x_ref, dy_ref, pq_ref, pk_ref, w_ref, out_ref, a_ref, h2_ref, g_ref, du_ref, dmid_ref, dmb_ref, dn_ref,
     ctx_s, inv_s, swap_s, unit_s, acc_s, back_s, pri_s, left_s, seq_sem, in_sem, out_sem) = rest[-34:]
    rows_all, width = x_ref.shape
    seqs, heads = pq_ref.shape[0], pq_ref.shape[1]
    pairs = heads // 2
    hidden = g_ref.shape[1]
    blocks = hidden // width
    mine = pl.ds(place * rows_all, rows_all)
    lane, sub = lanes(), subs()
    low = lane < HD

    def features(s):
        return [
            pltpu.make_async_copy(pq_hbm.at[s], pq_ref.at[s], seq_sem.at[0, s]),
            pltpu.make_async_copy(pk_hbm.at[s], pk_ref.at[s], seq_sem.at[1, s]),
        ]

    def dn_out(s):
        rows = pl.ds(pl.multiple_of(s * PAIR, PAIR), PAIR)
        return pltpu.make_async_copy(dn_ref.at[rows, :], dn_hbm.at[rows, :], seq_sem.at[2, s])

    for s in range(seqs):
        for copy in features(s):
            copy.start()
    tail = pl.ds(2 * hidden, width)
    loads = [
        pltpu.make_async_copy(w_hbm.at[:, tail], w_ref.at[:, tail], in_sem.at[0]),
        pltpu.make_async_copy(x_hbm.at[mine, :], x_ref, in_sem.at[1]),
        pltpu.make_async_copy(dy_hbm.at[mine, :], dy_ref, in_sem.at[2]),
        pltpu.make_async_copy(
            w_hbm.at[:, pl.ds(0, 2 * hidden)], w_ref.at[:, pl.ds(0, 2 * hidden)], in_sem.at[3]
        ),
    ]
    for copy in loads:
        copy.start()
    stores = []

    def store(have, there):
        copy = pltpu.make_async_copy(have, there, out_sem.at[len(stores)])
        copy.start()
        stores.append(copy)

    sum_ref[...] = jnp.zeros_like(sum_ref)

    def attend(s, carry):
        for copy in features(s):
            copy.wait()
        compose(s, core_ref, (pa_ref, pb_ref, po_ref), pri_s, False)
        rows = pl.ds(pl.multiple_of(s * PAIR, PAIR), PAIR)
        zsum = pri_s[width : width + ZROWS, :].astype(F32)
        invs = []
        for h in range(heads):
            phi = pq_ref[s, h].T
            score = jnp.where(sub >= lane, dot(phi, pk_ref[s, h]), 0.0).astype(LOW)
            left_s[h, :, :PAIR] = score
            left_s[h, :, PAIR:] = phi
            each = score.astype(F32) + phi.astype(F32) * zsum[h : h + 1, :]
            invs.append(1.0 / jnp.sum(each, axis=1, keepdims=True))
        for p in range(pairs):
            at = slice(p * PAIR, (p + 1) * PAIR)
            inv = jnp.where(low, invs[2 * p], invs[2 * p + 1])
            inv_s[rows, at] = inv
            swap_s[rows, at] = jnp.where(low, invs[2 * p + 1], invs[2 * p])
            right = jnp.concatenate([v_ref[rows, at], pri_s[at, :]], axis=0)
            left = jnp.concatenate([left_s[2 * p], left_s[2 * p + 1]], axis=0)
            both = dot(left, right)
            ctx = jnp.where(low, both[:PAIR], both[PAIR:]) * inv
            ctx_s[rows, at] = ctx
            a_ref[rows, at] = ctx.astype(LOW)
        return carry

    lax.fori_loop(0, seqs, attend, 0)
    store(a_ref, a_hbm.at[mine, :])
    w_out = w_ref.at[:, tail]
    loads[0].wait()
    loads[1].wait()
    mid = x_ref[...].astype(F32) + dot(a_ref[...], w_out[...]) + vec_ref[6:7, :]
    acc_s[...] = mid + vec_ref[12:13, :]
    unit, scale = normed(mid)
    unit_s[...] = unit
    h2_ref[...] = (unit * vec_ref[1:2, :] + vec_ref[7:8, :]).astype(LOW)
    store(h2_ref, h2_hbm.at[mine, :])
    back_s[...] = jnp.zeros_like(back_s)
    c0 = 0.7978845608028654
    c1 = 0.044715
    loads[2].wait()
    loads[3].wait()

    def block_out(j):
        at = pl.ds(pl.multiple_of(j * width, width), width)
        return [
            pltpu.make_async_copy(g_ref.at[:, at], g_hbm.at[mine, at], out_sem.at[5 + 2 * j]),
            pltpu.make_async_copy(du_ref.at[:, at], du_hbm.at[mine, at], out_sem.at[6 + 2 * j]),
        ]

    def mlp(j, carry):
        at = pl.ds(pl.multiple_of(j * width, width), width)
        at2 = pl.ds(pl.multiple_of(hidden + j * width, width), width)
        u = dot(h2_ref[...], w_ref[:, at]) + vec_ref[pl.ds(8 + j, 1), :]
        dg = dot_nt(dy_ref[...], w_ref[:, at2])
        sq = u * u
        th = jnp.tanh(c0 * (u + c1 * (u * sq)))
        half = 0.5 + 0.5 * th
        g = (u * half).astype(LOW)
        slope = half + (0.5 * u) * ((1.0 - th * th) * (c0 + (3.0 * c0 * c1) * sq))
        du = (slope * dg).astype(LOW)
        g_ref[:, at] = g
        du_ref[:, at] = du
        for copy in block_out(j):
            copy.start()
        sum_ref[pl.ds(8 + j, 1), :] = jnp.sum(du.astype(F32), axis=0, keepdims=True)
        acc_s[...] += dot(g, w_ref[:, at2])
        back_s[...] += dot_nt(du, w_ref[:, at])
        return carry

    lax.fori_loop(0, blocks, mlp, 0)
    out_ref[...] = acc_s[...].astype(LOW)
    store(out_ref, out_hbm.at[mine, :])
    dy = dy_ref[...].astype(F32)
    e = back_s[...]
    unit = unit_s[...]
    sum_ref[12:13, :] = jnp.sum(dy, axis=0, keepdims=True)
    sum_ref[1:2, :] = jnp.sum(e * unit, axis=0, keepdims=True)
    sum_ref[7:8, :] = jnp.sum(e, axis=0, keepdims=True)
    dmid = dy + norm_back(e, vec_ref[1:2, :], unit, scale)
    dmid_ref[...] = dmid
    store(dmid_ref, dmid_hbm.at[mine, :])
    dmb = dmid.astype(LOW)
    dmb_ref[...] = dmb
    store(dmb_ref, dmb_hbm.at[mine, :])
    sum_ref[6:7, :] = jnp.sum(dmb.astype(F32), axis=0, keepdims=True)
    back_s[...] = dot_nt(dmb, w_out[...])

    def back(s, carry):
        rows = pl.ds(pl.multiple_of(s * PAIR, PAIR), PAIR)
        odd = lane % 2 == 1
        across = jnp.where((sub < HD) != low, 1.0, 0.0).astype(LOW)
        across = jnp.concatenate([across, across], axis=0)
        for p in range(pairs):
            at = slice(p * PAIR, (p + 1) * PAIR)
            dctx = back_s[rows, at]
            dn = dctx * inv_s[rows, at]
            prod = dctx * ctx_s[rows, at]
            high = prod.astype(LOW)
            rest_prod = (prod - high.astype(F32)).astype(LOW)
            dd = -dot(jnp.concatenate([high, rest_prod], axis=1), across) * swap_s[rows, at]
            extra = jnp.where(odd, dd - dd.astype(LOW).astype(F32), dd)
            for which, own in ((0, low), (1, jnp.logical_not(low))):
                h = 2 * p + which
                aug = jnp.where(own, dn, jnp.where(edge_lanes(p, which), extra, 0.0))
                dn_ref[rows, h * PAIR : (h + 1) * PAIR] = aug.astype(LOW)
        dn_out(s).start()
        cols = jnp.zeros((PAIR, PAIR), F32)
        for p in range(pairs):
            got = []
            for which in range(2):
                h = 2 * p + which
                got.append(dot(pq_ref[s, h], dn_ref[rows, h * PAIR : (h + 1) * PAIR]))
                cols = jnp.where(edge_lanes(p, which), got[-1], cols)
            ds_ref[s, p * PAIR : (p + 1) * PAIR, :] = jnp.where(low, got[0], got[1]).astype(LOW)
        ds_ref[s, width : width + ZROWS, :] = dot_nt(head_lanes(False), cols.astype(LOW)).astype(LOW)
        return carry

    lax.fori_loop(0, seqs, back, 0)
    for copy in stores:
        copy.wait()
    for j in range(blocks):
        for copy in block_out(j):
            copy.wait()
    for s in range(seqs):
        dn_out(s).wait()


def leave_kernel(
    core_ref, qkv_ref, pq_ref, pk_ref, pa_ref, pb_ref, po_ref, la_ref, lb_ref, lo_ref, dn_ref, maps_ref, *rest
):
    dqkv_ref, gmap_ref, pri_s, dl_s, da_s, df_s, left_s, back_s = rest[-8:]
    width = qkv_ref.shape[1] // 3
    heads = pq_ref.shape[1]
    pairs = heads // 2
    step = pl.program_id(0)

    @pl.when(step == 0)
    def _():
        gmap_ref[...] = jnp.zeros_like(gmap_ref)

    compose(step, core_ref, (pa_ref, pb_ref, po_ref), pri_s, False)
    compose(step, core_ref, (la_ref, lb_ref, lo_ref), dl_s, True)
    lane, sub = lanes(), subs()
    low = lane < HD
    masks = [jnp.where(low, 1.0, 0.0).astype(LOW), jnp.where(low, 0.0, 1.0).astype(LOW)]
    zcol = dot_tn(pri_s[width : width + ZROWS, :], head_lanes(False)).astype(LOW)
    dzcol = dot_tn(dl_s[width : width + ZROWS, :], head_lanes(True)).astype(LOW)
    every = [(p, which, 2 * p + which) for p in range(pairs) for which in range(2)]
    column = lambda part, p: slice(part * width + p * PAIR, part * width + (p + 1) * PAIR)
    edge = lambda p, which: jnp.where(edge_lanes(p, which), 1.0, 0.0).astype(LOW)
    dn_of = lambda h: dn_ref[:, h * PAIR : (h + 1) * PAIR]
    for p, which, h in every:
        dn = dn_of(h)
        vaug = qkv_ref[:, column(2, p)] * masks[which] + edge(p, which)
        da_s[h, :, :PAIR] = jnp.where(sub >= lane, dot_nt(dn, vaug), 0.0).astype(LOW)
        da_s[h, :, PAIR:] = dn
        back_s[h, :, :PAIR] = jnp.where(sub <= lane, dot_nt(vaug, dn), 0.0).astype(LOW)
        back_s[h, :, PAIR:] = vaug
        keys = pk_ref[0, h].T
        left_s[h, :, :PAIR] = jnp.where(sub <= lane, dot(keys, pq_ref[0, h]), 0.0).astype(LOW)
        left_s[h, :, PAIR:] = keys
    for p, which, h in every:
        half = slice(which * HD, (which + 1) * HD)
        saug = pri_s[column(0, p), :] * masks[which] + zcol * edge(p, which)
        dpq = dot_nt(jnp.concatenate([pk_ref[0, h], saug], axis=1), da_s[h])
        df_s[0, p, half, :] = soft_back(pq_ref[0, h].astype(F32), dpq).astype(LOW)
    for p, which, h in every:
        half = slice(which * HD, (which + 1) * HD)
        laug = dl_s[column(0, p), :] * masks[which] + dzcol * edge(p, which)
        dpk = dot_nt(jnp.concatenate([pq_ref[0, h], laug], axis=1), back_s[h])
        df_s[1, p, half, :] = soft_back(pk_ref[0, h].astype(F32), dpk).astype(LOW)
    for p in range(pairs):
        dn = dn_of(2 * p) * masks[0] + dn_of(2 * p + 1) * masks[1]
        right = jnp.concatenate([dn, dl_s[column(0, p), :]], axis=0)
        left = jnp.concatenate([left_s[2 * p], left_s[2 * p + 1]], axis=0)
        both = dot(left, right)
        dqkv_ref[:, column(2, p)] = jnp.where(low, both[:PAIR], both[PAIR:]).astype(LOW)
    for part in range(2):
        for p in range(pairs):
            df = df_s[part, p]
            gmap_ref[part, p] += dot(df, qkv_ref[:, column(part, p)])
            dqkv_ref[:, column(part, p)] = dot(df.T, maps_ref[part, p]).astype(LOW)


def norm_kernel(x_ref, d_ref, w_ref, dmid_ref, vec_ref, dx_ref):
    e = dot_nt(d_ref[...], w_ref[...])
    unit, scale = normed(x_ref[...].astype(F32))
    dx_ref[...] = dmid_ref[...] + norm_back(e, vec_ref[0:1, :], unit, scale)


def put(value, core_ref, keep_ref, give_ref):
    count, rows, _ = keep_ref.shape
    value = value.reshape(count, 2, rows, value.shape[-1])
    even, odd = value[:, 0], value[:, 1]
    low = core_ref[0] == 0
    keep_ref[...] = jnp.where(low, even, odd).astype(LOW)
    give_ref[...] = jnp.where(low, odd, even).astype(LOW)


def weight_kernel(core_ref, h2_ref, du_ref, g_ref, dy_hbm, a_hbm, dmb_hbm, *rest):
    outs, (dy_ref, a_ref, dmb_ref, sem) = rest[:-4], rest[-4:]
    step = pl.program_id(0)
    pieces = ((dy_hbm, dy_ref), (a_hbm, a_ref), (dmb_hbm, dmb_ref))
    loads = [pltpu.make_async_copy(far, near, sem.at[k]) for k, (far, near) in enumerate(pieces)]

    @pl.when(step == 1)
    def _():
        for copy in loads:
            copy.start()

    @pl.when(step == (pl.num_programs(0) - 1) // 2)
    def _():
        for copy in loads:
            copy.wait()

    blocks = (pl.num_programs(0) - 1) // 2

    def write(value):
        if len(outs) == 1:
            outs[0][...] = value.astype(LOW)
        else:
            put(value, core_ref, *outs)

    @pl.when(step < blocks)
    def _():
        write(dot_tn(h2_ref[...], du_ref[...]))

    @pl.when(jnp.logical_and(step >= blocks, step < 2 * blocks))
    def _():
        write(dot_tn(g_ref[...], dy_ref[...]))

    @pl.when(step == 2 * blocks)
    def _():
        write(dot_tn(a_ref[...], dmb_ref[...]))


def first_kernel(core_ref, h_ref, d_ref, w_ref, g0_ref, g1_ref, row_ref, *rest):
    outs, (rows_s, gain_s, shift_s) = rest[:-3], rest[-3:]
    step = pl.program_id(0)
    last = pl.num_programs(0) - 1
    width = h_ref.shape[1]

    def write(value, start):
        at = pl.ds(start, value.shape[1])
        if len(outs) == 1:
            outs[0][:, at] = value.astype(LOW)
        else:
            put(value, core_ref, *(out.at[:, :, at] for out in outs))

    @pl.when(step == 0)
    def _():
        rows_s[...] = row_ref[...]
        gain_s[...] = jnp.zeros_like(gain_s)
        shift_s[...] = jnp.zeros_like(shift_s)

    at = pl.ds(pl.multiple_of(step * width, width), width)
    value = dot_tn(h_ref[...], d_ref[...])
    write(value, pl.multiple_of(step * width, width))
    w = w_ref[:, at].astype(F32)
    sums = jnp.sum(d_ref[...].astype(F32), axis=0, keepdims=True)
    rows_s[pl.ds(3 + step, 1), :] = sums
    gain_s[...] += jnp.sum(w * value, axis=1, keepdims=True)
    shift_s[...] += jnp.sum(w * sums, axis=1, keepdims=True)

    @pl.when(step == last)
    def _():
        lane, sub = lanes(), subs()
        fill = jnp.zeros((PAIR - ZROWS, PAIR), F32)
        blocks = []
        for p in range(g0_ref.shape[1]):
            at = slice(p * PAIR, (p + 1) * PAIR)
            q = (g0_ref[0, p] + g1_ref[0, p]).T
            k = (g0_ref[1, p] + g1_ref[1, p]).T
            upper = sub < HD
            q = jnp.where(upper, q, pltpu.roll(q, HD, 1))
            k = jnp.where(upper, pltpu.roll(k, HD, 1), k)
            cols = jnp.concatenate([rows_s[:, at], fill], axis=0).T
            own = w_ref[at, 3 * width + PAIR :].astype(F32)
            shift = shift_s[at]
            gain = (gain_s[at] - own[:, 2:3] * shift) / own[:, 0:1]
            cols = jnp.where(lane == 0, gain, jnp.where(lane == 2, shift, cols))
            blocks.append(jnp.concatenate([jnp.where(lane < HD, q, k), cols], axis=1))
        write(jnp.concatenate(blocks, axis=0), 3 * width)


def whole(shape):
    return pl.BlockSpec(shape, lambda i: (0,) * len(shape), pipeline_mode=pl.Buffered(1))


def part(shape, *at):
    return pl.BlockSpec(shape, lambda i: at, pipeline_mode=pl.Buffered(1))


PLAIN = pltpu.CompilerParams(vmem_limit_bytes=VMEM_BYTES)
PARAMS = dict(
    compiler_params=pltpu.CompilerParams(
        dimension_semantics=("arbitrary",), vmem_limit_bytes=VMEM_BYTES
    )
)


def cost(flops, size):
    return pl.CostEstimate(flops=20 * int(flops), bytes_accessed=20 * int(size), transcendentals=0)


def enter(m, held, x, w, maps, vec, heads):
    total, width = x.shape
    rows = total // 2
    seqs = rows // PAIR
    pack = width + ZROWS
    extra = [] if held is None else [held]
    return pl.pallas_call(
        enter_kernel,
        grid=(seqs,),
        in_specs=[
            part((rows, width), m, 0),
            part((width, 3 * width), 0, 0),
            whole(maps.shape),
            whole(vec.shape),
        ]
        + [pl.BlockSpec(memory_space=pl.ANY)] * len(extra),
        out_specs=[
            pl.BlockSpec((PAIR, width), lambda i: (m * seqs + i, 0)),
            pl.BlockSpec((PAIR, 3 * width), lambda i: (i, 0)),
            pl.BlockSpec((1, heads, PAIR, PAIR), lambda i: (i, 0, 0, 0)),
            pl.BlockSpec((1, heads, PAIR, PAIR), lambda i: (i, 0, 0, 0)),
            pl.BlockSpec((1, pack, PAIR), lambda i: (i, 0, 0)),
        ],
        out_shape=[
            jax.ShapeDtypeStruct((total, width), LOW),
            jax.ShapeDtypeStruct((rows, 3 * width), LOW),
            jax.ShapeDtypeStruct((seqs, heads, PAIR, PAIR), LOW),
            jax.ShapeDtypeStruct((seqs, heads, PAIR, PAIR), LOW),
            jax.ShapeDtypeStruct((seqs, pack, PAIR), LOW),
        ],
        scratch_shapes=[pltpu.VMEM((rows, width), LOW), pltpu.VMEM((rows, 3 * width), LOW)],
        input_output_aliases={4 + k: k for k in range(len(extra))},
        cost_estimate=cost(6 * rows * width * width, 12 * rows * width),
        name="enter",
        **PARAMS,
    )(x, w, maps, vec, *extra)


def middle(m, held, core, x, dy, qkv, pq, pk, pri, w, vec, hidden):
    total, width = x.shape
    rows = total // 2
    seqs, heads = pq.shape[0], pq.shape[1]
    pack = width + ZROWS
    extra = [] if held is None else list(held)
    shared = [(width, LOW)] * 3 + [(hidden, LOW)] * 2 + [(width, F32), (width, LOW)]
    far = pl.BlockSpec(memory_space=pl.ANY)
    dn = jax.ShapeDtypeStruct((rows, heads * PAIR), LOW)
    ends = [
        jax.ShapeDtypeStruct((seqs, pack, PAIR), LOW),
        jax.ShapeDtypeStruct((ZROWS, width), F32),
    ]
    return pl.pallas_call(
        functools.partial(middle_kernel, m),
        grid=(1,),
        in_specs=[pl.BlockSpec(memory_space=pltpu.SMEM), far, far, part((rows, width), 0, 2), far, far]
        + [whole(piece.shape) for piece in pri]
        + [far, whole(vec.shape)]
        + [far] * len(extra),
        out_specs=[far] * (len(shared) + 1) + [whole(end.shape) for end in ends],
        out_shape=[jax.ShapeDtypeStruct((total, n), t) for n, t in shared] + [dn] + ends,
        scratch_shapes=[
            pltpu.VMEM((rows, width), LOW),
            pltpu.VMEM((rows, width), LOW),
            pltpu.VMEM(pq.shape, LOW),
            pltpu.VMEM(pk.shape, LOW),
            pltpu.VMEM(w.shape, LOW),
        ]
        + [pltpu.VMEM((rows, n), t) for n, t in shared]
        + [pltpu.VMEM(dn.shape, LOW)]
        + [pltpu.VMEM((rows, width), F32)] * 6
        + [
            pltpu.VMEM((pack, PAIR), LOW),
            pltpu.VMEM((heads, PAIR, 2 * PAIR), LOW),
            pltpu.SemaphoreType.DMA((3, seqs)),
            pltpu.SemaphoreType.DMA((4,)),
            pltpu.SemaphoreType.DMA((5 + 2 * (hidden // width),)),
        ],
        input_output_aliases={11 + k: k for k in range(len(extra))},
        cost_estimate=cost(8 * rows * width * hidden + 4 * rows * width * width, 30 * rows * width),
        name="middle",
        **PARAMS,
    )(core, x, dy, qkv, pq, pk, *pri, w, vec, *extra)


def leave(m, held, core, qkv, pq, pk, pri, dl, dn, maps):
    rows, wide = qkv.shape
    total = 2 * rows
    seqs, heads = pq.shape[:2]
    pack = pri[2].shape[1]
    each = lambda array: pl.BlockSpec((1,) + array.shape[1:], lambda i: (i,) + (0,) * (array.ndim - 1))
    state = lambda pieces: [whole(pieces[0].shape), whole(pieces[1].shape), each(pieces[2])]
    extra = [] if held is None else [held]
    return pl.pallas_call(
        leave_kernel,
        grid=(seqs,),
        in_specs=[
            pl.BlockSpec(memory_space=pltpu.SMEM),
            pl.BlockSpec((PAIR, wide), lambda i: (i, 0)),
            each(pq),
            each(pk),
        ]
        + state(pri)
        + state(dl)
        + [pl.BlockSpec((PAIR, dn.shape[1]), lambda i: (i, 0)), whole(maps.shape)]
        + [pl.BlockSpec(memory_space=pl.ANY)] * len(extra),
        out_specs=[pl.BlockSpec((PAIR, wide), lambda i: (m * seqs + i, 0)), whole(maps.shape)],
        out_shape=[
            jax.ShapeDtypeStruct((total, wide), LOW),
            jax.ShapeDtypeStruct(maps.shape, F32),
        ],
        scratch_shapes=[
            pltpu.VMEM((pack, PAIR), LOW),
            pltpu.VMEM((pack, PAIR), LOW),
            pltpu.VMEM((heads, PAIR, 2 * PAIR), LOW),
            pltpu.VMEM((2, heads // 2, PAIR, PAIR), LOW),
            pltpu.VMEM((heads, PAIR, 2 * PAIR), LOW),
            pltpu.VMEM((heads, PAIR, 2 * PAIR), LOW),
        ],
        input_output_aliases={12 + k: k for k in range(len(extra))},
        cost_estimate=cost(8 * rows * wide * PAIR, 8 * rows * wide),
        name="leave",
        **PARAMS,
    )(core, qkv, pq, pk, *pri, *dl, dn, maps, *extra)


def norm_grads(x, dqkv, w, dmid, vec):
    total, width = x.shape
    rows = min(total, 256)
    return pl.pallas_call(
        norm_kernel,
        grid=(total // rows,),
        in_specs=[
            pl.BlockSpec((rows, width), lambda i: (i, 0)),
            pl.BlockSpec((rows, 3 * width), lambda i: (i, 0)),
            part((width, 3 * width), 0, 0),
            pl.BlockSpec((rows, width), lambda i: (i, 0)),
            whole(vec.shape),
        ],
        out_specs=pl.BlockSpec((rows, width), lambda i: (i, 0)),
        out_shape=jax.ShapeDtypeStruct((total, width), F32),
        cost_estimate=cost(6 * total * width * width, 12 * total * width),
        name="norm",
        **PARAMS,
    )(x, dqkv, w, dmid, vec)


def prepare(core, mine, theirs, heads):
    count, rows, columns = mine.shape
    width = 2 * count * rows
    outs = [
        jax.ShapeDtypeStruct((2, heads // 2, PAIR, PAIR), LOW),
        jax.ShapeDtypeStruct((ZROWS, width), F32),
    ]
    if rows % 8 != 0:
        low = core[0] == 0
        both = [jnp.where(low, mine, theirs), jnp.where(low, theirs, mine)]
        w = jnp.stack(both, axis=1).reshape(width, columns)
        maps, vec = pl.pallas_call(
            tail_kernel, out_shape=outs, name="tail", compiler_params=PLAIN
        )(w[:, columns - 2 * PAIR :])
        return w, maps, vec
    w, maps, vec = pl.pallas_call(
        prepare_kernel,
        grid=(1,),
        in_specs=[
            pl.BlockSpec(memory_space=pltpu.SMEM),
            whole(mine.shape),
            whole(theirs.shape),
        ],
        out_specs=[
            whole((count, 2, rows, columns)),
            whole(outs[0].shape),
            whole(outs[1].shape),
        ],
        out_shape=[jax.ShapeDtypeStruct((count, 2, rows, columns), LOW)] + outs,
        name="prepare",
        **PARAMS,
    )(core, mine, theirs)
    return w.reshape(width, columns), maps, vec


def out_halves(width, rows, columns, size):
    if rows % 8 != 0:
        return (
            [pl.BlockSpec((width, size), lambda i: (0, i))],
            [jax.ShapeDtypeStruct((width, columns), LOW)],
        )
    count = width // rows // 2
    return (
        [pl.BlockSpec((count, rows, size), lambda i: (0, 0, i))] * 2,
        [jax.ShapeDtypeStruct((count, rows, columns), LOW)] * 2,
    )


def weight_grads(core, rows, h2, du, g, dy, a, dmb):
    total, width = h2.shape
    blocks = du.shape[1] // width
    last = 2 * blocks
    block = (total, width)
    specs, shapes = out_halves(width, rows, (last + 1) * width, width)
    return pl.pallas_call(
        weight_kernel,
        grid=(last + 1,),
        in_specs=[
            pl.BlockSpec(memory_space=pltpu.SMEM),
            pl.BlockSpec(block, lambda i: (0, 0)),
            pl.BlockSpec(block, lambda i: (0, jnp.minimum(i, blocks - 1))),
            pl.BlockSpec(block, lambda i: (0, jnp.clip(i - blocks, 0, blocks - 1))),
        ]
        + [pl.BlockSpec(memory_space=pl.ANY)] * 3,
        out_specs=specs,
        out_shape=shapes,
        scratch_shapes=[pltpu.VMEM(block, LOW)] * 3 + [pltpu.SemaphoreType.DMA((3,))],
        cost_estimate=cost(2 * total * width * width * (last + 1), 20 * total * width),
        name="weights",
        **PARAMS,
    )(core, h2, du, g, dy, a, dmb)


def first_grads(core, rows, hid, dqkv, w, gmaps, sums):
    total, width = hid.shape
    specs, shapes = out_halves(width, rows, w.shape[1], w.shape[1])
    specs = [whole(shape.shape) for shape in shapes]
    return pl.pallas_call(
        first_kernel,
        grid=(3,),
        in_specs=[
            pl.BlockSpec(memory_space=pltpu.SMEM),
            whole(hid.shape),
            pl.BlockSpec((total, width), lambda i: (0, i)),
            whole(w.shape),
            whole(gmaps[0].shape),
            whole(gmaps[1].shape),
            whole(sums.shape),
        ],
        out_specs=specs,
        out_shape=shapes,
        scratch_shapes=[
            pltpu.VMEM((ZROWS, width), F32),
            pltpu.VMEM((width, 1), F32),
            pltpu.VMEM((width, 1), F32),
        ],
        cost_estimate=cost(6 * total * width * width, 12 * total * width),
        name="first",
        **PARAMS,
    )(core, hid, dqkv, w, *gmaps, sums)


def shards(tokens, w_qkv, w_feat, w_out, w_fc, w_proj, gains, biases, cotangent):
    micro_count, seq_count, seg_len, width = tokens.shape
    grid = grid_dims()
    rows = w_qkv.shape[0]
    hidden = w_fc.shape[1]
    ratio = hidden // width
    heads = width // HD
    pairs = heads // 2
    wide = 3 * width
    total = micro_count * seq_count * seg_len

    first = jnp.concatenate(
        [
            w_qkv.astype(LOW),
            jnp.transpose(w_feat, (1, 0, 2)).reshape(rows, PAIR).astype(LOW),
            jnp.pad(jnp.concatenate([gains, biases]).T.astype(LOW), ((0, 0), (0, PAIR - 13))),
        ],
        axis=1,
    )
    core = jnp.reshape(grid[1]["c"], (1,))
    first, maps, vec = prepare(core, *gather_rows(first, grid), heads)
    later = jnp.concatenate(
        [
            w_fc.astype(LOW).reshape(rows, width, ratio).swapaxes(1, 2).reshape(rows, hidden),
            w_proj.astype(LOW).reshape(rows, hidden),
            w_out.astype(LOW),
        ],
        axis=1,
    )
    later = lax.all_gather(later, AXES, axis=0, tiled=True)
    fc_bias = vec[8 : 8 + ratio].reshape(width, ratio).T
    mid_vec = jnp.concatenate([vec[:8], fc_bias, vec[8 + ratio :]])
    x = tokens.reshape(total, width)
    dy = cotangent.reshape(total, width)

    entered, swaps, steps = [], [], []
    for m in range(2):
        held = entered[0][0] if m else None
        held_vec = tie(vec, swaps[0][0]) if m else vec
        entered.append(enter(m, held, x, first, maps, held_vec, heads))
        own = entered[m][4]
        if m:
            steps[0].round(entered[1][1])
            own = tie(own, steps[0].running)
        swaps.append(swap(own, grid))
        steps.append(Steps(swaps[m][0], grid, False))
    hid = entered[1][0]
    steps[1].round()
    ready = steps[1].running
    priors = [steps[m].end(swaps[m][1]) for m in range(2)]
    held, mids, swaps, steps = None, [], [], []
    for m in range(2):
        _, qkv, pq, pk, _ = entered[m]
        held_vec = tie(mid_vec, swaps[0][0] if m else ready)
        got = middle(m, held, core, x, dy, qkv, pq, pk, priors[m], later, held_vec, hidden)
        held, rest = got[:7], got[7:]
        mids.append(rest)
        own = rest[1]
        if m:
            steps[0].round(rest[2])
            own = tie(own, steps[0].running)
        swaps.append(swap(own, grid))
        steps.append(Steps(swaps[m][0], grid, True))
    out, a, h2, g, du, dmid, dmb = held
    g_later = weight_grads(tie(core, swaps[1][0]), rows, h2, du, g, dy, a, dmb)
    if len(g_later) == 1:
        g_later = halves(g_later[0], grid, rows)
    inner = mids[0][2] + mids[1][2]
    g_fc_bias = inner[8 : 8 + ratio].T.reshape(ratio, width)
    sums = jnp.concatenate([inner[:8], g_fc_bias, inner[8 + ratio :]])
    keep, give = g_later
    laters = [steps[0].end(swaps[0][1], give)]
    steps[1].round(give)
    _, qkv, pq, pk, _ = entered[0]
    kept, gmap = leave(0, None, core, qkv, pq, pk, priors[0], laters[0], mids[0][0], maps)
    gmaps = [gmap]
    scatter = Scatter(keep, tie(give, laters[0][0], steps[1].running), grid, gmap)
    laters.append(steps[1].end(swaps[1][1], gmap))
    _, qkv, pq, pk, _ = entered[1]
    held_core = tie(core, scatter.left, scatter.right)
    dqkv, gmap = leave(1, kept, held_core, qkv, pq, pk, priors[1], laters[1], mids[1][0], maps)
    gmaps.append(gmap)
    g_qkv = first_grads(core, rows, hid, dqkv, first, gmaps, sums)
    if len(g_qkv) == 1:
        g_qkv = halves(g_qkv[0], grid, rows)
    scatter.one(g_qkv[0])
    ending = Scatter(*g_qkv, grid, scatter.left)
    held_vec = tie(vec, ending.left, ending.right, scatter.right)
    dx = norm_grads(x, dqkv, first, dmid, held_vec)
    scatter.two(dx)
    ending.one(scatter.left)
    ending.two()
    r_later = scatter.end(ending.left)
    last = ending.end().astype(F32)
    r_fc = r_later[:, :hidden]
    r_proj = r_later[:, hidden : 2 * hidden]
    r_out = r_later[:, 2 * hidden :]
    small = last[:, wide + PAIR :].T
    return (
        out.reshape(tokens.shape),
        dx.reshape(tokens.shape),
        last[:, :wide],
        jnp.transpose(last[:, wide : wide + PAIR].reshape(rows, 2, HD), (1, 0, 2)),
        r_out.astype(F32),
        r_fc.astype(F32).reshape(rows, ratio, width).swapaxes(1, 2).reshape(rows, hidden),
        r_proj.astype(F32).reshape(rows * ratio, width),
        small[:2],
        small[2:13],
    )


def solution(mesh):
    return jax.shard_map(
        shards,
        mesh=mesh,
        in_specs=(
            P(None, "dp", "seq", None),
            P(("dp", "seq"), None),
            P(None, ("dp", "seq"), None),
            P(("dp", "seq"), None),
            P(("dp", "seq"), None),
            P(("dp", "seq"), None),
            P(None, ("dp", "seq")),
            P(None, ("dp", "seq")),
            P(None, "dp", "seq", None),
        ),
        out_specs=(
            P(None, "dp", "seq", None),
            P(None, "dp", "seq", None),
            P(("dp", "seq"), None),
            P(None, ("dp", "seq"), None),
            P(("dp", "seq"), None),
            P(("dp", "seq"), None),
            P(("dp", "seq"), None),
            P(None, ("dp", "seq")),
            P(None, ("dp", "seq")),
        ),
        check_vma=False,
    )
```

```python
import functools

import jax
import jax.numpy as jnp
from jax import lax
from jax.experimental import pallas as pl
from jax.experimental.pallas import tpu as pltpu
from jax.sharding import PartitionSpec as P

HD = 64
PAIR = 2 * HD
AXES = ("dp", "seq")
LOW = jnp.bfloat16
F32 = jnp.float32
VMEM_BYTES = 60 * 1024 * 1024
ZROWS = 16

def grid_dims():
    n_dp, n_seq = lax.axis_size("dp"), lax.axis_size("seq")
    n_x = 1
    while n_x * n_x * 4 <= n_dp:
        n_x *= 2
    sizes = {"y": n_dp // n_x, "x": n_x, "z": n_seq // 2, "c": 2}
    at = lax.axis_index("dp") * n_seq + lax.axis_index("seq")
    place = {}
    for name in ("c", "z", "x", "y"):
        place[name] = lax.rem(at, sizes[name])
        at = at // sizes[name]
    return sizes, place


def turned(sizes, name, step):
    pairs = []
    for y in range(sizes["y"]):
        for x in range(sizes["x"]):
            for z in range(sizes["z"]):
                for c in range(sizes["c"]):
                    to = {"y": y, "x": x, "z": z, "c": c}
                    to[name] = (to[name] + step) % sizes[name]
                    flat = lambda p: ((p[0] * sizes["x"] + p[1]) * sizes["z"] + p[2]) * 2 + p[3]
                    pairs.append((flat((y, x, z, c)), flat((to["y"], to["x"], to["z"], to["c"]))))
    return pairs


def send(value, sizes, name, step):
    return lax.ppermute(value, AXES, turned(sizes, name, step))


def tie(value, *others):
    others = [other for other in others if other is not None]
    return lax.optimization_barrier((value, *others))[0] if others else value


def spread(own, got, place):
    at = lax.broadcasted_iota(jnp.int32, (2,) + (1,) * own.ndim, 0)
    return jnp.where(at == place, own[None], got[None])


def gather_dim(value, grid, name):
    sizes, place = grid
    count = sizes[name]
    if count == 1:
        return value[None]
    got = [value] + [send(value, sizes, name, k) for k in range(1, count)]
    if count == 2:
        return spread(got[0], got[1], place[name])
    order = jnp.stack(got[::-1] + got[::-1][:-1])
    return lax.dynamic_slice_in_dim(order, count - 1 - place[name], count, 0)


def gather_rows(value, grid):
    sizes, _ = grid
    out = gather_dim(value, grid, "z")
    columns = value.shape[1] // 2
    left, right = out[..., :columns], out[..., columns:]
    left, right = gather_dim(left, grid, "x"), gather_dim(right, grid, "y")
    left, right = gather_dim(left, grid, "y"), gather_dim(right, grid, "x")
    out = jnp.concatenate([left, jnp.swapaxes(right, 0, 1)], axis=-1)
    out = out.reshape((-1,) + value.shape)
    return out, send(out, sizes, "c", 1)


def scatter_dim(value, grid, name, axis, after=None):
    sizes, place = grid
    count = sizes[name]
    mine = lax.dynamic_index_in_dim(value, place[name], axis, keepdims=False)
    if count == 1:
        return mine
    total = mine.astype(F32)
    for k in range(1, count):
        to = lax.rem(place[name] + k, count)
        block = lax.dynamic_index_in_dim(value, to, axis, keepdims=False)
        total = total + tie(send(block, sizes, name, k), after).astype(F32)
    return total.astype(LOW)


class Scatter:
    def __init__(self, keep, give, grid, after=None):
        sizes, _ = grid
        self.grid = grid
        got = tie(send(give, sizes, "c", 1), after)
        shape = (sizes["y"], sizes["x"], sizes["z"]) + keep.shape[1:]
        keep, got = keep.reshape(shape), got.reshape(shape)
        cut = keep.shape[-1] // 256 * 128
        add = lambda a, b: (a.astype(F32) + b.astype(F32)).astype(LOW)
        self.left = add(keep[..., :cut], got[..., :cut])
        self.right = add(keep[..., cut:], got[..., cut:])

    def one(self, after=None):
        self.left = scatter_dim(self.left, self.grid, "x", 1, after)
        self.right = scatter_dim(self.right, self.grid, "y", 0, after)

    def two(self, after=None):
        self.left = scatter_dim(self.left, self.grid, "y", 0, after)
        self.right = scatter_dim(self.right, self.grid, "x", 0, after)

    def end(self, after=None):
        both = jnp.concatenate([self.left, self.right], axis=-1)
        return scatter_dim(both, self.grid, "z", 0, after)


def halves(value, grid, rows):
    _, place = grid
    value = value.reshape(-1, 2, rows, value.shape[-1])
    pick = lambda at: lax.dynamic_index_in_dim(value, at, 1, keepdims=False)
    return pick(place["c"]), pick(1 - place["c"])


def some(sizes, step, chosen):
    pairs = []
    for a, b in turned(sizes, "z", step):
        z = (a // 2) % sizes["z"]
        if 0 <= z + step < sizes["z"] and chosen(z):
            pairs.append((a, b))
    return pairs


def swap(own, grid):
    sizes, place = grid
    half = own.shape[0] // 2
    other = send(own, sizes, "c", 1)
    first = place["c"] * half
    mine = lax.dynamic_slice_in_dim(own, first, half, 0).astype(F32)
    mine = (mine + lax.dynamic_slice_in_dim(other, first, half, 0).astype(F32)).astype(LOW)
    return mine, other


class Steps:
    def __init__(self, mine, grid, reverse):
        self.running, self.mine, self.total, self.span = mine, mine, 0.0, 1
        self.sizes, self.reverse = grid[0], reverse

    def round(self, after=None):
        count, span = self.sizes["z"], self.span
        if span >= count:
            return
        back = lambda z: count - 1 - z if self.reverse else z
        four = count == 4 and self.reverse
        if four and span == 1:
            sends = [(1, lambda z: True), (2, lambda z: back(z) == 0)]
        elif four:
            sends = [(1, lambda z: back(z) == 2)]
        else:
            sends = [(d, lambda z: back(z) % (2 * span) == span - 1) for d in range(1, span + 1)]
        got = 0.0
        for d, chosen in sends:
            pairs = some(self.sizes, -d if self.reverse else d, chosen)
            got = got + tie(lax.ppermute(self.running, AXES, pairs), after).astype(F32)
        self.total = self.total + got
        self.running = got.astype(LOW)
        if not four:
            self.running = (self.mine.astype(F32) + self.total).astype(LOW)
        self.span = 2 * span

    def end(self, other, after=None):
        while self.span < self.sizes["z"]:
            self.round(after)
        total = jnp.asarray(self.total + jnp.zeros(self.running.shape, F32)).astype(LOW)
        return total, send(total, self.sizes, "c", 1), other


def dot(a, b):
    return jnp.dot(a, b, preferred_element_type=F32)


def dot_nt(a, b):
    return lax.dot_general(a, b, (((1,), (1,)), ((), ())), preferred_element_type=F32)


def dot_tn(a, b):
    return lax.dot_general(a, b, (((0,), (0,)), ((), ())), preferred_element_type=F32)


def normed(values):
    centred = values - jnp.mean(values, axis=-1, keepdims=True)
    spread = jnp.mean(centred * centred, axis=-1, keepdims=True)
    scale = lax.rsqrt(spread + 1e-05)
    return centred * scale, scale


def norm_back(grad, gain, unit, scale):
    eg = grad * gain
    inner = eg - jnp.mean(eg, axis=-1, keepdims=True)
    return scale * (inner - unit * jnp.mean(eg * unit, axis=-1, keepdims=True))


def lanes(shape=(PAIR, PAIR)):
    return lax.broadcasted_iota(jnp.int32, shape, 1)


def subs(shape=(PAIR, PAIR)):
    return lax.broadcasted_iota(jnp.int32, shape, 0)


def head_lanes(first_only):
    lane, row = lanes((ZROWS, PAIR)), subs((ZROWS, PAIR))
    head = (lane % HD) // 2 * 2 + jnp.where(lane < HD, 1, 0)
    hit = head == row
    if first_only:
        hit = jnp.logical_and(hit, lane % 2 == 0)
    return jnp.where(hit, 1.0, 0.0).astype(LOW)


def edge_lanes(p, which):
    return lanes() // 2 == (p if which else HD // 2 + p)


def soft_pair(logits):
    high = jnp.max(logits, axis=0, keepdims=True)
    small = jnp.min(logits, axis=0, keepdims=True)
    e1 = jnp.exp(logits - high)
    e2 = jnp.exp(small - logits)
    p1 = e1 * (1.0 / jnp.sum(e1, axis=0, keepdims=True))
    p2 = e2 * (1.0 / jnp.sum(e2, axis=0, keepdims=True))
    return jnp.concatenate([p1, p2], axis=0)


def soft_back(phi, grad):
    prod = phi * grad
    s1 = jnp.sum(prod[:HD], axis=0, keepdims=True)
    s2 = jnp.sum(prod[HD:], axis=0, keepdims=True)
    return (prod[:HD] - phi[:HD] * s1) - (prod[HD:] - phi[HD:] * s2)


def prepare_kernel(core_ref, mine_ref, theirs_ref, w_ref, maps_ref, vec_ref):
    cut = w_ref.shape[-1] - 2 * PAIR

    def write(even_ref, odd_ref):
        w_ref[:, 0] = even_ref[...]
        w_ref[:, 1] = odd_ref[...]
        even = even_ref[:, :, cut:].astype(F32)[:, None]
        odd = odd_ref[:, :, cut:].astype(F32)[:, None]
        tail = jnp.concatenate([even, odd], axis=1)
        split_tail(tail.reshape(-1, 2 * PAIR), maps_ref, vec_ref)

    @pl.when(core_ref[0] == 0)
    def _():
        write(mine_ref, theirs_ref)

    @pl.when(core_ref[0] != 0)
    def _():
        write(theirs_ref, mine_ref)


def tail_kernel(tail_ref, maps_ref, vec_ref):
    split_tail(tail_ref[...].astype(F32), maps_ref, vec_ref)


def split_tail(tail, maps_ref, vec_ref):
    low = lanes((HD, PAIR)) < HD
    for p in range(maps_ref.shape[1]):
        at = slice(p * PAIR, (p + 1) * PAIR)
        both = tail[at, :PAIR].T
        for which in range(2):
            one = both[which * HD : (which + 1) * HD]
            block = [jnp.where(low, one, 0.0), jnp.where(low, 0.0, one)]
            maps_ref[which, p] = jnp.concatenate(block, axis=0).astype(LOW)
        vec_ref[:, at] = tail[at, PAIR:].T[:ZROWS]


def enter_kernel(x_ref, w_ref, maps_ref, vec_ref, *rest):
    hid_ref, qkv_ref, pq_ref, pk_ref, st_ref, hid_s, qkv_s = rest[-7:]
    width = x_ref.shape[1]
    pairs = pq_ref.shape[1] // 2
    step = pl.program_id(0)

    @pl.when(step == 0)
    def _():
        unit, _ = normed(x_ref[...].astype(F32))
        hid_s[...] = (unit * vec_ref[0:1, :] + vec_ref[2:3, :]).astype(LOW)
        for part in range(3):
            span = slice(part * width, (part + 1) * width)
            value = dot(hid_s[...], w_ref[:, span]) + vec_ref[3 + part : 4 + part, :]
            qkv_s[:, span] = value.astype(LOW)

    rows = pl.ds(pl.multiple_of(step * PAIR, PAIR), PAIR)
    hid_ref[...] = hid_s[rows, :]
    qkv_ref[...] = qkv_s[rows, :]
    low = lanes() < HD
    ones = jnp.ones((PAIR, PAIR), LOW)
    for which, ref in ((1, pk_ref), (0, pq_ref)):
        for p in range(pairs):
            at = slice(which * width + p * PAIR, which * width + (p + 1) * PAIR)
            logits = dot_nt(maps_ref[which, p], qkv_s[rows, at])
            ref[0, 2 * p] = soft_pair(logits[:HD]).astype(LOW)
            ref[0, 2 * p + 1] = soft_pair(logits[HD:]).astype(LOW)
    cols = jnp.zeros((PAIR, PAIR), F32)
    for p in range(pairs):
        at = slice(p * PAIR, (p + 1) * PAIR)
        value = qkv_s[rows, 2 * width + p * PAIR : 2 * width + (p + 1) * PAIR]
        own = []
        for which in range(2):
            both = dot(pk_ref[0, 2 * p + which], jnp.concatenate([value, ones], axis=1))
            own.append(both[:, :PAIR])
            cols = jnp.where(edge_lanes(p, which), both[:, PAIR:], cols)
        st_ref[0, at, :] = jnp.where(low, own[0], own[1]).astype(LOW)
    st_ref[0, width : width + ZROWS, :] = dot_nt(head_lanes(True), cols.astype(LOW)).astype(LOW)


def compose(s, core_ref, refs, out_ref, reverse):
    mine_ref, theirs_ref, other_ref = refs
    half = mine_ref.shape[0]
    at = lax.rem(s, half)
    core = core_ref[0]

    @pl.when(s // half == core)
    def _():
        out_ref[...] = mine_ref[at]

    @pl.when(s // half != core)
    def _():
        out_ref[...] = theirs_ref[at]

    @pl.when(core == (0 if reverse else 1))
    def _():
        own = other_ref[0 if other_ref.shape[0] == 1 else s]
        out_ref[...] = (out_ref[...].astype(F32) + own.astype(F32)).astype(LOW)


def middle_kernel(
    place, core_ref, x_hbm, dy_hbm, v_ref, pq_hbm, pk_hbm, pa_ref, pb_ref, po_ref, w_hbm, vec_ref, *rest
):
    (out_hbm, a_hbm, h2_hbm, g_hbm, du_hbm, dmid_hbm, dmb_hbm, dn_hbm, ds_ref, sum_ref,
     x_ref, dy_ref, pq_ref, pk_ref, w_ref, out_ref, a_ref, h2_ref, g_ref, du_ref, dmid_ref, dmb_ref, dn_ref,
     ctx_s, inv_s, swap_s, unit_s, acc_s, back_s, pri_s, left_s, seq_sem, in_sem, out_sem) = rest[-34:]
    rows_all, width = x_ref.shape
    seqs, heads = pq_ref.shape[0], pq_ref.shape[1]
    pairs = heads // 2
    hidden = g_ref.shape[1]
    blocks = hidden // width
    mine = pl.ds(place * rows_all, rows_all)
    lane, sub = lanes(), subs()
    low = lane < HD

    def features(s):
        return [
            pltpu.make_async_copy(pq_hbm.at[s], pq_ref.at[s], seq_sem.at[0, s]),
            pltpu.make_async_copy(pk_hbm.at[s], pk_ref.at[s], seq_sem.at[1, s]),
        ]

    def dn_out(s):
        rows = pl.ds(pl.multiple_of(s * PAIR, PAIR), PAIR)
        return pltpu.make_async_copy(dn_ref.at[rows, :], dn_hbm.at[rows, :], seq_sem.at[2, s])

    for s in range(seqs):
        for copy in features(s):
            copy.start()
    tail = pl.ds(2 * hidden, width)
    loads = [
        pltpu.make_async_copy(w_hbm.at[:, tail], w_ref.at[:, tail], in_sem.at[0]),
        pltpu.make_async_copy(x_hbm.at[mine, :], x_ref, in_sem.at[1]),
        pltpu.make_async_copy(dy_hbm.at[mine, :], dy_ref, in_sem.at[2]),
        pltpu.make_async_copy(
            w_hbm.at[:, pl.ds(0, 2 * hidden)], w_ref.at[:, pl.ds(0, 2 * hidden)], in_sem.at[3]
        ),
    ]
    for copy in loads:
        copy.start()
    stores = []

    def store(have, there):
        copy = pltpu.make_async_copy(have, there, out_sem.at[len(stores)])
        copy.start()
        stores.append(copy)

    sum_ref[...] = jnp.zeros_like(sum_ref)

    def attend(s, carry):
        for copy in features(s):
            copy.wait()
        compose(s, core_ref, (pa_ref, pb_ref, po_ref), pri_s, False)
        rows = pl.ds(pl.multiple_of(s * PAIR, PAIR), PAIR)
        zsum = pri_s[width : width + ZROWS, :].astype(F32)
        invs = []
        for h in range(heads):
            phi = pq_ref[s, h].T
            score = jnp.where(sub >= lane, dot(phi, pk_ref[s, h]), 0.0).astype(LOW)
            left_s[h, :, :PAIR] = score
            left_s[h, :, PAIR:] = phi
            each = score.astype(F32) + phi.astype(F32) * zsum[h : h + 1, :]
            invs.append(1.0 / jnp.sum(each, axis=1, keepdims=True))
        for p in range(pairs):
            at = slice(p * PAIR, (p + 1) * PAIR)
            inv = jnp.where(low, invs[2 * p], invs[2 * p + 1])
            inv_s[rows, at] = inv
            swap_s[rows, at] = jnp.where(low, invs[2 * p + 1], invs[2 * p])
            right = jnp.concatenate([v_ref[rows, at], pri_s[at, :]], axis=0)
            left = jnp.concatenate([left_s[2 * p], left_s[2 * p + 1]], axis=0)
            both = dot(left, right)
            ctx = jnp.where(low, both[:PAIR], both[PAIR:]) * inv
            ctx_s[rows, at] = ctx
            a_ref[rows, at] = ctx.astype(LOW)
        return carry

    lax.fori_loop(0, seqs, attend, 0)
    store(a_ref, a_hbm.at[mine, :])
    w_out = w_ref.at[:, tail]
    loads[0].wait()
    loads[1].wait()
    mid = x_ref[...].astype(F32) + dot(a_ref[...], w_out[...]) + vec_ref[6:7, :]
    acc_s[...] = mid + vec_ref[12:13, :]
    unit, scale = normed(mid)
    unit_s[...] = unit
    h2_ref[...] = (unit * vec_ref[1:2, :] + vec_ref[7:8, :]).astype(LOW)
    store(h2_ref, h2_hbm.at[mine, :])
    back_s[...] = jnp.zeros_like(back_s)
    c0 = 0.7978845608028654
    c1 = 0.044715
    loads[2].wait()
    loads[3].wait()

    def block_out(j):
        at = pl.ds(pl.multiple_of(j * width, width), width)
        return [
            pltpu.make_async_copy(g_ref.at[:, at], g_hbm.at[mine, at], out_sem.at[5 + 2 * j]),
            pltpu.make_async_copy(du_ref.at[:, at], du_hbm.at[mine, at], out_sem.at[6 + 2 * j]),
        ]

    def mlp(j, carry):
        at = pl.ds(pl.multiple_of(j * width, width), width)
        at2 = pl.ds(pl.multiple_of(hidden + j * width, width), width)
        u = dot(h2_ref[...], w_ref[:, at]) + vec_ref[pl.ds(8 + j, 1), :]
        dg = dot_nt(dy_ref[...], w_ref[:, at2])
        sq = u * u
        th = jnp.tanh(c0 * (u + c1 * (u * sq)))
        half = 0.5 + 0.5 * th
        g = (u * half).astype(LOW)
        slope = half + (0.5 * u) * ((1.0 - th * th) * (c0 + (3.0 * c0 * c1) * sq))
        du = (slope * dg).astype(LOW)
        g_ref[:, at] = g
        du_ref[:, at] = du
        for copy in block_out(j):
            copy.start()
        sum_ref[pl.ds(8 + j, 1), :] = jnp.sum(du.astype(F32), axis=0, keepdims=True)
        acc_s[...] += dot(g, w_ref[:, at2])
        back_s[...] += dot_nt(du, w_ref[:, at])
        return carry

    lax.fori_loop(0, blocks, mlp, 0)
    out_ref[...] = acc_s[...].astype(LOW)
    store(out_ref, out_hbm.at[mine, :])
    dy = dy_ref[...].astype(F32)
    e = back_s[...]
    unit = unit_s[...]
    sum_ref[12:13, :] = jnp.sum(dy, axis=0, keepdims=True)
    sum_ref[1:2, :] = jnp.sum(e * unit, axis=0, keepdims=True)
    sum_ref[7:8, :] = jnp.sum(e, axis=0, keepdims=True)
    dmid = dy + norm_back(e, vec_ref[1:2, :], unit, scale)
    dmid_ref[...] = dmid
    store(dmid_ref, dmid_hbm.at[mine, :])
    dmb = dmid.astype(LOW)
    dmb_ref[...] = dmb
    store(dmb_ref, dmb_hbm.at[mine, :])
    sum_ref[6:7, :] = jnp.sum(dmb.astype(F32), axis=0, keepdims=True)
    back_s[...] = dot_nt(dmb, w_out[...])

    def back(s, carry):
        rows = pl.ds(pl.multiple_of(s * PAIR, PAIR), PAIR)
        odd = lane % 2 == 1
        across = jnp.where((sub < HD) != low, 1.0, 0.0).astype(LOW)
        across = jnp.concatenate([across, across], axis=0)
        for p in range(pairs):
            at = slice(p * PAIR, (p + 1) * PAIR)
            dctx = back_s[rows, at]
            dn = dctx * inv_s[rows, at]
            prod = dctx * ctx_s[rows, at]
            high = prod.astype(LOW)
            rest_prod = (prod - high.astype(F32)).astype(LOW)
            dd = -dot(jnp.concatenate([high, rest_prod], axis=1), across) * swap_s[rows, at]
            extra = jnp.where(odd, dd - dd.astype(LOW).astype(F32), dd)
            for which, own in ((0, low), (1, jnp.logical_not(low))):
                h = 2 * p + which
                aug = jnp.where(own, dn, jnp.where(edge_lanes(p, which), extra, 0.0))
                dn_ref[rows, h * PAIR : (h + 1) * PAIR] = aug.astype(LOW)
        dn_out(s).start()
        cols = jnp.zeros((PAIR, PAIR), F32)
        for p in range(pairs):
            got = []
            for which in range(2):
                h = 2 * p + which
                got.append(dot(pq_ref[s, h], dn_ref[rows, h * PAIR : (h + 1) * PAIR]))
                cols = jnp.where(edge_lanes(p, which), got[-1], cols)
            ds_ref[s, p * PAIR : (p + 1) * PAIR, :] = jnp.where(low, got[0], got[1]).astype(LOW)
        ds_ref[s, width : width + ZROWS, :] = dot_nt(head_lanes(False), cols.astype(LOW)).astype(LOW)
        return carry

    lax.fori_loop(0, seqs, back, 0)
    for copy in stores:
        copy.wait()
    for j in range(blocks):
        for copy in block_out(j):
            copy.wait()
    for s in range(seqs):
        dn_out(s).wait()


def leave_kernel(
    core_ref, qkv_ref, pq_ref, pk_ref, pa_ref, pb_ref, po_ref, la_ref, lb_ref, lo_ref, dn_ref, maps_ref, *rest
):
    dqkv_ref, gmap_ref, pri_s, dl_s, da_s, df_s, left_s, back_s = rest[-8:]
    width = qkv_ref.shape[1] // 3
    heads = pq_ref.shape[1]
    pairs = heads // 2
    step = pl.program_id(0)

    @pl.when(step == 0)
    def _():
        gmap_ref[...] = jnp.zeros_like(gmap_ref)

    compose(step, core_ref, (pa_ref, pb_ref, po_ref), pri_s, False)
    compose(step, core_ref, (la_ref, lb_ref, lo_ref), dl_s, True)
    lane, sub = lanes(), subs()
    low = lane < HD
    masks = [jnp.where(low, 1.0, 0.0).astype(LOW), jnp.where(low, 0.0, 1.0).astype(LOW)]
    zcol = dot_tn(pri_s[width : width + ZROWS, :], head_lanes(False)).astype(LOW)
    dzcol = dot_tn(dl_s[width : width + ZROWS, :], head_lanes(True)).astype(LOW)
    every = [(p, which, 2 * p + which) for p in range(pairs) for which in range(2)]
    column = lambda part, p: slice(part * width + p * PAIR, part * width + (p + 1) * PAIR)
    edge = lambda p, which: jnp.where(edge_lanes(p, which), 1.0, 0.0).astype(LOW)
    dn_of = lambda h: dn_ref[:, h * PAIR : (h + 1) * PAIR]
    for p, which, h in every:
        dn = dn_of(h)
        vaug = qkv_ref[:, column(2, p)] * masks[which] + edge(p, which)
        da_s[h, :, :PAIR] = jnp.where(sub >= lane, dot_nt(dn, vaug), 0.0).astype(LOW)
        da_s[h, :, PAIR:] = dn
        back_s[h, :, :PAIR] = jnp.where(sub <= lane, dot_nt(vaug, dn), 0.0).astype(LOW)
        back_s[h, :, PAIR:] = vaug
        keys = pk_ref[0, h].T
        left_s[h, :, :PAIR] = jnp.where(sub <= lane, dot(keys, pq_ref[0, h]), 0.0).astype(LOW)
        left_s[h, :, PAIR:] = keys
    for p, which, h in every:
        half = slice(which * HD, (which + 1) * HD)
        saug = pri_s[column(0, p), :] * masks[which] + zcol * edge(p, which)
        dpq = dot_nt(jnp.concatenate([pk_ref[0, h], saug], axis=1), da_s[h])
        df_s[0, p, half, :] = soft_back(pq_ref[0, h].astype(F32), dpq).astype(LOW)
    for p, which, h in every:
        half = slice(which * HD, (which + 1) * HD)
        laug = dl_s[column(0, p), :] * masks[which] + dzcol * edge(p, which)
        dpk = dot_nt(jnp.concatenate([pq_ref[0, h], laug], axis=1), back_s[h])
        df_s[1, p, half, :] = soft_back(pk_ref[0, h].astype(F32), dpk).astype(LOW)
    for p in range(pairs):
        dn = dn_of(2 * p) * masks[0] + dn_of(2 * p + 1) * masks[1]
        right = jnp.concatenate([dn, dl_s[column(0, p), :]], axis=0)
        left = jnp.concatenate([left_s[2 * p], left_s[2 * p + 1]], axis=0)
        both = dot(left, right)
        dqkv_ref[:, column(2, p)] = jnp.where(low, both[:PAIR], both[PAIR:]).astype(LOW)
    for part in range(2):
        for p in range(pairs):
            df = df_s[part, p]
            gmap_ref[part, p] += dot(df, qkv_ref[:, column(part, p)])
            dqkv_ref[:, column(part, p)] = dot(df.T, maps_ref[part, p]).astype(LOW)


def norm_kernel(x_ref, d_ref, w_ref, dmid_ref, vec_ref, dx_ref):
    e = dot_nt(d_ref[...], w_ref[...])
    unit, scale = normed(x_ref[...].astype(F32))
    dx_ref[...] = dmid_ref[...] + norm_back(e, vec_ref[0:1, :], unit, scale)


def put(value, core_ref, keep_ref, give_ref):
    count, rows, _ = keep_ref.shape
    value = value.reshape(count, 2, rows, value.shape[-1])
    even, odd = value[:, 0], value[:, 1]
    low = core_ref[0] == 0
    keep_ref[...] = jnp.where(low, even, odd).astype(LOW)
    give_ref[...] = jnp.where(low, odd, even).astype(LOW)


def weight_kernel(core_ref, h2_ref, du_ref, g_ref, dy_hbm, a_hbm, dmb_hbm, *rest):
    outs, (dy_ref, a_ref, dmb_ref, sem) = rest[:-4], rest[-4:]
    step = pl.program_id(0)
    pieces = ((dy_hbm, dy_ref), (a_hbm, a_ref), (dmb_hbm, dmb_ref))
    loads = [pltpu.make_async_copy(far, near, sem.at[k]) for k, (far, near) in enumerate(pieces)]

    @pl.when(step == 1)
    def _():
        for copy in loads:
            copy.start()

    @pl.when(step == (pl.num_programs(0) - 1) // 2)
    def _():
        for copy in loads:
            copy.wait()

    blocks = (pl.num_programs(0) - 1) // 2

    def write(value):
        if len(outs) == 1:
            outs[0][...] = value.astype(LOW)
        else:
            put(value, core_ref, *outs)

    @pl.when(step < blocks)
    def _():
        write(dot_tn(h2_ref[...], du_ref[...]))

    @pl.when(jnp.logical_and(step >= blocks, step < 2 * blocks))
    def _():
        write(dot_tn(g_ref[...], dy_ref[...]))

    @pl.when(step == 2 * blocks)
    def _():
        write(dot_tn(a_ref[...], dmb_ref[...]))


def first_kernel(core_ref, h_ref, d_ref, w_ref, g0_ref, g1_ref, row_ref, *rest):
    outs, (rows_s, gain_s, shift_s) = rest[:-3], rest[-3:]
    step = pl.program_id(0)
    last = pl.num_programs(0) - 1
    width = h_ref.shape[1]

    def write(value, start):
        at = pl.ds(start, value.shape[1])
        if len(outs) == 1:
            outs[0][:, at] = value.astype(LOW)
        else:
            put(value, core_ref, *(out.at[:, :, at] for out in outs))

    @pl.when(step == 0)
    def _():
        rows_s[...] = row_ref[...]
        gain_s[...] = jnp.zeros_like(gain_s)
        shift_s[...] = jnp.zeros_like(shift_s)

    at = pl.ds(pl.multiple_of(step * width, width), width)
    value = dot_tn(h_ref[...], d_ref[...])
    write(value, pl.multiple_of(step * width, width))
    w = w_ref[:, at].astype(F32)
    sums = jnp.sum(d_ref[...].astype(F32), axis=0, keepdims=True)
    rows_s[pl.ds(3 + step, 1), :] = sums
    gain_s[...] += jnp.sum(w * value, axis=1, keepdims=True)
    shift_s[...] += jnp.sum(w * sums, axis=1, keepdims=True)

    @pl.when(step == last)
    def _():
        lane, sub = lanes(), subs()
        fill = jnp.zeros((PAIR - ZROWS, PAIR), F32)
        blocks = []
        for p in range(g0_ref.shape[1]):
            at = slice(p * PAIR, (p + 1) * PAIR)
            q = (g0_ref[0, p] + g1_ref[0, p]).T
            k = (g0_ref[1, p] + g1_ref[1, p]).T
            upper = sub < HD
            q = jnp.where(upper, q, pltpu.roll(q, HD, 1))
            k = jnp.where(upper, pltpu.roll(k, HD, 1), k)
            cols = jnp.concatenate([rows_s[:, at], fill], axis=0).T
            own = w_ref[at, 3 * width + PAIR :].astype(F32)
            shift = shift_s[at]
            gain = (gain_s[at] - own[:, 2:3] * shift) / own[:, 0:1]
            cols = jnp.where(lane == 0, gain, jnp.where(lane == 2, shift, cols))
            blocks.append(jnp.concatenate([jnp.where(lane < HD, q, k), cols], axis=1))
        write(jnp.concatenate(blocks, axis=0), 3 * width)


def whole(shape):
    return pl.BlockSpec(shape, lambda i: (0,) * len(shape), pipeline_mode=pl.Buffered(1))


def part(shape, *at):
    return pl.BlockSpec(shape, lambda i: at, pipeline_mode=pl.Buffered(1))


PLAIN = pltpu.CompilerParams(vmem_limit_bytes=VMEM_BYTES)
PARAMS = dict(
    compiler_params=pltpu.CompilerParams(
        dimension_semantics=("arbitrary",), vmem_limit_bytes=VMEM_BYTES
    )
)


def params(size):
    return dict(
        compiler_params=pltpu.CompilerParams(
            dimension_semantics=("arbitrary",), vmem_limit_bytes=size * 1024 * 1024
        )
    )


def cost(flops, size):
    return pl.CostEstimate(flops=20 * int(flops), bytes_accessed=20 * int(size), transcendentals=0)


def enter(m, held, x, w, maps, vec, heads):
    total, width = x.shape
    rows = total // 2
    seqs = rows // PAIR
    pack = width + ZROWS
    extra = [] if held is None else [held]
    return pl.pallas_call(
        enter_kernel,
        grid=(seqs,),
        in_specs=[
            part((rows, width), m, 0),
            part((width, 3 * width), 0, 0),
            whole(maps.shape),
            whole(vec.shape),
        ]
        + [pl.BlockSpec(memory_space=pl.ANY)] * len(extra),
        out_specs=[
            pl.BlockSpec((PAIR, width), lambda i: (m * seqs + i, 0)),
            pl.BlockSpec((PAIR, 3 * width), lambda i: (i, 0)),
            pl.BlockSpec((1, heads, PAIR, PAIR), lambda i: (i, 0, 0, 0)),
            pl.BlockSpec((1, heads, PAIR, PAIR), lambda i: (i, 0, 0, 0)),
            pl.BlockSpec((1, pack, PAIR), lambda i: (i, 0, 0)),
        ],
        out_shape=[
            jax.ShapeDtypeStruct((total, width), LOW),
            jax.ShapeDtypeStruct((rows, 3 * width), LOW),
            jax.ShapeDtypeStruct((seqs, heads, PAIR, PAIR), LOW),
            jax.ShapeDtypeStruct((seqs, heads, PAIR, PAIR), LOW),
            jax.ShapeDtypeStruct((seqs, pack, PAIR), LOW),
        ],
        scratch_shapes=[pltpu.VMEM((rows, width), LOW), pltpu.VMEM((rows, 3 * width), LOW)],
        input_output_aliases={4 + k: k for k in range(len(extra))},
        cost_estimate=cost(6 * rows * width * width, 12 * rows * width),
        name="enter",
        **PARAMS,
    )(x, w, maps, vec, *extra)


def middle(m, held, core, x, dy, qkv, pq, pk, pri, w, vec, hidden):
    total, width = x.shape
    rows = total // 2
    seqs, heads = pq.shape[0], pq.shape[1]
    pack = width + ZROWS
    extra = [] if held is None else list(held)
    shared = [(width, LOW)] * 3 + [(hidden, LOW)] * 2 + [(width, F32), (width, LOW)]
    far = pl.BlockSpec(memory_space=pl.ANY)
    dn = jax.ShapeDtypeStruct((rows, heads * PAIR), LOW)
    ends = [
        jax.ShapeDtypeStruct((seqs, pack, PAIR), LOW),
        jax.ShapeDtypeStruct((ZROWS, width), F32),
    ]
    return pl.pallas_call(
        functools.partial(middle_kernel, m),
        grid=(1,),
        in_specs=[pl.BlockSpec(memory_space=pltpu.SMEM), far, far, part((rows, width), 0, 2), far, far]
        + [whole(piece.shape) for piece in pri]
        + [far, whole(vec.shape)]
        + [far] * len(extra),
        out_specs=[far] * (len(shared) + 1) + [whole(end.shape) for end in ends],
        out_shape=[jax.ShapeDtypeStruct((total, n), t) for n, t in shared] + [dn] + ends,
        scratch_shapes=[
            pltpu.VMEM((rows, width), LOW),
            pltpu.VMEM((rows, width), LOW),
            pltpu.VMEM(pq.shape, LOW),
            pltpu.VMEM(pk.shape, LOW),
            pltpu.VMEM(w.shape, LOW),
        ]
        + [pltpu.VMEM((rows, n), t) for n, t in shared]
        + [pltpu.VMEM(dn.shape, LOW)]
        + [pltpu.VMEM((rows, width), F32)] * 6
        + [
            pltpu.VMEM((pack, PAIR), LOW),
            pltpu.VMEM((heads, PAIR, 2 * PAIR), LOW),
            pltpu.SemaphoreType.DMA((3, seqs)),
            pltpu.SemaphoreType.DMA((4,)),
            pltpu.SemaphoreType.DMA((5 + 2 * (hidden // width),)),
        ],
        input_output_aliases={11 + k: k for k in range(len(extra))},
        cost_estimate=cost(8 * rows * width * hidden + 4 * rows * width * width, 30 * rows * width),
        name="middle",
        **PARAMS,
    )(core, x, dy, qkv, pq, pk, *pri, w, vec, *extra)


def leave(m, held, core, qkv, pq, pk, pri, dl, dn, maps):
    rows, wide = qkv.shape
    total = 2 * rows
    seqs, heads = pq.shape[:2]
    pack = pri[2].shape[1]
    each = lambda array: pl.BlockSpec((1,) + array.shape[1:], lambda i: (i,) + (0,) * (array.ndim - 1))
    state = lambda pieces: [whole(pieces[0].shape), whole(pieces[1].shape), each(pieces[2])]
    extra = [] if held is None else [held]
    return pl.pallas_call(
        leave_kernel,
        grid=(seqs,),
        in_specs=[
            pl.BlockSpec(memory_space=pltpu.SMEM),
            pl.BlockSpec((PAIR, wide), lambda i: (i, 0)),
            each(pq),
            each(pk),
        ]
        + state(pri)
        + state(dl)
        + [pl.BlockSpec((PAIR, dn.shape[1]), lambda i: (i, 0)), whole(maps.shape)]
        + [pl.BlockSpec(memory_space=pl.ANY)] * len(extra),
        out_specs=[pl.BlockSpec((PAIR, wide), lambda i: (m * seqs + i, 0)), whole(maps.shape)],
        out_shape=[
            jax.ShapeDtypeStruct((total, wide), LOW),
            jax.ShapeDtypeStruct(maps.shape, F32),
        ],
        scratch_shapes=[
            pltpu.VMEM((pack, PAIR), LOW),
            pltpu.VMEM((pack, PAIR), LOW),
            pltpu.VMEM((heads, PAIR, 2 * PAIR), LOW),
            pltpu.VMEM((2, heads // 2, PAIR, PAIR), LOW),
            pltpu.VMEM((heads, PAIR, 2 * PAIR), LOW),
            pltpu.VMEM((heads, PAIR, 2 * PAIR), LOW),
        ],
        input_output_aliases={12 + k: k for k in range(len(extra))},
        cost_estimate=cost(8 * rows * wide * PAIR, 8 * rows * wide),
        name="leave",
        **params(24 if m else 60),
    )(core, qkv, pq, pk, *pri, *dl, dn, maps, *extra)


def norm_grads(x, dqkv, w, dmid, vec):
    total, width = x.shape
    rows = min(total, 256)
    return pl.pallas_call(
        norm_kernel,
        grid=(total // rows,),
        in_specs=[
            pl.BlockSpec((rows, width), lambda i: (i, 0)),
            pl.BlockSpec((rows, 3 * width), lambda i: (i, 0)),
            part((width, 3 * width), 0, 0),
            pl.BlockSpec((rows, width), lambda i: (i, 0)),
            whole(vec.shape),
        ],
        out_specs=pl.BlockSpec((rows, width), lambda i: (i, 0)),
        out_shape=jax.ShapeDtypeStruct((total, width), F32),
        cost_estimate=cost(6 * total * width * width, 12 * total * width),
        name="norm",
        **params(24),
    )(x, dqkv, w, dmid, vec)


def prepare(core, mine, theirs, heads):
    count, rows, columns = mine.shape
    width = 2 * count * rows
    outs = [
        jax.ShapeDtypeStruct((2, heads // 2, PAIR, PAIR), LOW),
        jax.ShapeDtypeStruct((ZROWS, width), F32),
    ]
    if rows % 8 != 0:
        low = core[0] == 0
        both = [jnp.where(low, mine, theirs), jnp.where(low, theirs, mine)]
        w = jnp.stack(both, axis=1).reshape(width, columns)
        maps, vec = pl.pallas_call(
            tail_kernel, out_shape=outs, name="tail", compiler_params=PLAIN
        )(w[:, columns - 2 * PAIR :])
        return w, maps, vec
    w, maps, vec = pl.pallas_call(
        prepare_kernel,
        grid=(1,),
        in_specs=[
            pl.BlockSpec(memory_space=pltpu.SMEM),
            whole(mine.shape),
            whole(theirs.shape),
        ],
        out_specs=[
            whole((count, 2, rows, columns)),
            whole(outs[0].shape),
            whole(outs[1].shape),
        ],
        out_shape=[jax.ShapeDtypeStruct((count, 2, rows, columns), LOW)] + outs,
        name="prepare",
        **params(20),
    )(core, mine, theirs)
    return w.reshape(width, columns), maps, vec


def out_halves(width, rows, columns, size):
    if rows % 8 != 0:
        return (
            [pl.BlockSpec((width, size), lambda i: (0, i))],
            [jax.ShapeDtypeStruct((width, columns), LOW)],
        )
    count = width // rows // 2
    return (
        [pl.BlockSpec((count, rows, size), lambda i: (0, 0, i))] * 2,
        [jax.ShapeDtypeStruct((count, rows, columns), LOW)] * 2,
    )


def weight_grads(core, rows, h2, du, g, dy, a, dmb):
    total, width = h2.shape
    blocks = du.shape[1] // width
    last = 2 * blocks
    block = (total, width)
    specs, shapes = out_halves(width, rows, (last + 1) * width, width)
    return pl.pallas_call(
        weight_kernel,
        grid=(last + 1,),
        in_specs=[
            pl.BlockSpec(memory_space=pltpu.SMEM),
            pl.BlockSpec(block, lambda i: (0, 0)),
            pl.BlockSpec(block, lambda i: (0, jnp.minimum(i, blocks - 1))),
            pl.BlockSpec(block, lambda i: (0, jnp.clip(i - blocks, 0, blocks - 1))),
        ]
        + [pl.BlockSpec(memory_space=pl.ANY)] * 3,
        out_specs=specs,
        out_shape=shapes,
        scratch_shapes=[pltpu.VMEM(block, LOW)] * 3 + [pltpu.SemaphoreType.DMA((3,))],
        cost_estimate=cost(2 * total * width * width * (last + 1), 20 * total * width),
        name="weights",
        **PARAMS,
    )(core, h2, du, g, dy, a, dmb)


def first_grads(core, rows, hid, dqkv, w, gmaps, sums):
    total, width = hid.shape
    specs, shapes = out_halves(width, rows, w.shape[1], w.shape[1])
    specs = [whole(shape.shape) for shape in shapes]
    return pl.pallas_call(
        first_kernel,
        grid=(3,),
        in_specs=[
            pl.BlockSpec(memory_space=pltpu.SMEM),
            whole(hid.shape),
            pl.BlockSpec((total, width), lambda i: (0, i)),
            whole(w.shape),
            whole(gmaps[0].shape),
            whole(gmaps[1].shape),
            whole(sums.shape),
        ],
        out_specs=specs,
        out_shape=shapes,
        scratch_shapes=[
            pltpu.VMEM((ZROWS, width), F32),
            pltpu.VMEM((width, 1), F32),
            pltpu.VMEM((width, 1), F32),
        ],
        cost_estimate=cost(6 * total * width * width, 12 * total * width),
        name="first",
        **params(32),
    )(core, hid, dqkv, w, *gmaps, sums)


def shards(tokens, w_qkv, w_feat, w_out, w_fc, w_proj, gains, biases, cotangent):
    micro_count, seq_count, seg_len, width = tokens.shape
    grid = grid_dims()
    rows = w_qkv.shape[0]
    hidden = w_fc.shape[1]
    ratio = hidden // width
    heads = width // HD
    pairs = heads // 2
    wide = 3 * width
    total = micro_count * seq_count * seg_len

    first = jnp.concatenate(
        [
            w_qkv.astype(LOW),
            jnp.transpose(w_feat, (1, 0, 2)).reshape(rows, PAIR).astype(LOW),
            jnp.pad(jnp.concatenate([gains, biases]).T.astype(LOW), ((0, 0), (0, PAIR - 13))),
        ],
        axis=1,
    )
    core = jnp.reshape(grid[1]["c"], (1,))
    first, maps, vec = prepare(core, *gather_rows(first, grid), heads)
    later = jnp.concatenate(
        [
            w_fc.astype(LOW).reshape(rows, width, ratio).swapaxes(1, 2).reshape(rows, hidden),
            w_proj.astype(LOW).reshape(rows, hidden),
            w_out.astype(LOW),
        ],
        axis=1,
    )
    later = lax.all_gather(later, AXES, axis=0, tiled=True)
    fc_bias = vec[8 : 8 + ratio].reshape(width, ratio).T
    mid_vec = jnp.concatenate([vec[:8], fc_bias, vec[8 + ratio :]])
    x = tokens.reshape(total, width)
    dy = cotangent.reshape(total, width)

    entered, swaps, steps = [], [], []
    for m in range(2):
        held = entered[0][0] if m else None
        held_vec = tie(vec, swaps[0][0]) if m else vec
        entered.append(enter(m, held, x, first, maps, held_vec, heads))
        own = entered[m][4]
        if m:
            steps[0].round(entered[1][1])
            own = tie(own, steps[0].running)
        swaps.append(swap(own, grid))
        steps.append(Steps(swaps[m][0], grid, False))
    hid = entered[1][0]
    steps[1].round()
    ready = steps[1].running
    priors = [steps[m].end(swaps[m][1]) for m in range(2)]
    held, mids, swaps, steps = None, [], [], []
    for m in range(2):
        _, qkv, pq, pk, _ = entered[m]
        held_vec = tie(mid_vec, swaps[0][0] if m else ready)
        got = middle(m, held, core, x, dy, qkv, pq, pk, priors[m], later, held_vec, hidden)
        held, rest = got[:7], got[7:]
        mids.append(rest)
        own = rest[1]
        if m:
            steps[0].round(rest[2])
            own = tie(own, steps[0].running)
        swaps.append(swap(own, grid))
        steps.append(Steps(swaps[m][0], grid, True))
    out, a, h2, g, du, dmid, dmb = held
    g_later = weight_grads(tie(core, swaps[1][0]), rows, h2, du, g, dy, a, dmb)
    if len(g_later) == 1:
        g_later = halves(g_later[0], grid, rows)
    inner = mids[0][2] + mids[1][2]
    g_fc_bias = inner[8 : 8 + ratio].T.reshape(ratio, width)
    sums = jnp.concatenate([inner[:8], g_fc_bias, inner[8 + ratio :]])
    keep, give = g_later
    laters = [steps[0].end(swaps[0][1], give)]
    steps[1].round(give)
    _, qkv, pq, pk, _ = entered[0]
    kept, gmap = leave(0, None, core, qkv, pq, pk, priors[0], laters[0], mids[0][0], maps)
    gmaps = [gmap]
    scatter = Scatter(keep, tie(give, laters[0][0], steps[1].running), grid, gmap)
    laters.append(steps[1].end(swaps[1][1], gmap))
    _, qkv, pq, pk, _ = entered[1]
    held_core = tie(core, scatter.left, scatter.right)
    dqkv, gmap = leave(1, kept, held_core, qkv, pq, pk, priors[1], laters[1], mids[1][0], maps)
    gmaps.append(gmap)
    g_qkv = first_grads(core, rows, hid, dqkv, first, gmaps, sums)
    if len(g_qkv) == 1:
        g_qkv = halves(g_qkv[0], grid, rows)
    scatter.one(g_qkv[0])
    ending = Scatter(*g_qkv, grid, scatter.left)
    held_vec = tie(vec, ending.left, ending.right, scatter.right)
    dx = norm_grads(x, dqkv, first, dmid, held_vec)
    scatter.two(dx)
    ending.one(scatter.left)
    ending.two()
    r_later = scatter.end(ending.left)
    last = ending.end().astype(F32)
    r_fc = r_later[:, :hidden]
    r_proj = r_later[:, hidden : 2 * hidden]
    r_out = r_later[:, 2 * hidden :]
    small = last[:, wide + PAIR :].T
    return (
        out.reshape(tokens.shape),
        dx.reshape(tokens.shape),
        last[:, :wide],
        jnp.transpose(last[:, wide : wide + PAIR].reshape(rows, 2, HD), (1, 0, 2)),
        r_out.astype(F32),
        r_fc.astype(F32).reshape(rows, ratio, width).swapaxes(1, 2).reshape(rows, hidden),
        r_proj.astype(F32).reshape(rows * ratio, width),
        small[:2],
        small[2:13],
    )


def solution(mesh):
    return jax.shard_map(
        shards,
        mesh=mesh,
        in_specs=(
            P(None, "dp", "seq", None),
            P(("dp", "seq"), None),
            P(None, ("dp", "seq"), None),
            P(("dp", "seq"), None),
            P(("dp", "seq"), None),
            P(("dp", "seq"), None),
            P(None, ("dp", "seq")),
            P(None, ("dp", "seq")),
            P(None, "dp", "seq", None),
        ),
        out_specs=(
            P(None, "dp", "seq", None),
            P(None, "dp", "seq", None),
            P(("dp", "seq"), None),
            P(None, ("dp", "seq"), None),
            P(("dp", "seq"), None),
            P(("dp", "seq"), None),
            P(("dp", "seq"), None),
            P(None, ("dp", "seq")),
            P(None, ("dp", "seq")),
        ),
        check_vma=False,
    )
```

```python
import functools

import jax
import jax.numpy as jnp
from jax import lax
from jax.experimental import pallas as pl
from jax.experimental.pallas import tpu as pltpu
from jax.sharding import PartitionSpec as P

HD = 64
PAIR = 2 * HD
AXES = ("dp", "seq")
LOW = jnp.bfloat16
F32 = jnp.float32
VMEM_BYTES = 60 * 1024 * 1024
ZROWS = 16

def grid_dims():
    n_dp, n_seq = lax.axis_size("dp"), lax.axis_size("seq")
    n_x = 1
    while n_x * n_x * 4 <= n_dp:
        n_x *= 2
    sizes = {"y": n_dp // n_x, "x": n_x, "z": n_seq // 2, "c": 2}
    at = lax.axis_index("dp") * n_seq + lax.axis_index("seq")
    place = {}
    for name in ("c", "z", "x", "y"):
        place[name] = lax.rem(at, sizes[name])
        at = at // sizes[name]
    return sizes, place


def turned(sizes, name, step):
    pairs = []
    for y in range(sizes["y"]):
        for x in range(sizes["x"]):
            for z in range(sizes["z"]):
                for c in range(sizes["c"]):
                    to = {"y": y, "x": x, "z": z, "c": c}
                    to[name] = (to[name] + step) % sizes[name]
                    flat = lambda p: ((p[0] * sizes["x"] + p[1]) * sizes["z"] + p[2]) * 2 + p[3]
                    pairs.append((flat((y, x, z, c)), flat((to["y"], to["x"], to["z"], to["c"]))))
    return pairs


def send(value, sizes, name, step):
    return lax.ppermute(value, AXES, turned(sizes, name, step))


def tie(value, *others):
    others = [other for other in others if other is not None]
    return lax.optimization_barrier((value, *others))[0] if others else value


def spread(own, got, place):
    at = lax.broadcasted_iota(jnp.int32, (2,) + (1,) * own.ndim, 0)
    return jnp.where(at == place, own[None], got[None])


def gather_dim(value, grid, name):
    sizes, place = grid
    count = sizes[name]
    if count == 1:
        return value[None]
    got = [value] + [send(value, sizes, name, k) for k in range(1, count)]
    if count == 2:
        return spread(got[0], got[1], place[name])
    order = jnp.stack(got[::-1] + got[::-1][:-1])
    return lax.dynamic_slice_in_dim(order, count - 1 - place[name], count, 0)


def gather_rows(value, grid):
    sizes, _ = grid
    out = gather_dim(value, grid, "z")
    columns = value.shape[1] // 2
    left, right = out[..., :columns], out[..., columns:]
    left, right = gather_dim(left, grid, "x"), gather_dim(right, grid, "y")
    left, right = gather_dim(left, grid, "y"), gather_dim(right, grid, "x")
    out = jnp.concatenate([left, jnp.swapaxes(right, 0, 1)], axis=-1)
    out = out.reshape((-1,) + value.shape)
    return out, send(out, sizes, "c", 1)


def scatter_dim(value, grid, name, axis, after=None):
    sizes, place = grid
    count = sizes[name]
    mine = lax.dynamic_index_in_dim(value, place[name], axis, keepdims=False)
    if count == 1:
        return mine
    total = mine.astype(F32)
    for k in range(1, count):
        to = lax.rem(place[name] + k, count)
        block = lax.dynamic_index_in_dim(value, to, axis, keepdims=False)
        total = total + tie(send(block, sizes, name, k), after).astype(F32)
    return total.astype(LOW)


class Scatter:
    def __init__(self, keep, give, grid, after=None):
        sizes, _ = grid
        self.grid = grid
        got = tie(send(give, sizes, "c", 1), after)
        shape = (sizes["y"], sizes["x"], sizes["z"]) + keep.shape[1:]
        keep, got = keep.reshape(shape), got.reshape(shape)
        cut = keep.shape[-1] // 256 * 128
        add = lambda a, b: (a.astype(F32) + b.astype(F32)).astype(LOW)
        self.left = add(keep[..., :cut], got[..., :cut])
        self.right = add(keep[..., cut:], got[..., cut:])

    def one(self, after=None):
        self.left = scatter_dim(self.left, self.grid, "x", 1, after)
        self.right = scatter_dim(self.right, self.grid, "y", 0, after)

    def two(self, after=None):
        self.left = scatter_dim(self.left, self.grid, "y", 0, after)
        self.right = scatter_dim(self.right, self.grid, "x", 0, after)

    def end(self, after=None):
        both = jnp.concatenate([self.left, self.right], axis=-1)
        return scatter_dim(both, self.grid, "z", 0, after)


def halves(value, grid, rows):
    _, place = grid
    value = value.reshape(-1, 2, rows, value.shape[-1])
    pick = lambda at: lax.dynamic_index_in_dim(value, at, 1, keepdims=False)
    return pick(place["c"]), pick(1 - place["c"])


def some(sizes, step, chosen):
    pairs = []
    for a, b in turned(sizes, "z", step):
        z = (a // 2) % sizes["z"]
        if 0 <= z + step < sizes["z"] and chosen(z):
            pairs.append((a, b))
    return pairs


def swap(own, grid):
    sizes, place = grid
    half = own.shape[0] // 2
    other = send(own, sizes, "c", 1)
    first = place["c"] * half
    mine = lax.dynamic_slice_in_dim(own, first, half, 0).astype(F32)
    mine = (mine + lax.dynamic_slice_in_dim(other, first, half, 0).astype(F32)).astype(LOW)
    return mine, other


class Steps:
    def __init__(self, mine, grid, reverse):
        self.running, self.mine, self.total, self.span = mine, mine, 0.0, 1
        self.sizes, self.reverse = grid[0], reverse

    def round(self, after=None):
        count, span = self.sizes["z"], self.span
        if span >= count:
            return
        back = lambda z: count - 1 - z if self.reverse else z
        four = count == 4 and self.reverse
        if four and span == 1:
            sends = [(1, lambda z: True), (2, lambda z: back(z) == 0)]
        elif four:
            sends = [(1, lambda z: back(z) == 2)]
        else:
            sends = [(d, lambda z: back(z) % (2 * span) == span - 1) for d in range(1, span + 1)]
        got = 0.0
        for d, chosen in sends:
            pairs = some(self.sizes, -d if self.reverse else d, chosen)
            got = got + tie(lax.ppermute(self.running, AXES, pairs), after).astype(F32)
        self.total = self.total + got
        self.running = got.astype(LOW)
        if not four:
            self.running = (self.mine.astype(F32) + self.total).astype(LOW)
        self.span = 2 * span

    def end(self, other, after=None):
        while self.span < self.sizes["z"]:
            self.round(after)
        total = jnp.asarray(self.total + jnp.zeros(self.running.shape, F32)).astype(LOW)
        return total, send(total, self.sizes, "c", 1), other


def dot(a, b):
    return jnp.dot(a, b, preferred_element_type=F32)


def dot_nt(a, b):
    return lax.dot_general(a, b, (((1,), (1,)), ((), ())), preferred_element_type=F32)


def dot_tn(a, b):
    return lax.dot_general(a, b, (((0,), (0,)), ((), ())), preferred_element_type=F32)


def normed(values):
    centred = values - jnp.mean(values, axis=-1, keepdims=True)
    spread = jnp.mean(centred * centred, axis=-1, keepdims=True)
    scale = lax.rsqrt(spread + 1e-05)
    return centred * scale, scale


def norm_back(grad, gain, unit, scale):
    eg = grad * gain
    inner = eg - jnp.mean(eg, axis=-1, keepdims=True)
    return scale * (inner - unit * jnp.mean(eg * unit, axis=-1, keepdims=True))


def lanes(shape=(PAIR, PAIR)):
    return lax.broadcasted_iota(jnp.int32, shape, 1)


def subs(shape=(PAIR, PAIR)):
    return lax.broadcasted_iota(jnp.int32, shape, 0)


def head_lanes(first_only):
    lane, row = lanes((ZROWS, PAIR)), subs((ZROWS, PAIR))
    head = (lane % HD) // 2 * 2 + jnp.where(lane < HD, 1, 0)
    hit = head == row
    if first_only:
        hit = jnp.logical_and(hit, lane % 2 == 0)
    return jnp.where(hit, 1.0, 0.0).astype(LOW)


def edge_lanes(p, which):
    return lanes() // 2 == (p if which else HD // 2 + p)


def soft_pair(logits):
    high = jnp.max(logits, axis=0, keepdims=True)
    small = jnp.min(logits, axis=0, keepdims=True)
    e1 = jnp.exp(logits - high)
    e2 = jnp.exp(small - logits)
    p1 = e1 * (1.0 / jnp.sum(e1, axis=0, keepdims=True))
    p2 = e2 * (1.0 / jnp.sum(e2, axis=0, keepdims=True))
    return jnp.concatenate([p1, p2], axis=0)


def soft_back(phi, grad):
    prod = phi * grad
    s1 = jnp.sum(prod[:HD], axis=0, keepdims=True)
    s2 = jnp.sum(prod[HD:], axis=0, keepdims=True)
    return (prod[:HD] - phi[:HD] * s1) - (prod[HD:] - phi[HD:] * s2)


def prepare_kernel(core_ref, mine_ref, theirs_ref, w_ref, maps_ref, vec_ref):
    cut = w_ref.shape[-1] - 2 * PAIR

    def write(even_ref, odd_ref):
        w_ref[:, 0] = even_ref[...]
        w_ref[:, 1] = odd_ref[...]
        even = even_ref[:, :, cut:].astype(F32)[:, None]
        odd = odd_ref[:, :, cut:].astype(F32)[:, None]
        tail = jnp.concatenate([even, odd], axis=1)
        split_tail(tail.reshape(-1, 2 * PAIR), maps_ref, vec_ref)

    @pl.when(core_ref[0] == 0)
    def _():
        write(mine_ref, theirs_ref)

    @pl.when(core_ref[0] != 0)
    def _():
        write(theirs_ref, mine_ref)


def tail_kernel(tail_ref, maps_ref, vec_ref):
    split_tail(tail_ref[...].astype(F32), maps_ref, vec_ref)


def split_tail(tail, maps_ref, vec_ref):
    low = lanes((HD, PAIR)) < HD
    for p in range(maps_ref.shape[1]):
        at = slice(p * PAIR, (p + 1) * PAIR)
        both = tail[at, :PAIR].T
        for which in range(2):
            one = both[which * HD : (which + 1) * HD]
            block = [jnp.where(low, one, 0.0), jnp.where(low, 0.0, one)]
            maps_ref[which, p] = jnp.concatenate(block, axis=0).astype(LOW)
        vec_ref[:, at] = tail[at, PAIR:].T[:ZROWS]


def enter_kernel(x_ref, w_ref, maps_ref, vec_ref, *rest):
    hid_ref, qkv_ref, pq_ref, pk_ref, st_ref, hid_s, qkv_s = rest[-7:]
    width = x_ref.shape[1]
    pairs = pq_ref.shape[1] // 2
    step = pl.program_id(0)

    @pl.when(step == 0)
    def _():
        unit, _ = normed(x_ref[...].astype(F32))
        hid_s[...] = (unit * vec_ref[0:1, :] + vec_ref[2:3, :]).astype(LOW)
        for part in range(3):
            span = slice(part * width, (part + 1) * width)
            value = dot(hid_s[...], w_ref[:, span]) + vec_ref[3 + part : 4 + part, :]
            qkv_s[:, span] = value.astype(LOW)

    rows = pl.ds(pl.multiple_of(step * PAIR, PAIR), PAIR)
    hid_ref[...] = hid_s[rows, :]
    qkv_ref[...] = qkv_s[rows, :]
    low = lanes() < HD
    ones = jnp.ones((PAIR, PAIR), LOW)
    for which, ref in ((1, pk_ref), (0, pq_ref)):
        for p in range(pairs):
            at = slice(which * width + p * PAIR, which * width + (p + 1) * PAIR)
            logits = dot_nt(maps_ref[which, p], qkv_s[rows, at])
            ref[0, 2 * p] = soft_pair(logits[:HD]).astype(LOW)
            ref[0, 2 * p + 1] = soft_pair(logits[HD:]).astype(LOW)
    cols = jnp.zeros((PAIR, PAIR), F32)
    for p in range(pairs):
        at = slice(p * PAIR, (p + 1) * PAIR)
        value = qkv_s[rows, 2 * width + p * PAIR : 2 * width + (p + 1) * PAIR]
        own = []
        for which in range(2):
            both = dot(pk_ref[0, 2 * p + which], jnp.concatenate([value, ones], axis=1))
            own.append(both[:, :PAIR])
            cols = jnp.where(edge_lanes(p, which), both[:, PAIR:], cols)
        st_ref[0, at, :] = jnp.where(low, own[0], own[1]).astype(LOW)
    st_ref[0, width : width + ZROWS, :] = dot_nt(head_lanes(True), cols.astype(LOW)).astype(LOW)


def compose(s, core_ref, refs, out_ref, reverse):
    mine_ref, theirs_ref, other_ref = refs
    half = mine_ref.shape[0]
    at = lax.rem(s, half)
    core = core_ref[0]

    @pl.when(s // half == core)
    def _():
        out_ref[...] = mine_ref[at]

    @pl.when(s // half != core)
    def _():
        out_ref[...] = theirs_ref[at]

    @pl.when(core == (0 if reverse else 1))
    def _():
        own = other_ref[0 if other_ref.shape[0] == 1 else s]
        out_ref[...] = (out_ref[...].astype(F32) + own.astype(F32)).astype(LOW)


def middle_kernel(
    place, core_ref, x_hbm, dy_hbm, v_ref, pq_hbm, pk_hbm, pa_ref, pb_ref, po_ref, w_hbm, vec_ref, *rest
):
    (out_hbm, a_hbm, h2_hbm, g_hbm, du_hbm, dmid_hbm, dmb_hbm, dn_hbm, ds_ref, sum_ref,
     x_ref, dy_ref, pq_ref, pk_ref, w_ref, out_ref, a_ref, h2_ref, g_ref, du_ref, dmid_ref, dmb_ref, dn_ref,
     ctx_s, inv_s, swap_s, unit_s, acc_s, back_s, pri_s, left_s, seq_sem, in_sem, out_sem) = rest[-34:]
    rows_all, width = x_ref.shape
    seqs, heads = pq_ref.shape[0], pq_ref.shape[1]
    pairs = heads // 2
    hidden = g_ref.shape[1]
    blocks = hidden // width
    mine = pl.ds(place * rows_all, rows_all)
    lane, sub = lanes(), subs()
    low = lane < HD

    def features(s):
        return [
            pltpu.make_async_copy(pq_hbm.at[s], pq_ref.at[s], seq_sem.at[0, s]),
            pltpu.make_async_copy(pk_hbm.at[s], pk_ref.at[s], seq_sem.at[1, s]),
        ]

    def dn_out(s):
        rows = pl.ds(pl.multiple_of(s * PAIR, PAIR), PAIR)
        return pltpu.make_async_copy(dn_ref.at[rows, :], dn_hbm.at[rows, :], seq_sem.at[2, s])

    for s in range(seqs):
        for copy in features(s):
            copy.start()
    tail = pl.ds(2 * hidden, width)
    loads = [
        pltpu.make_async_copy(w_hbm.at[:, tail], w_ref.at[:, tail], in_sem.at[0]),
        pltpu.make_async_copy(x_hbm.at[mine, :], x_ref, in_sem.at[1]),
        pltpu.make_async_copy(dy_hbm.at[mine, :], dy_ref, in_sem.at[2]),
        pltpu.make_async_copy(
            w_hbm.at[:, pl.ds(0, 2 * hidden)], w_ref.at[:, pl.ds(0, 2 * hidden)], in_sem.at[3]
        ),
    ]
    for copy in loads:
        copy.start()
    stores = []

    def store(have, there):
        copy = pltpu.make_async_copy(have, there, out_sem.at[len(stores)])
        copy.start()
        stores.append(copy)

    sum_ref[...] = jnp.zeros_like(sum_ref)

    def attend(s, carry):
        for copy in features(s):
            copy.wait()
        compose(s, core_ref, (pa_ref, pb_ref, po_ref), pri_s, False)
        rows = pl.ds(pl.multiple_of(s * PAIR, PAIR), PAIR)
        zsum = pri_s[width : width + ZROWS, :].astype(F32)
        invs = []
        for h in range(heads):
            phi = pq_ref[s, h].T
            score = jnp.where(sub >= lane, dot(phi, pk_ref[s, h]), 0.0).astype(LOW)
            left_s[h, :, :PAIR] = score
            left_s[h, :, PAIR:] = phi
            each = score.astype(F32) + phi.astype(F32) * zsum[h : h + 1, :]
            invs.append(1.0 / jnp.sum(each, axis=1, keepdims=True))
        for p in range(pairs):
            at = slice(p * PAIR, (p + 1) * PAIR)
            inv = jnp.where(low, invs[2 * p], invs[2 * p + 1])
            inv_s[rows, at] = inv
            swap_s[rows, at] = jnp.where(low, invs[2 * p + 1], invs[2 * p])
            right = jnp.concatenate([v_ref[rows, at], pri_s[at, :]], axis=0)
            left = jnp.concatenate([left_s[2 * p], left_s[2 * p + 1]], axis=0)
            both = dot(left, right)
            ctx = jnp.where(low, both[:PAIR], both[PAIR:]) * inv
            ctx_s[rows, at] = ctx
            a_ref[rows, at] = ctx.astype(LOW)
        return carry

    lax.fori_loop(0, seqs, attend, 0)
    store(a_ref, a_hbm.at[mine, :])
    w_out = w_ref.at[:, tail]
    loads[0].wait()
    loads[1].wait()
    mid = x_ref[...].astype(F32) + dot(a_ref[...], w_out[...]) + vec_ref[6:7, :]
    acc_s[...] = mid + vec_ref[12:13, :]
    unit, scale = normed(mid)
    unit_s[...] = unit
    h2_ref[...] = (unit * vec_ref[1:2, :] + vec_ref[7:8, :]).astype(LOW)
    store(h2_ref, h2_hbm.at[mine, :])
    back_s[...] = jnp.zeros_like(back_s)
    c0 = 0.7978845608028654
    c1 = 0.044715
    loads[2].wait()
    loads[3].wait()

    def block_out(j):
        at = pl.ds(pl.multiple_of(j * width, width), width)
        return [
            pltpu.make_async_copy(g_ref.at[:, at], g_hbm.at[mine, at], out_sem.at[5 + 2 * j]),
            pltpu.make_async_copy(du_ref.at[:, at], du_hbm.at[mine, at], out_sem.at[6 + 2 * j]),
        ]

    def mlp(j, carry):
        at = pl.ds(pl.multiple_of(j * width, width), width)
        at2 = pl.ds(pl.multiple_of(hidden + j * width, width), width)
        u = dot(h2_ref[...], w_ref[:, at]) + vec_ref[pl.ds(8 + j, 1), :]
        dg = dot_nt(dy_ref[...], w_ref[:, at2])
        sq = u * u
        th = jnp.tanh(c0 * (u + c1 * (u * sq)))
        half = 0.5 + 0.5 * th
        g = (u * half).astype(LOW)
        slope = half + (0.5 * u) * ((1.0 - th * th) * (c0 + (3.0 * c0 * c1) * sq))
        du = (slope * dg).astype(LOW)
        g_ref[:, at] = g
        du_ref[:, at] = du
        for copy in block_out(j):
            copy.start()
        sum_ref[pl.ds(8 + j, 1), :] = jnp.sum(du.astype(F32), axis=0, keepdims=True)
        acc_s[...] += dot(g, w_ref[:, at2])
        back_s[...] += dot_nt(du, w_ref[:, at])
        return carry

    lax.fori_loop(0, blocks, mlp, 0)
    out_ref[...] = acc_s[...].astype(LOW)
    store(out_ref, out_hbm.at[mine, :])
    dy = dy_ref[...].astype(F32)
    e = back_s[...]
    unit = unit_s[...]
    sum_ref[12:13, :] = jnp.sum(dy, axis=0, keepdims=True)
    sum_ref[1:2, :] = jnp.sum(e * unit, axis=0, keepdims=True)
    sum_ref[7:8, :] = jnp.sum(e, axis=0, keepdims=True)
    dmid = dy + norm_back(e, vec_ref[1:2, :], unit, scale)
    dmid_ref[...] = dmid
    store(dmid_ref, dmid_hbm.at[mine, :])
    dmb = dmid.astype(LOW)
    dmb_ref[...] = dmb
    store(dmb_ref, dmb_hbm.at[mine, :])
    sum_ref[6:7, :] = jnp.sum(dmb.astype(F32), axis=0, keepdims=True)
    back_s[...] = dot_nt(dmb, w_out[...])

    def back(s, carry):
        rows = pl.ds(pl.multiple_of(s * PAIR, PAIR), PAIR)
        odd = lane % 2 == 1
        across = jnp.where((sub < HD) != low, 1.0, 0.0).astype(LOW)
        across = jnp.concatenate([across, across], axis=0)
        for p in range(pairs):
            at = slice(p * PAIR, (p + 1) * PAIR)
            dctx = back_s[rows, at]
            dn = dctx * inv_s[rows, at]
            prod = dctx * ctx_s[rows, at]
            high = prod.astype(LOW)
            rest_prod = (prod - high.astype(F32)).astype(LOW)
            dd = -dot(jnp.concatenate([high, rest_prod], axis=1), across) * swap_s[rows, at]
            extra = jnp.where(odd, dd - dd.astype(LOW).astype(F32), dd)
            for which, own in ((0, low), (1, jnp.logical_not(low))):
                h = 2 * p + which
                aug = jnp.where(own, dn, jnp.where(edge_lanes(p, which), extra, 0.0))
                dn_ref[rows, h * PAIR : (h + 1) * PAIR] = aug.astype(LOW)
        dn_out(s).start()
        cols = jnp.zeros((PAIR, PAIR), F32)
        for p in range(pairs):
            got = []
            for which in range(2):
                h = 2 * p + which
                got.append(dot(pq_ref[s, h], dn_ref[rows, h * PAIR : (h + 1) * PAIR]))
                cols = jnp.where(edge_lanes(p, which), got[-1], cols)
            ds_ref[s, p * PAIR : (p + 1) * PAIR, :] = jnp.where(low, got[0], got[1]).astype(LOW)
        ds_ref[s, width : width + ZROWS, :] = dot_nt(head_lanes(False), cols.astype(LOW)).astype(LOW)
        return carry

    lax.fori_loop(0, seqs, back, 0)
    for copy in stores:
        copy.wait()
    for j in range(blocks):
        for copy in block_out(j):
            copy.wait()
    for s in range(seqs):
        dn_out(s).wait()


def leave_kernel(
    core_ref, qkv_ref, pq_ref, pk_ref, pa_ref, pb_ref, po_ref, la_ref, lb_ref, lo_ref, dn_ref, maps_ref, *rest
):
    dqkv_ref, gmap_ref, pri_s, dl_s, da_s, df_s, left_s, back_s = rest[-8:]
    width = qkv_ref.shape[1] // 3
    heads = pq_ref.shape[1]
    pairs = heads // 2
    step = pl.program_id(0)

    @pl.when(step == 0)
    def _():
        gmap_ref[...] = jnp.zeros_like(gmap_ref)

    compose(step, core_ref, (pa_ref, pb_ref, po_ref), pri_s, False)
    compose(step, core_ref, (la_ref, lb_ref, lo_ref), dl_s, True)
    lane, sub = lanes(), subs()
    low = lane < HD
    masks = [jnp.where(low, 1.0, 0.0).astype(LOW), jnp.where(low, 0.0, 1.0).astype(LOW)]
    zcol = dot_tn(pri_s[width : width + ZROWS, :], head_lanes(False)).astype(LOW)
    dzcol = dot_tn(dl_s[width : width + ZROWS, :], head_lanes(True)).astype(LOW)
    every = [(p, which, 2 * p + which) for p in range(pairs) for which in range(2)]
    column = lambda part, p: slice(part * width + p * PAIR, part * width + (p + 1) * PAIR)
    edge = lambda p, which: jnp.where(edge_lanes(p, which), 1.0, 0.0).astype(LOW)
    dn_of = lambda h: dn_ref[:, h * PAIR : (h + 1) * PAIR]
    for p, which, h in every:
        dn = dn_of(h)
        vaug = qkv_ref[:, column(2, p)] * masks[which] + edge(p, which)
        da_s[h, :, :PAIR] = jnp.where(sub >= lane, dot_nt(dn, vaug), 0.0).astype(LOW)
        da_s[h, :, PAIR:] = dn
        back_s[h, :, :PAIR] = jnp.where(sub <= lane, dot_nt(vaug, dn), 0.0).astype(LOW)
        back_s[h, :, PAIR:] = vaug
        keys = pk_ref[0, h].T
        left_s[h, :, :PAIR] = jnp.where(sub <= lane, dot(keys, pq_ref[0, h]), 0.0).astype(LOW)
        left_s[h, :, PAIR:] = keys
    for p, which, h in every:
        half = slice(which * HD, (which + 1) * HD)
        saug = pri_s[column(0, p), :] * masks[which] + zcol * edge(p, which)
        dpq = dot_nt(jnp.concatenate([pk_ref[0, h], saug], axis=1), da_s[h])
        df_s[0, p, half, :] = soft_back(pq_ref[0, h].astype(F32), dpq).astype(LOW)
    for p, which, h in every:
        half = slice(which * HD, (which + 1) * HD)
        laug = dl_s[column(0, p), :] * masks[which] + dzcol * edge(p, which)
        dpk = dot_nt(jnp.concatenate([pq_ref[0, h], laug], axis=1), back_s[h])
        df_s[1, p, half, :] = soft_back(pk_ref[0, h].astype(F32), dpk).astype(LOW)
    for p in range(pairs):
        dn = dn_of(2 * p) * masks[0] + dn_of(2 * p + 1) * masks[1]
        right = jnp.concatenate([dn, dl_s[column(0, p), :]], axis=0)
        left = jnp.concatenate([left_s[2 * p], left_s[2 * p + 1]], axis=0)
        both = dot(left, right)
        dqkv_ref[:, column(2, p)] = jnp.where(low, both[:PAIR], both[PAIR:]).astype(LOW)
    for part in range(2):
        for p in range(pairs):
            df = df_s[part, p]
            gmap_ref[part, p] += dot(df, qkv_ref[:, column(part, p)])
            dqkv_ref[:, column(part, p)] = dot(df.T, maps_ref[part, p]).astype(LOW)


def norm_kernel(x_ref, d_ref, w_ref, dmid_ref, vec_ref, dx_ref):
    e = dot_nt(d_ref[...], w_ref[...])
    unit, scale = normed(x_ref[...].astype(F32))
    dx_ref[...] = dmid_ref[...] + norm_back(e, vec_ref[0:1, :], unit, scale)


def put(value, core_ref, keep_ref, give_ref):
    count, rows, _ = keep_ref.shape
    value = value.reshape(count, 2, rows, value.shape[-1])
    even, odd = value[:, 0], value[:, 1]
    low = core_ref[0] == 0
    keep_ref[...] = jnp.where(low, even, odd).astype(LOW)
    give_ref[...] = jnp.where(low, odd, even).astype(LOW)


def weight_kernel(core_ref, h2_ref, du_ref, g_ref, dy_hbm, a_hbm, dmb_hbm, *rest):
    outs, (dy_ref, a_ref, dmb_ref, sem) = rest[:-4], rest[-4:]
    step = pl.program_id(0)
    pieces = ((dy_hbm, dy_ref), (a_hbm, a_ref), (dmb_hbm, dmb_ref))
    loads = [pltpu.make_async_copy(far, near, sem.at[k]) for k, (far, near) in enumerate(pieces)]

    @pl.when(step == 1)
    def _():
        for copy in loads:
            copy.start()

    @pl.when(step == (pl.num_programs(0) - 1) // 2)
    def _():
        for copy in loads:
            copy.wait()

    blocks = (pl.num_programs(0) - 1) // 2

    def write(value):
        if len(outs) == 1:
            outs[0][...] = value.astype(LOW)
        else:
            put(value, core_ref, *outs)

    @pl.when(step < blocks)
    def _():
        write(dot_tn(h2_ref[...], du_ref[...]))

    @pl.when(jnp.logical_and(step >= blocks, step < 2 * blocks))
    def _():
        write(dot_tn(g_ref[...], dy_ref[...]))

    @pl.when(step == 2 * blocks)
    def _():
        write(dot_tn(a_ref[...], dmb_ref[...]))


def first_kernel(core_ref, h_ref, d_ref, w_ref, g0_ref, g1_ref, row_ref, *rest):
    outs, (rows_s, gain_s, shift_s) = rest[:-3], rest[-3:]
    step = pl.program_id(0)
    last = pl.num_programs(0) - 1
    width = h_ref.shape[1]

    def write(value, start):
        at = pl.ds(start, value.shape[1])
        if len(outs) == 1:
            outs[0][:, at] = value.astype(LOW)
        else:
            put(value, core_ref, *(out.at[:, :, at] for out in outs))

    @pl.when(step == 0)
    def _():
        rows_s[...] = row_ref[...]
        gain_s[...] = jnp.zeros_like(gain_s)
        shift_s[...] = jnp.zeros_like(shift_s)

    at = pl.ds(pl.multiple_of(step * width, width), width)
    value = dot_tn(h_ref[...], d_ref[...])
    write(value, pl.multiple_of(step * width, width))
    w = w_ref[:, at].astype(F32)
    sums = jnp.sum(d_ref[...].astype(F32), axis=0, keepdims=True)
    rows_s[pl.ds(3 + step, 1), :] = sums
    gain_s[...] += jnp.sum(w * value, axis=1, keepdims=True)
    shift_s[...] += jnp.sum(w * sums, axis=1, keepdims=True)

    @pl.when(step == last)
    def _():
        lane, sub = lanes(), subs()
        fill = jnp.zeros((PAIR - ZROWS, PAIR), F32)
        blocks = []
        for p in range(g0_ref.shape[1]):
            at = slice(p * PAIR, (p + 1) * PAIR)
            q = (g0_ref[0, p] + g1_ref[0, p]).T
            k = (g0_ref[1, p] + g1_ref[1, p]).T
            upper = sub < HD
            q = jnp.where(upper, q, pltpu.roll(q, HD, 1))
            k = jnp.where(upper, pltpu.roll(k, HD, 1), k)
            cols = jnp.concatenate([rows_s[:, at], fill], axis=0).T
            own = w_ref[at, 3 * width + PAIR :].astype(F32)
            shift = shift_s[at]
            gain = (gain_s[at] - own[:, 2:3] * shift) / own[:, 0:1]
            cols = jnp.where(lane == 0, gain, jnp.where(lane == 2, shift, cols))
            blocks.append(jnp.concatenate([jnp.where(lane < HD, q, k), cols], axis=1))
        write(jnp.concatenate(blocks, axis=0), 3 * width)


def whole(shape):
    return pl.BlockSpec(shape, lambda i: (0,) * len(shape), pipeline_mode=pl.Buffered(1))


def part(shape, *at):
    return pl.BlockSpec(shape, lambda i: at, pipeline_mode=pl.Buffered(1))


PLAIN = pltpu.CompilerParams(vmem_limit_bytes=VMEM_BYTES)
PARAMS = dict(
    compiler_params=pltpu.CompilerParams(
        dimension_semantics=("arbitrary",), vmem_limit_bytes=VMEM_BYTES
    )
)


def params(size):
    return dict(
        compiler_params=pltpu.CompilerParams(
            dimension_semantics=("arbitrary",), vmem_limit_bytes=size * 1024 * 1024
        )
    )


def cost(flops, size):
    return pl.CostEstimate(flops=20 * int(flops), bytes_accessed=20 * int(size), transcendentals=0)


def enter(m, held, x, w, maps, vec, heads):
    total, width = x.shape
    rows = total // 2
    seqs = rows // PAIR
    pack = width + ZROWS
    extra = [] if held is None else [held]
    return pl.pallas_call(
        enter_kernel,
        grid=(seqs,),
        in_specs=[
            part((rows, width), m, 0),
            part((width, 3 * width), 0, 0),
            whole(maps.shape),
            whole(vec.shape),
        ]
        + [pl.BlockSpec(memory_space=pl.ANY)] * len(extra),
        out_specs=[
            pl.BlockSpec((PAIR, width), lambda i: (m * seqs + i, 0)),
            pl.BlockSpec((PAIR, 3 * width), lambda i: (i, 0)),
            pl.BlockSpec((1, heads, PAIR, PAIR), lambda i: (i, 0, 0, 0)),
            pl.BlockSpec((1, heads, PAIR, PAIR), lambda i: (i, 0, 0, 0)),
            pl.BlockSpec((1, pack, PAIR), lambda i: (i, 0, 0)),
        ],
        out_shape=[
            jax.ShapeDtypeStruct((total, width), LOW),
            jax.ShapeDtypeStruct((rows, 3 * width), LOW),
            jax.ShapeDtypeStruct((seqs, heads, PAIR, PAIR), LOW),
            jax.ShapeDtypeStruct((seqs, heads, PAIR, PAIR), LOW),
            jax.ShapeDtypeStruct((seqs, pack, PAIR), LOW),
        ],
        scratch_shapes=[pltpu.VMEM((rows, width), LOW), pltpu.VMEM((rows, 3 * width), LOW)],
        input_output_aliases={4 + k: k for k in range(len(extra))},
        cost_estimate=cost(6 * rows * width * width, 12 * rows * width),
        name="enter",
        **PARAMS,
    )(x, w, maps, vec, *extra)


def middle(m, held, core, x, dy, qkv, pq, pk, pri, w, vec, hidden):
    total, width = x.shape
    rows = total // 2
    seqs, heads = pq.shape[0], pq.shape[1]
    pack = width + ZROWS
    extra = [] if held is None else list(held)
    shared = [(width, LOW)] * 3 + [(hidden, LOW)] * 2 + [(width, F32), (width, LOW)]
    far = pl.BlockSpec(memory_space=pl.ANY)
    dn = jax.ShapeDtypeStruct((rows, heads * PAIR), LOW)
    ends = [
        jax.ShapeDtypeStruct((seqs, pack, PAIR), LOW),
        jax.ShapeDtypeStruct((ZROWS, width), F32),
    ]
    return pl.pallas_call(
        functools.partial(middle_kernel, m),
        grid=(1,),
        in_specs=[pl.BlockSpec(memory_space=pltpu.SMEM), far, far, part((rows, width), 0, 2), far, far]
        + [whole(piece.shape) for piece in pri]
        + [far, whole(vec.shape)]
        + [far] * len(extra),
        out_specs=[far] * (len(shared) + 1) + [whole(end.shape) for end in ends],
        out_shape=[jax.ShapeDtypeStruct((total, n), t) for n, t in shared] + [dn] + ends,
        scratch_shapes=[
            pltpu.VMEM((rows, width), LOW),
            pltpu.VMEM((rows, width), LOW),
            pltpu.VMEM(pq.shape, LOW),
            pltpu.VMEM(pk.shape, LOW),
            pltpu.VMEM(w.shape, LOW),
        ]
        + [pltpu.VMEM((rows, n), t) for n, t in shared]
        + [pltpu.VMEM(dn.shape, LOW)]
        + [pltpu.VMEM((rows, width), F32)] * 6
        + [
            pltpu.VMEM((pack, PAIR), LOW),
            pltpu.VMEM((heads, PAIR, 2 * PAIR), LOW),
            pltpu.SemaphoreType.DMA((3, seqs)),
            pltpu.SemaphoreType.DMA((4,)),
            pltpu.SemaphoreType.DMA((5 + 2 * (hidden // width),)),
        ],
        input_output_aliases={11 + k: k for k in range(len(extra))},
        cost_estimate=cost(8 * rows * width * hidden + 4 * rows * width * width, 30 * rows * width),
        name="middle",
        **PARAMS,
    )(core, x, dy, qkv, pq, pk, *pri, w, vec, *extra)


def leave(m, held, core, qkv, pq, pk, pri, dl, dn, maps):
    rows, wide = qkv.shape
    total = 2 * rows
    seqs, heads = pq.shape[:2]
    pack = pri[2].shape[1]
    each = lambda array: pl.BlockSpec((1,) + array.shape[1:], lambda i: (i,) + (0,) * (array.ndim - 1))
    state = lambda pieces: [whole(pieces[0].shape), whole(pieces[1].shape), each(pieces[2])]
    extra = [] if held is None else [held]
    return pl.pallas_call(
        leave_kernel,
        grid=(seqs,),
        in_specs=[
            pl.BlockSpec(memory_space=pltpu.SMEM),
            pl.BlockSpec((PAIR, wide), lambda i: (i, 0)),
            each(pq),
            each(pk),
        ]
        + state(pri)
        + state(dl)
        + [pl.BlockSpec((PAIR, dn.shape[1]), lambda i: (i, 0)), whole(maps.shape)]
        + [pl.BlockSpec(memory_space=pl.ANY)] * len(extra),
        out_specs=[pl.BlockSpec((PAIR, wide), lambda i: (m * seqs + i, 0)), whole(maps.shape)],
        out_shape=[
            jax.ShapeDtypeStruct((total, wide), LOW),
            jax.ShapeDtypeStruct(maps.shape, F32),
        ],
        scratch_shapes=[
            pltpu.VMEM((pack, PAIR), LOW),
            pltpu.VMEM((pack, PAIR), LOW),
            pltpu.VMEM((heads, PAIR, 2 * PAIR), LOW),
            pltpu.VMEM((2, heads // 2, PAIR, PAIR), LOW),
            pltpu.VMEM((heads, PAIR, 2 * PAIR), LOW),
            pltpu.VMEM((heads, PAIR, 2 * PAIR), LOW),
        ],
        input_output_aliases={12 + k: k for k in range(len(extra))},
        cost_estimate=cost(8 * rows * wide * PAIR, 8 * rows * wide),
        name="leave",
        **params(24 if m else 60),
    )(core, qkv, pq, pk, *pri, *dl, dn, maps, *extra)


def norm_grads(x, dqkv, w, dmid, vec):
    total, width = x.shape
    rows = min(total, 256)
    return pl.pallas_call(
        norm_kernel,
        grid=(total // rows,),
        in_specs=[
            pl.BlockSpec((rows, width), lambda i: (i, 0)),
            pl.BlockSpec((rows, 3 * width), lambda i: (i, 0)),
            part((width, 3 * width), 0, 0),
            pl.BlockSpec((rows, width), lambda i: (i, 0)),
            whole(vec.shape),
        ],
        out_specs=pl.BlockSpec((rows, width), lambda i: (i, 0)),
        out_shape=jax.ShapeDtypeStruct((total, width), F32),
        cost_estimate=cost(6 * total * width * width, 12 * total * width),
        name="norm",
        **params(24),
    )(x, dqkv, w, dmid, vec)


def prepare(core, mine, theirs, heads):
    count, rows, columns = mine.shape
    width = 2 * count * rows
    outs = [
        jax.ShapeDtypeStruct((2, heads // 2, PAIR, PAIR), LOW),
        jax.ShapeDtypeStruct((ZROWS, width), F32),
    ]
    if rows % 8 != 0:
        low = core[0] == 0
        both = [jnp.where(low, mine, theirs), jnp.where(low, theirs, mine)]
        w = jnp.stack(both, axis=1).reshape(width, columns)
        maps, vec = pl.pallas_call(
            tail_kernel, out_shape=outs, name="tail", compiler_params=PLAIN
        )(w[:, columns - 2 * PAIR :])
        return w, maps, vec
    w, maps, vec = pl.pallas_call(
        prepare_kernel,
        grid=(1,),
        in_specs=[
            pl.BlockSpec(memory_space=pltpu.SMEM),
            whole(mine.shape),
            whole(theirs.shape),
        ],
        out_specs=[
            whole((count, 2, rows, columns)),
            whole(outs[0].shape),
            whole(outs[1].shape),
        ],
        out_shape=[jax.ShapeDtypeStruct((count, 2, rows, columns), LOW)] + outs,
        name="prepare",
        **params(20),
    )(core, mine, theirs)
    return w.reshape(width, columns), maps, vec


def out_halves(width, rows, columns, size):
    if rows % 8 != 0:
        return (
            [pl.BlockSpec((width, size), lambda i: (0, i))],
            [jax.ShapeDtypeStruct((width, columns), LOW)],
        )
    count = width // rows // 2
    return (
        [pl.BlockSpec((count, rows, size), lambda i: (0, 0, i))] * 2,
        [jax.ShapeDtypeStruct((count, rows, columns), LOW)] * 2,
    )


def weight_grads(core, rows, h2, du, g, dy, a, dmb):
    total, width = h2.shape
    blocks = du.shape[1] // width
    last = 2 * blocks
    block = (total, width)
    specs, shapes = out_halves(width, rows, (last + 1) * width, width)
    return pl.pallas_call(
        weight_kernel,
        grid=(last + 1,),
        in_specs=[
            pl.BlockSpec(memory_space=pltpu.SMEM),
            pl.BlockSpec(block, lambda i: (0, 0)),
            pl.BlockSpec(block, lambda i: (0, jnp.minimum(i, blocks - 1))),
            pl.BlockSpec(block, lambda i: (0, jnp.clip(i - blocks, 0, blocks - 1))),
        ]
        + [pl.BlockSpec(memory_space=pl.ANY)] * 3,
        out_specs=specs,
        out_shape=shapes,
        scratch_shapes=[pltpu.VMEM(block, LOW)] * 3 + [pltpu.SemaphoreType.DMA((3,))],
        cost_estimate=cost(2 * total * width * width * (last + 1), 20 * total * width),
        name="weights",
        **params(36),
    )(core, h2, du, g, dy, a, dmb)


def first_grads(core, rows, hid, dqkv, w, gmaps, sums):
    total, width = hid.shape
    specs, shapes = out_halves(width, rows, w.shape[1], w.shape[1])
    specs = [whole(shape.shape) for shape in shapes]
    return pl.pallas_call(
        first_kernel,
        grid=(3,),
        in_specs=[
            pl.BlockSpec(memory_space=pltpu.SMEM),
            whole(hid.shape),
            pl.BlockSpec((total, width), lambda i: (0, i)),
            whole(w.shape),
            whole(gmaps[0].shape),
            whole(gmaps[1].shape),
            whole(sums.shape),
        ],
        out_specs=specs,
        out_shape=shapes,
        scratch_shapes=[
            pltpu.VMEM((ZROWS, width), F32),
            pltpu.VMEM((width, 1), F32),
            pltpu.VMEM((width, 1), F32),
        ],
        cost_estimate=cost(6 * total * width * width, 12 * total * width),
        name="first",
        **params(32),
    )(core, hid, dqkv, w, *gmaps, sums)


def shards(tokens, w_qkv, w_feat, w_out, w_fc, w_proj, gains, biases, cotangent):
    micro_count, seq_count, seg_len, width = tokens.shape
    grid = grid_dims()
    rows = w_qkv.shape[0]
    hidden = w_fc.shape[1]
    ratio = hidden // width
    heads = width // HD
    pairs = heads // 2
    wide = 3 * width
    total = micro_count * seq_count * seg_len

    first = jnp.concatenate(
        [
            w_qkv.astype(LOW),
            jnp.transpose(w_feat, (1, 0, 2)).reshape(rows, PAIR).astype(LOW),
            jnp.pad(jnp.concatenate([gains, biases]).T.astype(LOW), ((0, 0), (0, PAIR - 13))),
        ],
        axis=1,
    )
    core = jnp.reshape(grid[1]["c"], (1,))
    first, maps, vec = prepare(core, *gather_rows(first, grid), heads)
    later = jnp.concatenate(
        [
            w_fc.astype(LOW).reshape(rows, width, ratio).swapaxes(1, 2).reshape(rows, hidden),
            w_proj.astype(LOW).reshape(rows, hidden),
            w_out.astype(LOW),
        ],
        axis=1,
    )
    later = lax.all_gather(later, AXES, axis=0, tiled=True)
    fc_bias = vec[8 : 8 + ratio].reshape(width, ratio).T
    mid_vec = jnp.concatenate([vec[:8], fc_bias, vec[8 + ratio :]])
    x = tokens.reshape(total, width)
    dy = cotangent.reshape(total, width)

    entered, swaps, steps = [], [], []
    for m in range(2):
        held = entered[0][0] if m else None
        held_vec = tie(vec, swaps[0][0]) if m else vec
        entered.append(enter(m, held, x, first, maps, held_vec, heads))
        own = entered[m][4]
        if m:
            steps[0].round(entered[1][1])
            own = tie(own, steps[0].running)
        swaps.append(swap(own, grid))
        steps.append(Steps(swaps[m][0], grid, False))
    hid = entered[1][0]
    steps[1].round()
    ready = steps[1].running
    priors = [steps[m].end(swaps[m][1]) for m in range(2)]
    held, mids, swaps, steps = None, [], [], []
    for m in range(2):
        _, qkv, pq, pk, _ = entered[m]
        held_vec = tie(mid_vec, swaps[0][0] if m else ready)
        got = middle(m, held, core, x, dy, qkv, pq, pk, priors[m], later, held_vec, hidden)
        held, rest = got[:7], got[7:]
        mids.append(rest)
        own = rest[1]
        if m:
            steps[0].round(rest[2])
            own = tie(own, steps[0].running)
        swaps.append(swap(own, grid))
        steps.append(Steps(swaps[m][0], grid, True))
    out, a, h2, g, du, dmid, dmb = held
    g_later = weight_grads(tie(core, swaps[1][0]), rows, h2, du, g, dy, a, dmb)
    if len(g_later) == 1:
        g_later = halves(g_later[0], grid, rows)
    inner = mids[0][2] + mids[1][2]
    g_fc_bias = inner[8 : 8 + ratio].T.reshape(ratio, width)
    sums = jnp.concatenate([inner[:8], g_fc_bias, inner[8 + ratio :]])
    keep, give = g_later
    laters = [steps[0].end(swaps[0][1], give)]
    steps[1].round(give)
    _, qkv, pq, pk, _ = entered[0]
    kept, gmap = leave(0, None, core, qkv, pq, pk, priors[0], laters[0], mids[0][0], maps)
    gmaps = [gmap]
    scatter = Scatter(keep, tie(give, laters[0][0], steps[1].running), grid, gmap)
    laters.append(steps[1].end(swaps[1][1], gmap))
    _, qkv, pq, pk, _ = entered[1]
    held_core = tie(core, scatter.left, scatter.right)
    dqkv, gmap = leave(1, kept, held_core, qkv, pq, pk, priors[1], laters[1], mids[1][0], maps)
    gmaps.append(gmap)
    g_qkv = first_grads(core, rows, hid, dqkv, first, gmaps, sums)
    if len(g_qkv) == 1:
        g_qkv = halves(g_qkv[0], grid, rows)
    scatter.one(g_qkv[0])
    ending = Scatter(*g_qkv, grid, scatter.left)
    held_vec = tie(vec, ending.left, ending.right, scatter.right)
    dx = norm_grads(x, dqkv, first, dmid, held_vec)
    scatter.two(dx)
    ending.one(scatter.left)
    ending.two()
    r_later = scatter.end(ending.left)
    last = ending.end().astype(F32)
    r_fc = r_later[:, :hidden]
    r_proj = r_later[:, hidden : 2 * hidden]
    r_out = r_later[:, 2 * hidden :]
    small = last[:, wide + PAIR :].T
    return (
        out.reshape(tokens.shape),
        dx.reshape(tokens.shape),
        last[:, :wide],
        jnp.transpose(last[:, wide : wide + PAIR].reshape(rows, 2, HD), (1, 0, 2)),
        r_out.astype(F32),
        r_fc.astype(F32).reshape(rows, ratio, width).swapaxes(1, 2).reshape(rows, hidden),
        r_proj.astype(F32).reshape(rows * ratio, width),
        small[:2],
        small[2:13],
    )


def solution(mesh):
    return jax.shard_map(
        shards,
        mesh=mesh,
        in_specs=(
            P(None, "dp", "seq", None),
            P(("dp", "seq"), None),
            P(None, ("dp", "seq"), None),
            P(("dp", "seq"), None),
            P(("dp", "seq"), None),
            P(("dp", "seq"), None),
            P(None, ("dp", "seq")),
            P(None, ("dp", "seq")),
            P(None, "dp", "seq", None),
        ),
        out_specs=(
            P(None, "dp", "seq", None),
            P(None, "dp", "seq", None),
            P(("dp", "seq"), None),
            P(None, ("dp", "seq"), None),
            P(("dp", "seq"), None),
            P(("dp", "seq"), None),
            P(("dp", "seq"), None),
            P(None, ("dp", "seq")),
            P(None, ("dp", "seq")),
        ),
        check_vma=False,
    )
```
